32 devices in a mesh: lat: 8 (over z, y), lon: 4 (over x, core).
Axes of the slice: x: 2, y: 2, z: 4, core: 2. Of those that a mesh axis runs over, the one named last changes fastest.
Arguments:
- field: bfloat16 [32, 256, 3600], P(None, 'lat', 'lon'), may hold values from -6 to 6
- offsets: int32 [9, 2], replicated, may hold values from -2 to 2, as said below
- conv_weight: float32 [32, 9], replicated, may hold values from -2 to 2
- legendre: bfloat16 [64, 64, 128], P(('lat', 'lon')), may hold values from -5 to 5
- quad_weight: float32 [128], replicated, may hold values from 0.5 to 2
- band_limit: int32 [128], replicated, may hold values from 1 to 64, as said below
- mix_weight: bfloat16 [2, 64, 32, 32], replicated, may hold values from -0.125 to 0.125
Outputs:
- block_out: bfloat16 [32, 256, 3600], P(None, 'lat', 'lon')
The draws below stay inside these ranges and needn't reach their ends.
Inputs may be any that keep to these rules, and one draw needn't show every extreme that they name: `offsets`: every offset lies within two rows and two columns; the taps include a row offset of +2, one of -2, a column offset of +2 and one of -2. `band_limit`: rows near the poles keep few orders; the rows nearest the equator keep all 64 orders.
All inputs are finite; a program needn't handle non-finite values.
Results may differ from the reference program's by a relative error of at most 0.01.
Values may be sent and summed in bfloat16 or wider, within the bound.
No kernel may reach another device: no remote copies, remote signals or barrier semaphores. Data moves between devices by JAX's collectives and lax.ppermute only.
A program may use at most 128 MiB of HBM per device.

```python
import math
import jax
import jax.numpy as jnp
from jax import lax

C = 32
KTAPS = 9
NLON = 3600
NLAT = 256
HALF = 128
MM = 64


def draw_offsets(key, part):
    loose_pairs = jax.random.randint(key, (KTAPS, 2), -2, 3)
    extremes = jnp.array([[2, 0], [-2, 0], [0, 2], [0, -2]], jnp.int32)
    pinned = jnp.array([[1, 0], [1, 0], [0, 1], [0, 1]], jnp.int32)
    head_rows = extremes * pinned + loose_pairs[:4] * (1 - pinned)
    return jnp.concatenate([head_rows, loose_pairs[4:]], axis=0).astype(jnp.int32)


def draw_band_limit(key, part):
    row_ids = jnp.arange(NLAT // 2, dtype=jnp.int32)
    ramp_value = 2 * MM * (row_ids + 1) // (NLAT // 2)
    jitter = jax.random.randint(key, (NLAT // 2,), 0, MM // 4 + 1)
    return jnp.clip(ramp_value - jitter, 1, MM).astype(jnp.int32)


def block_levels(key, dims, split, low, largest):
    gain, own = 1.0, jax.random.fold_in(key, 6)
    for position, shards_of in split:
        heights = jnp.exp(jax.random.uniform(jax.random.fold_in(own, position), (shards_of,), jnp.float32, low / len(split), largest / len(split)))
        gain = gain * jnp.repeat(heights, dims[position] // shards_of).reshape([-1 if axis == position else 1 for axis in range(len(dims))])
    return gain


def gaussian(stream_key, dims, deviation, limit, split=(), kind=jnp.bfloat16):
    gain = block_levels(stream_key, dims, split, -0.22, 0.18) if split else 1.0
    entries = jax.random.normal(stream_key, dims, jnp.float32) * deviation * gain
    return jnp.minimum(jnp.maximum(entries, -limit), limit).astype(kind)


def setup_inputs(seed: int = 0) -> dict:
    keys = jax.random.split(jax.random.key(seed), 8)
    return {
        "field": gaussian(keys[0], (C, NLAT, NLON), 1.0, 6.0, ((1, 8), (2, 4))),
        "offsets": draw_offsets(jax.random.fold_in(keys[7], 71), 0),
        "conv_weight": gaussian(keys[2], (C, KTAPS), KTAPS ** -0.5, 2.0, (), jnp.float32),
        "legendre": gaussian(keys[3], (MM, MM, HALF), 1.0, 5.0, ((0, 32),)),
        "quad_weight": jnp.clip(jnp.exp(jax.random.uniform(keys[4], (HALF,), jnp.float32, math.log(0.5), math.log(2.0))), 0.5, 2.0),
        "band_limit": draw_band_limit(jax.random.fold_in(keys[7], 71), 0),
        "mix_weight": gaussian(keys[6], (2, MM, C, C), (C * MM) ** -0.5, 0.125),
    }


def wave_table(orders, points, period, inverse_form):
    angles = (orders[:, None] * points[None, :] % period).astype(jnp.float32) * (2.0 * math.pi / period)
    factor = jnp.full(orders.shape, 1.0 / math.sqrt(period), jnp.float32)
    if inverse_form:
        factor = jnp.where(orders == 0, 1.0, 2.0).astype(jnp.float32) * factor
    stacked = jnp.stack([factor[:, None] * jnp.cos(angles), -factor[:, None] * jnp.sin(angles)], axis=1)
    return stacked.astype(jnp.bfloat16)

def conv_plane(lat_plane, weights, offsets):
    padded = jnp.pad(lat_plane, ((2, 2), (0, 0)))
    padded = jnp.concatenate([padded[:, -2:], padded, padded[:, :2]], axis=1)
    running = jnp.zeros(lat_plane.shape, jnp.float32)
    for tap_index in range(KTAPS):
        window = lax.dynamic_slice(padded, (2 + offsets[tap_index, 0], 2 + offsets[tap_index, 1]), lat_plane.shape)
        running = running + weights[tap_index] * window.astype(jnp.float32)
    return running.astype(jnp.bfloat16)

def reference(field, offsets, conv_weight, legendre, quad_weight, band_limit, mix_weight):
    half_rows = NLAT // 2
    orders = jnp.arange(MM, dtype=jnp.int32)
    points = jnp.arange(NLON, dtype=jnp.int32)
    forward = wave_table(orders, points, NLON, False).reshape(2 * MM, NLON)
    inverse = wave_table(orders, points, NLON, True).reshape(2 * MM, NLON)

    def analyse(packed):
        lat_plane, weights = packed
        conv_out = conv_plane(lat_plane, weights, offsets)
        return jnp.dot(conv_out, forward.T, preferred_element_type=jnp.float32).astype(jnp.bfloat16)
    spectrum = lax.map(analyse, (field, conv_weight))
    spectrum = jnp.transpose(spectrum.reshape(C, NLAT, MM, 2), (2, 0, 1, 3))

    def per_order(packed):
        order_id, table_rows, order_part = packed
        north_part = order_part[:, :half_rows].astype(jnp.float32)
        south_part = jnp.flip(order_part[:, half_rows:], axis=1).astype(jnp.float32)
        kept_mask = (order_id < band_limit).astype(jnp.float32)
        weight_q = quad_weight * kept_mask * (1.0 / math.sqrt(half_rows))
        even_terms = (weight_q[None, :, None] * (north_part + south_part)).astype(jnp.bfloat16)
        odd_terms = (weight_q[None, :, None] * (north_part - south_part)).astype(jnp.bfloat16)
        degrees = jnp.arange(MM, dtype=jnp.int32)
        same_parity = (degrees + order_id) % 2 == 0
        degree_plane = table_rows.astype(jnp.float32)
        coef_even = jnp.einsum('li,cip->lpc', degree_plane, even_terms.astype(jnp.float32))
        coef_odd = jnp.einsum('li,cip->lpc', degree_plane, odd_terms.astype(jnp.float32))
        triangle = (degrees >= order_id).astype(jnp.float32)
        coeffs = jnp.where(same_parity[:, None, None], coef_even, coef_odd) * triangle[:, None, None]
        coeffs = lax.optimization_barrier(coeffs.astype(jnp.bfloat16)).astype(jnp.float32)
        w_real = mix_weight[0].astype(jnp.float32)
        w_imag = mix_weight[1].astype(jnp.float32)
        real_in = coeffs[:, 0]
        imag_in = coeffs[:, 1]
        real_out = jnp.einsum('lc,lcd->ld', real_in, w_real) - jnp.einsum('lc,lcd->ld', imag_in, w_imag)
        imag_out = jnp.einsum('lc,lcd->ld', imag_in, w_real) + jnp.einsum('lc,lcd->ld', real_in, w_imag)
        mixed = jnp.stack([real_out, imag_out], axis=1)
        mixed = lax.optimization_barrier(mixed.astype(jnp.bfloat16)).astype(jnp.float32)
        even_back = jnp.einsum('li,lpc->cip', degree_plane, jnp.where(same_parity[:, None, None], mixed, 0.0))
        odd_back = jnp.einsum('li,lpc->cip', degree_plane, jnp.where(same_parity[:, None, None], 0.0, mixed))
        north_out = (even_back + odd_back) * kept_mask[None, :, None]
        south_out = (even_back - odd_back) * kept_mask[None, :, None]
        return jnp.concatenate([north_out, jnp.flip(south_out, axis=1)], axis=1).astype(jnp.bfloat16)
    grid_spectrum = lax.map(per_order, (orders, legendre, spectrum))
    grid_spectrum = jnp.transpose(grid_spectrum, (1, 2, 0, 3)).reshape(C, NLAT, 2 * MM)

    def synthesise(packed):
        lat_plane, weights, spectral_rows = packed
        conv_out = conv_plane(lat_plane, weights, offsets)
        synthesis = jnp.dot(spectral_rows, inverse, preferred_element_type=jnp.float32)
        return (conv_out.astype(jnp.float32) + jax.nn.gelu(synthesis, approximate=True)).astype(jnp.bfloat16)
    return lax.map(synthesise, (field, conv_weight, grid_spectrum))
```

```python
import math

import jax
import jax.numpy as jnp
from jax import lax
from jax.sharding import PartitionSpec as P

KTAPS = 9
BOTH = ("lat", "lon")


def padded(cells, sides, width, closed):
    for axis, dim in sides:
        count = lax.axis_size(axis)
        ends = count if closed else count - 1
        head = lax.slice_in_dim(cells, 0, width, axis=dim)
        tail = lax.slice_in_dim(cells, cells.shape[dim] - width, cells.shape[dim], axis=dim)
        cells = jnp.concatenate(
            [
                lax.ppermute(tail, axis, [(i, (i + 1) % count) for i in range(ends)]),
                cells,
                lax.ppermute(head, axis, [((i + 1) % count, i) for i in range(ends)]),
            ],
            axis=dim,
        )
    return cells


def wave_table(orders, points, period, inverse_form):
    angles = (orders[:, None] * points[None, :] % period).astype(jnp.float32) * (
        2.0 * math.pi / period
    )
    factor = jnp.full(orders.shape, 1.0 / math.sqrt(period), jnp.float32)
    if inverse_form:
        factor = jnp.where(orders == 0, 1.0, 2.0).astype(jnp.float32) * factor
    stacked = jnp.stack(
        [factor[:, None] * jnp.cos(angles), -factor[:, None] * jnp.sin(angles)], axis=1
    )
    return stacked.astype(jnp.bfloat16)


def per_device(field, offsets, conv_weight, legendre, quad_weight, band_limit, mix_weight):
    channels, lat_rows, lon_cols = field.shape
    m_dev = legendre.shape[0]
    lon_count = lax.axis_size("lon")
    lat_count = lax.axis_size("lat")
    n_dev = lon_count * lat_count
    total_lon = lon_cols * lon_count
    total_lat = lat_rows * lat_count
    half_rows = total_lat // 2
    orders_all = m_dev * n_dev
    lon_points = lax.axis_index("lon") * lon_cols + lax.iota(jnp.int32, lon_cols)
    me = lax.axis_index("lat") * lon_count + lax.axis_index("lon")
    mine = me * m_dev + lax.iota(jnp.int32, m_dev)

    forward_rows = wave_table(
        lax.iota(jnp.int32, orders_all), lon_points, total_lon, False
    ).reshape(orders_all * 2, lon_cols)
    flat_field = field.reshape(channels * lat_rows, lon_cols)
    partial = lax.dot_general(
        forward_rows, flat_field, (((1,), (1,)), ((), ())), preferred_element_type=jnp.float32
    ).reshape(n_dev, m_dev, 2, channels, lat_rows)
    gathered = lax.all_to_all(partial, BOTH, 0, 0, tiled=True)
    summed = gathered.reshape(lat_count, lon_count, m_dev, 2, channels, lat_rows).sum(axis=1)
    raw_spec = jnp.transpose(summed, (1, 2, 3, 0, 4)).reshape(m_dev, 2, channels, total_lat)

    rim = jnp.pad(raw_spec, ((0, 0), (0, 0), (0, 0), (2, 2)))
    spec_acc = jnp.zeros(raw_spec.shape, jnp.float32)
    for tap_index in range(KTAPS):
        window = lax.dynamic_slice_in_dim(rim, 2 + offsets[tap_index, 0], total_lat, axis=3)
        turn = ((mine * offsets[tap_index, 1]) % total_lon).astype(jnp.float32) * (
            2.0 * math.pi / total_lon
        )
        cos_t = jnp.cos(turn)[:, None, None]
        sin_t = jnp.sin(turn)[:, None, None]
        real_part = cos_t * window[:, 0] - sin_t * window[:, 1]
        imag_part = sin_t * window[:, 0] + cos_t * window[:, 1]
        tap_w = conv_weight[:, tap_index][None, None, :, None]
        spec_acc = spec_acc + tap_w * jnp.stack([real_part, imag_part], axis=1)
    spectrum = spec_acc.astype(jnp.bfloat16)

    north_part = spectrum[..., :half_rows].astype(jnp.float32)
    south_part = jnp.flip(spectrum[..., half_rows:], axis=3).astype(jnp.float32)
    kept_mask = (mine[:, None] < band_limit[None, :]).astype(jnp.float32)
    weight_q = quad_weight[None, :] * kept_mask * (1.0 / math.sqrt(half_rows))
    even_terms = (weight_q[:, None, None, :] * (north_part + south_part)).astype(jnp.bfloat16)
    odd_terms = (weight_q[:, None, None, :] * (north_part - south_part)).astype(jnp.bfloat16)
    paired = legendre.reshape(m_dev, orders_all // 2, 2, half_rows)
    mix_pairs = mix_weight.reshape(2, orders_all // 2, 2, channels, channels)
    even_sum = jnp.zeros((m_dev, 2, channels, half_rows), jnp.float32)
    odd_sum = jnp.zeros((m_dev, 2, channels, half_rows), jnp.float32)
    for parity in range(2):
        same_parity = ((parity + mine) % 2 == 0)[:, None, None, None]
        operand = jnp.where(same_parity, even_terms, odd_terms)
        degree_plane = paired[:, :, parity]
        coeffs = jnp.einsum(
            "mui,mpci->mupc", degree_plane, operand, preferred_element_type=jnp.float32
        )
        degrees = 2 * lax.iota(jnp.int32, orders_all // 2) + parity
        triangle = (degrees[None, :] >= mine[:, None]).astype(jnp.float32)
        coeffs = (coeffs * triangle[:, :, None, None]).astype(jnp.bfloat16)
        with_real = jnp.einsum(
            "mupc,ucd->mupd", coeffs, mix_pairs[0, :, parity], preferred_element_type=jnp.float32
        )
        with_imag = jnp.einsum(
            "mupc,ucd->mupd", coeffs, mix_pairs[1, :, parity], preferred_element_type=jnp.float32
        )
        mixed = jnp.stack(
            [with_real[:, :, 0] - with_imag[:, :, 1], with_real[:, :, 1] + with_imag[:, :, 0]],
            axis=2,
        ).astype(jnp.bfloat16)
        returned = jnp.einsum(
            "mui,mupc->mpci", degree_plane, mixed, preferred_element_type=jnp.float32
        )
        even_sum = even_sum + jnp.where(same_parity, returned, 0.0)
        odd_sum = odd_sum + jnp.where(same_parity, 0.0, returned)
    north_out = (even_sum + odd_sum) * kept_mask[:, None, None, :]
    south_out = (even_sum - odd_sum) * kept_mask[:, None, None, :]
    grid_spectrum = jnp.concatenate([north_out, jnp.flip(south_out, axis=3)], axis=3).astype(
        jnp.bfloat16
    )

    by_group = jnp.transpose(
        grid_spectrum.reshape(m_dev, 2, channels, lat_count, lat_rows), (3, 0, 1, 2, 4)
    )
    outgoing = jnp.broadcast_to(
        by_group[:, None], (lat_count, lon_count, m_dev, 2, channels, lat_rows)
    ).reshape(n_dev, m_dev, 2, channels, lat_rows)
    full_rows = lax.all_to_all(outgoing, BOTH, 0, 0, tiled=True)
    spectral_rows = full_rows.reshape(orders_all * 2, channels * lat_rows)
    inverse_rows = wave_table(
        lax.iota(jnp.int32, orders_all), lon_points, total_lon, True
    ).reshape(orders_all * 2, lon_cols)
    synthesis = lax.dot_general(
        spectral_rows, inverse_rows, (((0,), (0,)), ((), ())), preferred_element_type=jnp.float32
    ).reshape(channels, lat_rows, lon_cols)

    rimmed = padded(field, (("lat", 1),), 2, False)
    rimmed = padded(rimmed, (("lon", 2),), 2, True)
    running = jnp.zeros(field.shape, jnp.float32)
    for tap_index in range(KTAPS):
        window = lax.dynamic_slice(
            rimmed,
            (jnp.int32(0), 2 + offsets[tap_index, 0], 2 + offsets[tap_index, 1]),
            field.shape,
        )
        running = running + conv_weight[:, tap_index][:, None, None] * window.astype(jnp.float32)
    conv_out = running.astype(jnp.bfloat16)
    return (conv_out.astype(jnp.float32) + jax.nn.gelu(synthesis, approximate=True)).astype(
        jnp.bfloat16
    )


def solution(mesh):
    placed = (P(None, "lat", "lon"), P(), P(), P(BOTH, None, None), P(), P(), P())
    return jax.shard_map(
        per_device, mesh=mesh, in_specs=placed, out_specs=P(None, "lat", "lon"), check_vma=False
    )
```

```python
import math

import jax
import jax.numpy as jnp
from jax import lax
from jax.sharding import PartitionSpec as P
from jax.experimental import pallas as pl
from jax.experimental.pallas import tpu as pltpu

KTAPS = 9
BOTH = ("lat", "lon")


def wave_table(orders, points, period, inverse_form):
    angles = (orders[:, None] * points[None, :] % period).astype(jnp.float32) * (
        2.0 * math.pi / period
    )
    factor = jnp.full(orders.shape, 1.0 / math.sqrt(period), jnp.float32)
    if inverse_form:
        factor = jnp.where(orders == 0, 1.0, 2.0).astype(jnp.float32) * factor
    stacked = jnp.stack(
        [factor[:, None] * jnp.cos(angles), -factor[:, None] * jnp.sin(angles)], axis=1
    )
    return stacked.astype(jnp.bfloat16)


def per_device(field, offsets, conv_weight, legendre, quad_weight, band_limit, mix_weight):
    channels, lat_rows, lon_cols = field.shape
    m_dev = legendre.shape[0]
    lon_count = lax.axis_size("lon")
    lat_count = lax.axis_size("lat")
    n_dev = lon_count * lat_count
    total_lon = lon_cols * lon_count
    total_lat = lat_rows * lat_count
    half_rows = total_lat // 2
    orders_all = m_dev * n_dev
    lon_points = lax.axis_index("lon") * lon_cols + lax.iota(jnp.int32, lon_cols)
    me = lax.axis_index("lat") * lon_count + lax.axis_index("lon")
    mine = me * m_dev + lax.iota(jnp.int32, m_dev)

    forward_rows = wave_table(
        lax.iota(jnp.int32, orders_all), lon_points, total_lon, False
    ).reshape(orders_all * 2, lon_cols)
    flat_field = field.reshape(channels * lat_rows, lon_cols)
    partial = lax.dot_general(
        forward_rows, flat_field, (((1,), (1,)), ((), ())), preferred_element_type=jnp.float32
    ).reshape(n_dev, m_dev, 2, channels, lat_rows)
    gathered = lax.all_to_all(partial, BOTH, 0, 0, tiled=True)
    summed = gathered.reshape(lat_count, lon_count, m_dev, 2, channels, lat_rows).sum(axis=1)
    raw_spec = jnp.transpose(summed, (1, 2, 3, 0, 4)).reshape(m_dev, 2, channels, total_lat)

    rim = jnp.pad(raw_spec, ((0, 0), (0, 0), (0, 0), (2, 2)))
    turns = ((mine[None, :] * offsets[:, 1:2]) % total_lon).astype(jnp.float32) * (
        2.0 * math.pi / total_lon
    )
    cos_all = jnp.cos(turns)
    sin_all = jnp.sin(turns)
    spec_acc = jnp.zeros(raw_spec.shape, jnp.float32)
    for tap_index in range(KTAPS):
        window = lax.dynamic_slice_in_dim(rim, 2 + offsets[tap_index, 0], total_lat, axis=3)
        cos_t = cos_all[tap_index][:, None, None]
        sin_t = sin_all[tap_index][:, None, None]
        real_part = cos_t * window[:, 0] - sin_t * window[:, 1]
        imag_part = sin_t * window[:, 0] + cos_t * window[:, 1]
        tap_w = conv_weight[:, tap_index][None, None, :, None]
        spec_acc = spec_acc + tap_w * jnp.stack([real_part, imag_part], axis=1)
    spectrum = spec_acc.astype(jnp.bfloat16)

    north_part = spectrum[..., :half_rows].astype(jnp.float32)
    south_part = jnp.flip(spectrum[..., half_rows:], axis=3).astype(jnp.float32)
    kept_mask = (mine[:, None] < band_limit[None, :]).astype(jnp.float32)
    weight_q = quad_weight[None, :] * kept_mask * (1.0 / math.sqrt(half_rows))
    even_terms = (weight_q[:, None, None, :] * (north_part + south_part)).astype(jnp.bfloat16)
    odd_terms = (weight_q[:, None, None, :] * (north_part - south_part)).astype(jnp.bfloat16)
    paired = legendre.reshape(m_dev, orders_all // 2, 2, half_rows)
    mix_pairs = mix_weight.reshape(2, orders_all // 2, 2, channels, channels)
    even_sum = jnp.zeros((m_dev, 2, channels, half_rows), jnp.float32)
    odd_sum = jnp.zeros((m_dev, 2, channels, half_rows), jnp.float32)
    for parity in range(2):
        same_parity = ((parity + mine) % 2 == 0)[:, None, None, None]
        operand = jnp.where(same_parity, even_terms, odd_terms)
        degree_plane = paired[:, :, parity]
        coeffs = jnp.einsum(
            "mui,mpci->mupc", degree_plane, operand, preferred_element_type=jnp.float32
        )
        degrees = 2 * lax.iota(jnp.int32, orders_all // 2) + parity
        triangle = (degrees[None, :] >= mine[:, None]).astype(jnp.float32)
        coeffs = (coeffs * triangle[:, :, None, None]).astype(jnp.bfloat16)
        with_real = jnp.einsum(
            "mupc,ucd->mupd", coeffs, mix_pairs[0, :, parity], preferred_element_type=jnp.float32
        )
        with_imag = jnp.einsum(
            "mupc,ucd->mupd", coeffs, mix_pairs[1, :, parity], preferred_element_type=jnp.float32
        )
        mixed = jnp.stack(
            [with_real[:, :, 0] - with_imag[:, :, 1], with_real[:, :, 1] + with_imag[:, :, 0]],
            axis=2,
        ).astype(jnp.bfloat16)
        returned = jnp.einsum(
            "mui,mupc->mpci", degree_plane, mixed, preferred_element_type=jnp.float32
        )
        even_sum = even_sum + jnp.where(same_parity, returned, 0.0)
        odd_sum = odd_sum + jnp.where(same_parity, 0.0, returned)
    north_out = (even_sum + odd_sum) * kept_mask[:, None, None, :]
    south_out = (even_sum - odd_sum) * kept_mask[:, None, None, :]
    grid_spectrum = jnp.concatenate([north_out, jnp.flip(south_out, axis=3)], axis=3).astype(
        jnp.bfloat16
    )

    by_group = jnp.transpose(
        grid_spectrum.reshape(m_dev, 2, channels, lat_count, lat_rows), (3, 0, 1, 2, 4)
    )
    outgoing = jnp.broadcast_to(
        by_group[:, None], (lat_count, lon_count, m_dev, 2, channels, lat_rows)
    ).reshape(n_dev, m_dev, 2, channels, lat_rows)
    full_rows = lax.all_to_all(outgoing, BOTH, 0, 0, tiled=True)
    spectral_rows = full_rows.reshape(orders_all * 2, channels * lat_rows)
    inverse_rows = wave_table(
        lax.iota(jnp.int32, orders_all), lon_points, total_lon, True
    ).reshape(orders_all * 2, lon_cols)
    synthesis = lax.dot_general(
        spectral_rows, inverse_rows, (((0,), (0,)), ((), ())), preferred_element_type=jnp.float32
    ).reshape(channels, lat_rows, lon_cols)

    rim_rows = lat_rows + 8
    rim_cols = ((lon_cols + 4 + 127) // 128) * 128
    lat_n = lax.axis_size("lat")
    south = lax.ppermute(
        field[:, :2], "lat", [((i + 1), i) for i in range(lat_n - 1)]
    )
    north = lax.ppermute(
        field[:, lat_rows - 2 :], "lat", [(i, (i + 1)) for i in range(lat_n - 1)]
    )
    rows_ext = jnp.concatenate(
        [field, south, jnp.zeros((channels, 4, lon_cols), field.dtype), north], axis=1
    )
    east = lax.ppermute(
        rows_ext[:, :, :2], "lon", [((i + 1) % lon_count, i) for i in range(lon_count)]
    )
    west = lax.ppermute(
        rows_ext[:, :, lon_cols - 2 :], "lon", [(i, (i + 1) % lon_count) for i in range(lon_count)]
    )
    rim = jnp.concatenate(
        [
            rows_ext,
            east,
            jnp.zeros((channels, rim_rows, rim_cols - lon_cols - 4), field.dtype),
            west,
        ],
        axis=2,
    )
    return finish(offsets, conv_weight, rim, synthesis)


def finish(offsets, conv_weight, rim, synthesis):
    channels, lat_rows, lon_cols = synthesis.shape
    rim_rows, rim_cols = rim.shape[1], rim.shape[2]
    block_c = 8

    def body(offs_ref, w_ref, rim_ref, syn_ref, out_ref):
        blk = pl.program_id(0)
        for c in range(block_c):
            x = rim_ref[c].astype(jnp.float32)
            acc = jnp.zeros((rim_rows, rim_cols), jnp.float32)
            for k in range(KTAPS):
                dr = offs_ref[k, 0]
                dc = offs_ref[k, 1]
                y = pltpu.roll(x, lax.rem(rim_rows - dr, rim_rows), 0)
                y = pltpu.roll(y, lax.rem(rim_cols - dc, rim_cols), 1)
                acc = acc + w_ref[blk * block_c + c, k] * y
            conv = acc[:lat_rows, :lon_cols].astype(jnp.bfloat16).astype(jnp.float32)
            out_ref[c] = (conv + jax.nn.gelu(syn_ref[c], approximate=True)).astype(jnp.bfloat16)

    return pl.pallas_call(
        body,
        grid_spec=pltpu.PrefetchScalarGridSpec(
            num_scalar_prefetch=2,
            grid=(channels // block_c,),
            in_specs=[
                pl.BlockSpec((block_c, rim_rows, rim_cols), lambda b, o, w: (b, 0, 0)),
                pl.BlockSpec((block_c, lat_rows, lon_cols), lambda b, o, w: (b, 0, 0)),
            ],
            out_specs=pl.BlockSpec((block_c, lat_rows, lon_cols), lambda b, o, w: (b, 0, 0)),
        ),
        out_shape=jax.ShapeDtypeStruct((channels, lat_rows, lon_cols), jnp.bfloat16),
    )(offsets, conv_weight, rim, synthesis)


def solution(mesh):
    placed = (P(None, "lat", "lon"), P(), P(), P(BOTH, None, None), P(), P(), P())
    return jax.shard_map(
        per_device, mesh=mesh, in_specs=placed, out_specs=P(None, "lat", "lon"), check_vma=False
    )
```

```python
import math

import jax
import jax.numpy as jnp
from jax import lax
from jax.sharding import PartitionSpec as P
from jax.experimental import pallas as pl
from jax.experimental.pallas import tpu as pltpu

KTAPS = 9
BOTH = ("lat", "lon")


def wave_table(orders, points, period, inverse_form):
    angles = (orders[:, None] * points[None, :] % period).astype(jnp.float32) * (
        2.0 * math.pi / period
    )
    factor = jnp.full(orders.shape, 1.0 / math.sqrt(period), jnp.float32)
    if inverse_form:
        factor = jnp.where(orders == 0, 1.0, 2.0).astype(jnp.float32) * factor
    stacked = jnp.stack(
        [factor[:, None] * jnp.cos(angles), -factor[:, None] * jnp.sin(angles)], axis=1
    )
    return stacked.astype(jnp.bfloat16)


def per_device(field, offsets, conv_weight, legendre, quad_weight, band_limit, mix_weight):
    channels, lat_rows, lon_cols = field.shape
    m_dev = legendre.shape[0]
    lon_count = lax.axis_size("lon")
    lat_count = lax.axis_size("lat")
    n_dev = lon_count * lat_count
    total_lon = lon_cols * lon_count
    total_lat = lat_rows * lat_count
    half_rows = total_lat // 2
    orders_all = m_dev * n_dev
    lon_points = lax.axis_index("lon") * lon_cols + lax.iota(jnp.int32, lon_cols)
    me = lax.axis_index("lat") * lon_count + lax.axis_index("lon")
    mine = me * m_dev + lax.iota(jnp.int32, m_dev)

    forward_rows = wave_table(
        lax.iota(jnp.int32, orders_all), lon_points, total_lon, False
    ).reshape(orders_all * 2, lon_cols)
    flat_field = field.reshape(channels * lat_rows, lon_cols)
    partial = lax.dot_general(
        forward_rows, flat_field, (((1,), (1,)), ((), ())), preferred_element_type=jnp.float32
    ).reshape(n_dev, m_dev, 2, channels, lat_rows)
    gathered = lax.all_to_all(partial, BOTH, 0, 0, tiled=True)
    summed = gathered.reshape(lat_count, lon_count, m_dev, 2, channels, lat_rows).sum(axis=1)
    raw_spec = jnp.transpose(summed, (1, 2, 3, 0, 4)).reshape(m_dev, 2, channels, total_lat)

    rim = jnp.pad(raw_spec, ((0, 0), (0, 0), (0, 0), (2, 2)))
    turns = ((mine[None, :] * offsets[:, 1:2]) % total_lon).astype(jnp.float32) * (
        2.0 * math.pi / total_lon
    )
    cos_all = jnp.cos(turns)
    sin_all = jnp.sin(turns)
    spec_acc = jnp.zeros(raw_spec.shape, jnp.float32)
    for tap_index in range(KTAPS):
        window = lax.dynamic_slice_in_dim(rim, 2 + offsets[tap_index, 0], total_lat, axis=3)
        cos_t = cos_all[tap_index][:, None, None]
        sin_t = sin_all[tap_index][:, None, None]
        real_part = cos_t * window[:, 0] - sin_t * window[:, 1]
        imag_part = sin_t * window[:, 0] + cos_t * window[:, 1]
        tap_w = conv_weight[:, tap_index][None, None, :, None]
        spec_acc = spec_acc + tap_w * jnp.stack([real_part, imag_part], axis=1)
    spectrum = spec_acc.astype(jnp.bfloat16)

    north_part = spectrum[..., :half_rows].astype(jnp.float32)
    south_part = jnp.flip(spectrum[..., half_rows:], axis=3).astype(jnp.float32)
    kept_mask = (mine[:, None] < band_limit[None, :]).astype(jnp.float32)
    weight_q = quad_weight[None, :] * kept_mask * (1.0 / math.sqrt(half_rows))
    even_terms = (weight_q[:, None, None, :] * (north_part + south_part)).astype(jnp.bfloat16)
    odd_terms = (weight_q[:, None, None, :] * (north_part - south_part)).astype(jnp.bfloat16)
    paired = legendre.reshape(m_dev, orders_all // 2, 2, half_rows)
    mix_pairs = mix_weight.reshape(2, orders_all // 2, 2, channels, channels)
    even_sum = jnp.zeros((m_dev, 2, channels, half_rows), jnp.float32)
    odd_sum = jnp.zeros((m_dev, 2, channels, half_rows), jnp.float32)
    for parity in range(2):
        same_parity = ((parity + mine) % 2 == 0)[:, None, None, None]
        operand = jnp.where(same_parity, even_terms, odd_terms)
        degree_plane = paired[:, :, parity]
        coeffs = jnp.einsum(
            "mui,mpci->mupc", degree_plane, operand, preferred_element_type=jnp.float32
        )
        degrees = 2 * lax.iota(jnp.int32, orders_all // 2) + parity
        triangle = (degrees[None, :] >= mine[:, None]).astype(jnp.float32)
        coeffs = (coeffs * triangle[:, :, None, None]).astype(jnp.bfloat16)
        with_real = jnp.einsum(
            "mupc,ucd->mupd", coeffs, mix_pairs[0, :, parity], preferred_element_type=jnp.float32
        )
        with_imag = jnp.einsum(
            "mupc,ucd->mupd", coeffs, mix_pairs[1, :, parity], preferred_element_type=jnp.float32
        )
        mixed = jnp.stack(
            [with_real[:, :, 0] - with_imag[:, :, 1], with_real[:, :, 1] + with_imag[:, :, 0]],
            axis=2,
        ).astype(jnp.bfloat16)
        returned = jnp.einsum(
            "mui,mupc->mpci", degree_plane, mixed, preferred_element_type=jnp.float32
        )
        even_sum = even_sum + jnp.where(same_parity, returned, 0.0)
        odd_sum = odd_sum + jnp.where(same_parity, 0.0, returned)
    north_out = (even_sum + odd_sum) * kept_mask[:, None, None, :]
    south_out = (even_sum - odd_sum) * kept_mask[:, None, None, :]
    grid_spectrum = jnp.concatenate([north_out, jnp.flip(south_out, axis=3)], axis=3).astype(
        jnp.bfloat16
    )

    by_group = jnp.transpose(
        grid_spectrum.reshape(m_dev, 2, channels, lat_count, lat_rows), (3, 0, 1, 2, 4)
    )
    outgoing = jnp.broadcast_to(
        by_group[:, None], (lat_count, lon_count, m_dev, 2, channels, lat_rows)
    ).reshape(n_dev, m_dev, 2, channels, lat_rows)
    full_rows = lax.all_to_all(outgoing, BOTH, 0, 0, tiled=True)
    spectral_rows = full_rows.reshape(orders_all * 2, channels * lat_rows)
    inverse_rows = wave_table(
        lax.iota(jnp.int32, orders_all), lon_points, total_lon, True
    ).reshape(orders_all * 2, lon_cols)
    synthesis = lax.dot_general(
        spectral_rows, inverse_rows, (((0,), (0,)), ((), ())), preferred_element_type=jnp.float32
    ).reshape(channels, lat_rows, lon_cols)

    rim_cols = ((lon_cols + 4 + 127) // 128) * 128
    lat_n = lax.axis_size("lat")
    south = lax.ppermute(
        field[:, :2], "lat", [((i + 1), i) for i in range(lat_n - 1)]
    )
    north = lax.ppermute(
        field[:, lat_rows - 2 :], "lat", [(i, (i + 1)) for i in range(lat_n - 1)]
    )
    rows_ext = jnp.concatenate(
        [north, field, south, jnp.zeros((channels, 4, lon_cols), field.dtype)], axis=1
    )
    rim_rows = rows_ext.shape[1]
    east = lax.ppermute(
        rows_ext[:, :, :2], "lon", [((i + 1) % lon_count, i) for i in range(lon_count)]
    )
    west = lax.ppermute(
        rows_ext[:, :, lon_cols - 2 :], "lon", [(i, (i + 1) % lon_count) for i in range(lon_count)]
    )
    rim = jnp.concatenate(
        [
            rows_ext,
            east,
            jnp.zeros((channels, rim_rows, rim_cols - lon_cols - 4), field.dtype),
            west,
        ],
        axis=2,
    )
    conv_out = depthwise_conv(offsets, conv_weight, rim, lat_rows, lon_cols)
    return (conv_out.astype(jnp.float32) + jax.nn.gelu(synthesis, approximate=True)).astype(
        jnp.bfloat16
    )


def depthwise_conv(offsets, conv_weight, rim, lat_rows, lon_cols):
    channels, rim_rows, rim_cols = rim.shape
    block_c = 8

    def body(offs_ref, w_ref, rim_ref, out_ref):
        blk = pl.program_id(0)
        for c in range(block_c):
            x = rim_ref[c].astype(jnp.float32)
            acc = jnp.zeros((rim_rows, rim_cols), jnp.float32)
            for k in range(KTAPS):
                dr = offs_ref[k, 0]
                dc = offs_ref[k, 1]
                y = pltpu.roll(x, lax.rem(rim_rows - dr - 2, rim_rows), 0)
                y = pltpu.roll(y, lax.rem(rim_cols - dc, rim_cols), 1)
                acc = acc + w_ref[blk * block_c + c, k] * y
            out_ref[c] = acc[:lat_rows, :lon_cols].astype(jnp.bfloat16)

    return pl.pallas_call(
        body,
        grid_spec=pltpu.PrefetchScalarGridSpec(
            num_scalar_prefetch=2,
            grid=(channels // block_c,),
            in_specs=[pl.BlockSpec((block_c, rim_rows, rim_cols), lambda b, o, w: (b, 0, 0))],
            out_specs=pl.BlockSpec((block_c, lat_rows, lon_cols), lambda b, o, w: (b, 0, 0)),
        ),
        out_shape=jax.ShapeDtypeStruct((channels, lat_rows, lon_cols), jnp.bfloat16),
        cost_estimate=pl.CostEstimate(
            flops=40 * KTAPS * channels * rim_rows * rim_cols,
            transcendentals=0,
            bytes_accessed=channels * (rim_rows * rim_cols + lat_rows * lon_cols) * 2,
        ),
    )(offsets, conv_weight, rim)


def solution(mesh):
    placed = (P(None, "lat", "lon"), P(), P(), P(BOTH, None, None), P(), P(), P())
    return jax.shard_map(
        per_device, mesh=mesh, in_specs=placed, out_specs=P(None, "lat", "lon"), check_vma=False
    )
```

```python
import math

import jax
import jax.numpy as jnp
from jax import lax
from jax.sharding import PartitionSpec as P
from jax.experimental import pallas as pl
from jax.experimental.pallas import tpu as pltpu

KTAPS = 9
BOTH = ("lat", "lon")


def wave_table(orders, points, period, inverse_form):
    angles = (orders[:, None] * points[None, :] % period).astype(jnp.float32) * (
        2.0 * math.pi / period
    )
    factor = jnp.full(orders.shape, 1.0 / math.sqrt(period), jnp.float32)
    if inverse_form:
        factor = jnp.where(orders == 0, 1.0, 2.0).astype(jnp.float32) * factor
    stacked = jnp.stack(
        [factor[:, None] * jnp.cos(angles), -factor[:, None] * jnp.sin(angles)], axis=1
    )
    return stacked.astype(jnp.bfloat16)


def per_device(field, offsets, conv_weight, legendre, quad_weight, band_limit, mix_weight):
    channels, lat_rows, lon_cols = field.shape
    m_dev = legendre.shape[0]
    lon_count = lax.axis_size("lon")
    lat_count = lax.axis_size("lat")
    n_dev = lon_count * lat_count
    total_lon = lon_cols * lon_count
    total_lat = lat_rows * lat_count
    half_rows = total_lat // 2
    orders_all = m_dev * n_dev
    lon_points = lax.axis_index("lon") * lon_cols + lax.iota(jnp.int32, lon_cols)
    me = lax.axis_index("lat") * lon_count + lax.axis_index("lon")
    mine = me * m_dev + lax.iota(jnp.int32, m_dev)

    forward_rows = wave_table(
        lax.iota(jnp.int32, orders_all), lon_points, total_lon, False
    ).reshape(orders_all * 2, lon_cols)
    flat_field = field.reshape(channels * lat_rows, lon_cols)
    partial = lax.dot_general(
        forward_rows, flat_field, (((1,), (1,)), ((), ())), preferred_element_type=jnp.float32
    ).reshape(n_dev, m_dev, 2, channels, lat_rows)
    gathered_raw = lax.all_to_all(partial, BOTH, 0, 0, tiled=True)
    rim_cols = ((lon_cols + 4 + 127) // 128) * 128
    lat_n = lax.axis_size("lat")
    south = lax.ppermute(
        field[:, :2], "lat", [((i + 1), i) for i in range(lat_n - 1)]
    )
    north = lax.ppermute(
        field[:, lat_rows - 2 :], "lat", [(i, (i + 1)) for i in range(lat_n - 1)]
    )
    rows_ext = jnp.concatenate(
        [north, field, south, jnp.zeros((channels, 4, lon_cols), field.dtype)], axis=1
    )
    rim_rows = rows_ext.shape[1]
    east = lax.ppermute(
        rows_ext[:, :, :2], "lon", [((i + 1) % lon_count, i) for i in range(lon_count)]
    )
    west = lax.ppermute(
        rows_ext[:, :, lon_cols - 2 :], "lon", [(i, (i + 1) % lon_count) for i in range(lon_count)]
    )
    rim = jnp.concatenate(
        [
            rows_ext,
            east,
            jnp.zeros((channels, rim_rows, rim_cols - lon_cols - 4), field.dtype),
            west,
        ],
        axis=2,
    )
    conv_out = depthwise_conv(offsets, conv_weight, rim, lat_rows, lon_cols)
    gathered, conv_out = lax.optimization_barrier((gathered_raw, conv_out))
    summed = gathered.reshape(lat_count, lon_count, m_dev, 2, channels, lat_rows).sum(axis=1)
    raw_spec = jnp.transpose(summed, (1, 2, 3, 0, 4)).reshape(m_dev, 2, channels, total_lat)

    rim = jnp.pad(raw_spec, ((0, 0), (0, 0), (0, 0), (2, 2)))
    turns = ((mine[None, :] * offsets[:, 1:2]) % total_lon).astype(jnp.float32) * (
        2.0 * math.pi / total_lon
    )
    cos_all = jnp.cos(turns)
    sin_all = jnp.sin(turns)
    spec_acc = jnp.zeros(raw_spec.shape, jnp.float32)
    for tap_index in range(KTAPS):
        window = lax.dynamic_slice_in_dim(rim, 2 + offsets[tap_index, 0], total_lat, axis=3)
        cos_t = cos_all[tap_index][:, None, None]
        sin_t = sin_all[tap_index][:, None, None]
        real_part = cos_t * window[:, 0] - sin_t * window[:, 1]
        imag_part = sin_t * window[:, 0] + cos_t * window[:, 1]
        tap_w = conv_weight[:, tap_index][None, None, :, None]
        spec_acc = spec_acc + tap_w * jnp.stack([real_part, imag_part], axis=1)
    spectrum = spec_acc.astype(jnp.bfloat16)

    north_part = spectrum[..., :half_rows].astype(jnp.float32)
    south_part = jnp.flip(spectrum[..., half_rows:], axis=3).astype(jnp.float32)
    kept_mask = (mine[:, None] < band_limit[None, :]).astype(jnp.float32)
    weight_q = quad_weight[None, :] * kept_mask * (1.0 / math.sqrt(half_rows))
    even_terms = (weight_q[:, None, None, :] * (north_part + south_part)).astype(jnp.bfloat16)
    odd_terms = (weight_q[:, None, None, :] * (north_part - south_part)).astype(jnp.bfloat16)
    paired = legendre.reshape(m_dev, orders_all // 2, 2, half_rows)
    mix_pairs = mix_weight.reshape(2, orders_all // 2, 2, channels, channels)
    even_sum = jnp.zeros((m_dev, 2, channels, half_rows), jnp.float32)
    odd_sum = jnp.zeros((m_dev, 2, channels, half_rows), jnp.float32)
    for parity in range(2):
        same_parity = ((parity + mine) % 2 == 0)[:, None, None, None]
        operand = jnp.where(same_parity, even_terms, odd_terms)
        degree_plane = paired[:, :, parity]
        coeffs = jnp.einsum(
            "mui,mpci->mupc", degree_plane, operand, preferred_element_type=jnp.float32
        )
        degrees = 2 * lax.iota(jnp.int32, orders_all // 2) + parity
        triangle = (degrees[None, :] >= mine[:, None]).astype(jnp.float32)
        coeffs = (coeffs * triangle[:, :, None, None]).astype(jnp.bfloat16)
        with_real = jnp.einsum(
            "mupc,ucd->mupd", coeffs, mix_pairs[0, :, parity], preferred_element_type=jnp.float32
        )
        with_imag = jnp.einsum(
            "mupc,ucd->mupd", coeffs, mix_pairs[1, :, parity], preferred_element_type=jnp.float32
        )
        mixed = jnp.stack(
            [with_real[:, :, 0] - with_imag[:, :, 1], with_real[:, :, 1] + with_imag[:, :, 0]],
            axis=2,
        ).astype(jnp.bfloat16)
        returned = jnp.einsum(
            "mui,mupc->mpci", degree_plane, mixed, preferred_element_type=jnp.float32
        )
        even_sum = even_sum + jnp.where(same_parity, returned, 0.0)
        odd_sum = odd_sum + jnp.where(same_parity, 0.0, returned)
    north_out = (even_sum + odd_sum) * kept_mask[:, None, None, :]
    south_out = (even_sum - odd_sum) * kept_mask[:, None, None, :]
    grid_spectrum = jnp.concatenate([north_out, jnp.flip(south_out, axis=3)], axis=3).astype(
        jnp.bfloat16
    )

    by_group = jnp.transpose(
        grid_spectrum.reshape(m_dev, 2, channels, lat_count, lat_rows), (3, 0, 1, 2, 4)
    )
    outgoing = jnp.broadcast_to(
        by_group[:, None], (lat_count, lon_count, m_dev, 2, channels, lat_rows)
    ).reshape(n_dev, m_dev, 2, channels, lat_rows)
    full_rows = lax.all_to_all(outgoing, BOTH, 0, 0, tiled=True)
    spectral_rows = full_rows.reshape(orders_all * 2, channels * lat_rows)
    inverse_rows = wave_table(
        lax.iota(jnp.int32, orders_all), lon_points, total_lon, True
    ).reshape(orders_all * 2, lon_cols)
    synthesis = lax.dot_general(
        spectral_rows, inverse_rows, (((0,), (0,)), ((), ())), preferred_element_type=jnp.float32
    ).reshape(channels, lat_rows, lon_cols)

    return (conv_out.astype(jnp.float32) + jax.nn.gelu(synthesis, approximate=True)).astype(
        jnp.bfloat16
    )


def depthwise_conv(offsets, conv_weight, rim, lat_rows, lon_cols):
    channels, rim_rows, rim_cols = rim.shape
    block_c = 8

    def body(offs_ref, w_ref, rim_ref, out_ref):
        blk = pl.program_id(0)
        for c in range(block_c):
            x = rim_ref[c].astype(jnp.float32)
            acc = jnp.zeros((rim_rows, rim_cols), jnp.float32)
            for k in range(KTAPS):
                dr = offs_ref[k, 0]
                dc = offs_ref[k, 1]
                y = pltpu.roll(x, lax.rem(rim_rows - dr - 2, rim_rows), 0)
                y = pltpu.roll(y, lax.rem(rim_cols - dc, rim_cols), 1)
                acc = acc + w_ref[blk * block_c + c, k] * y
            out_ref[c] = acc[:lat_rows, :lon_cols].astype(jnp.bfloat16)

    return pl.pallas_call(
        body,
        grid_spec=pltpu.PrefetchScalarGridSpec(
            num_scalar_prefetch=2,
            grid=(channels // block_c,),
            in_specs=[pl.BlockSpec((block_c, rim_rows, rim_cols), lambda b, o, w: (b, 0, 0))],
            out_specs=pl.BlockSpec((block_c, lat_rows, lon_cols), lambda b, o, w: (b, 0, 0)),
        ),
        out_shape=jax.ShapeDtypeStruct((channels, lat_rows, lon_cols), jnp.bfloat16),
        cost_estimate=pl.CostEstimate(
            flops=40 * KTAPS * channels * rim_rows * rim_cols,
            transcendentals=0,
            bytes_accessed=channels * (rim_rows * rim_cols + lat_rows * lon_cols) * 2,
        ),
    )(offsets, conv_weight, rim)


def solution(mesh):
    placed = (P(None, "lat", "lon"), P(), P(), P(BOTH, None, None), P(), P(), P())
    return jax.shard_map(
        per_device, mesh=mesh, in_specs=placed, out_specs=P(None, "lat", "lon"), check_vma=False
    )
```

```python
import math

import jax
import jax.numpy as jnp
from jax import lax
from jax.sharding import PartitionSpec as P
from jax.experimental import pallas as pl
from jax.experimental.pallas import tpu as pltpu

KTAPS = 9
BOTH = ("lat", "lon")


def wave_table(orders, points, period, inverse_form):
    angles = (orders[:, None] * points[None, :] % period).astype(jnp.float32) * (
        2.0 * math.pi / period
    )
    factor = jnp.full(orders.shape, 1.0 / math.sqrt(period), jnp.float32)
    if inverse_form:
        factor = jnp.where(orders == 0, 1.0, 2.0).astype(jnp.float32) * factor
    stacked = jnp.stack(
        [factor[:, None] * jnp.cos(angles), -factor[:, None] * jnp.sin(angles)], axis=1
    )
    return stacked.astype(jnp.bfloat16)


def per_device(field, offsets, conv_weight, legendre, quad_weight, band_limit, mix_weight):
    channels, lat_rows, lon_cols = field.shape
    m_dev = legendre.shape[0]
    lon_count = lax.axis_size("lon")
    lat_count = lax.axis_size("lat")
    n_dev = lon_count * lat_count
    total_lon = lon_cols * lon_count
    total_lat = lat_rows * lat_count
    half_rows = total_lat // 2
    orders_all = m_dev * n_dev
    lon_points = lax.axis_index("lon") * lon_cols + lax.iota(jnp.int32, lon_cols)
    me = lax.axis_index("lat") * lon_count + lax.axis_index("lon")
    mine = me * m_dev + lax.iota(jnp.int32, m_dev)

    forward_rows = wave_table(
        lax.iota(jnp.int32, orders_all), lon_points, total_lon, False
    ).reshape(orders_all * 2, lon_cols)
    flat_field = field.reshape(channels * lat_rows, lon_cols)
    partial = lax.dot_general(
        forward_rows, flat_field, (((1,), (1,)), ((), ())), preferred_element_type=jnp.float32
    ).reshape(n_dev, m_dev, 2, channels, lat_rows)
    gathered_raw = lax.all_to_all(partial, BOTH, 0, 0, tiled=True)
    rim_cols = ((lon_cols + 4 + 127) // 128) * 128
    lat_n = lax.axis_size("lat")
    lon_n = lon_count

    def lin(a, b):
        return a * lon_n + b % lon_n

    down = [(i, i + 1) for i in range(lat_n - 1)]
    up = [(i + 1, i) for i in range(lat_n - 1)]
    north = lax.ppermute(field[:, lat_rows - 2 :], "lat", down)
    south = lax.ppermute(field[:, :2], "lat", up)
    east = lax.ppermute(field[:, :, :2], "lon", [((i + 1) % lon_n, i) for i in range(lon_n)])
    west = lax.ppermute(
        field[:, :, lon_cols - 2 :], "lon", [(i, (i + 1) % lon_n) for i in range(lon_n)]
    )
    grid_pairs = [(a, b) for a in range(lat_n) for b in range(lon_n)]
    north_east = lax.ppermute(
        field[:, lat_rows - 2 :, :2], BOTH,
        [(lin(a, b), lin(a + 1, b - 1)) for a, b in grid_pairs if a < lat_n - 1],
    )
    north_west = lax.ppermute(
        field[:, lat_rows - 2 :, lon_cols - 2 :], BOTH,
        [(lin(a, b), lin(a + 1, b + 1)) for a, b in grid_pairs if a < lat_n - 1],
    )
    south_east = lax.ppermute(
        field[:, :2, :2], BOTH,
        [(lin(a, b), lin(a - 1, b - 1)) for a, b in grid_pairs if a > 0],
    )
    south_west = lax.ppermute(
        field[:, :2, lon_cols - 2 :], BOTH,
        [(lin(a, b), lin(a - 1, b + 1)) for a, b in grid_pairs if a > 0],
    )

    def band(centre, right, left):
        gap = jnp.zeros((channels, centre.shape[1], rim_cols - lon_cols - 4), field.dtype)
        return jnp.concatenate([centre, right, gap, left], axis=2)

    rim = jnp.concatenate(
        [
            band(north, north_east, north_west),
            band(field, east, west),
            band(south, south_east, south_west),
            jnp.zeros((channels, 4, rim_cols), field.dtype),
        ],
        axis=1,
    )
    conv_out = depthwise_conv(offsets, conv_weight, rim, lat_rows, lon_cols)
    gathered, conv_out = lax.optimization_barrier((gathered_raw, conv_out))
    summed = gathered.reshape(lat_count, lon_count, m_dev, 2, channels, lat_rows).sum(axis=1)
    raw_spec = jnp.transpose(summed, (1, 2, 3, 0, 4)).reshape(m_dev, 2, channels, total_lat)

    rim = jnp.pad(raw_spec, ((0, 0), (0, 0), (0, 0), (2, 2)))
    turns = ((mine[None, :] * offsets[:, 1:2]) % total_lon).astype(jnp.float32) * (
        2.0 * math.pi / total_lon
    )
    cos_all = jnp.cos(turns)
    sin_all = jnp.sin(turns)
    spec_acc = jnp.zeros(raw_spec.shape, jnp.float32)
    for tap_index in range(KTAPS):
        window = lax.dynamic_slice_in_dim(rim, 2 + offsets[tap_index, 0], total_lat, axis=3)
        cos_t = cos_all[tap_index][:, None, None]
        sin_t = sin_all[tap_index][:, None, None]
        real_part = cos_t * window[:, 0] - sin_t * window[:, 1]
        imag_part = sin_t * window[:, 0] + cos_t * window[:, 1]
        tap_w = conv_weight[:, tap_index][None, None, :, None]
        spec_acc = spec_acc + tap_w * jnp.stack([real_part, imag_part], axis=1)
    spectrum = spec_acc.astype(jnp.bfloat16)

    north_part = spectrum[..., :half_rows].astype(jnp.float32)
    south_part = jnp.flip(spectrum[..., half_rows:], axis=3).astype(jnp.float32)
    kept_mask = (mine[:, None] < band_limit[None, :]).astype(jnp.float32)
    weight_q = quad_weight[None, :] * kept_mask * (1.0 / math.sqrt(half_rows))
    even_terms = (weight_q[:, None, None, :] * (north_part + south_part)).astype(jnp.bfloat16)
    odd_terms = (weight_q[:, None, None, :] * (north_part - south_part)).astype(jnp.bfloat16)
    paired = legendre.reshape(m_dev, orders_all // 2, 2, half_rows)
    mix_pairs = mix_weight.reshape(2, orders_all // 2, 2, channels, channels)
    even_sum = jnp.zeros((m_dev, 2, channels, half_rows), jnp.float32)
    odd_sum = jnp.zeros((m_dev, 2, channels, half_rows), jnp.float32)
    for parity in range(2):
        same_parity = ((parity + mine) % 2 == 0)[:, None, None, None]
        operand = jnp.where(same_parity, even_terms, odd_terms)
        degree_plane = paired[:, :, parity]
        coeffs = jnp.einsum(
            "mui,mpci->mupc", degree_plane, operand, preferred_element_type=jnp.float32
        )
        degrees = 2 * lax.iota(jnp.int32, orders_all // 2) + parity
        triangle = (degrees[None, :] >= mine[:, None]).astype(jnp.float32)
        coeffs = (coeffs * triangle[:, :, None, None]).astype(jnp.bfloat16)
        with_real = jnp.einsum(
            "mupc,ucd->mupd", coeffs, mix_pairs[0, :, parity], preferred_element_type=jnp.float32
        )
        with_imag = jnp.einsum(
            "mupc,ucd->mupd", coeffs, mix_pairs[1, :, parity], preferred_element_type=jnp.float32
        )
        mixed = jnp.stack(
            [with_real[:, :, 0] - with_imag[:, :, 1], with_real[:, :, 1] + with_imag[:, :, 0]],
            axis=2,
        ).astype(jnp.bfloat16)
        returned = jnp.einsum(
            "mui,mupc->mpci", degree_plane, mixed, preferred_element_type=jnp.float32
        )
        even_sum = even_sum + jnp.where(same_parity, returned, 0.0)
        odd_sum = odd_sum + jnp.where(same_parity, 0.0, returned)
    north_out = (even_sum + odd_sum) * kept_mask[:, None, None, :]
    south_out = (even_sum - odd_sum) * kept_mask[:, None, None, :]
    grid_spectrum = jnp.concatenate([north_out, jnp.flip(south_out, axis=3)], axis=3).astype(
        jnp.bfloat16
    )

    by_group = jnp.transpose(
        grid_spectrum.reshape(m_dev, 2, channels, lat_count, lat_rows), (3, 0, 1, 2, 4)
    )
    outgoing = jnp.broadcast_to(
        by_group[:, None], (lat_count, lon_count, m_dev, 2, channels, lat_rows)
    ).reshape(n_dev, m_dev, 2, channels, lat_rows)
    full_rows = lax.all_to_all(outgoing, BOTH, 0, 0, tiled=True)
    spectral_rows = full_rows.reshape(orders_all * 2, channels * lat_rows)
    inverse_rows = wave_table(
        lax.iota(jnp.int32, orders_all), lon_points, total_lon, True
    ).reshape(orders_all * 2, lon_cols)
    synthesis = lax.dot_general(
        spectral_rows, inverse_rows, (((0,), (0,)), ((), ())), preferred_element_type=jnp.float32
    ).reshape(channels, lat_rows, lon_cols)

    return (conv_out.astype(jnp.float32) + jax.nn.gelu(synthesis, approximate=True)).astype(
        jnp.bfloat16
    )


def depthwise_conv(offsets, conv_weight, rim, lat_rows, lon_cols):
    channels, rim_rows, rim_cols = rim.shape
    block_c = 8

    def body(offs_ref, w_ref, rim_ref, out_ref):
        blk = pl.program_id(0)
        for c in range(block_c):
            x = rim_ref[c].astype(jnp.float32)
            acc = jnp.zeros((rim_rows, rim_cols), jnp.float32)
            for k in range(KTAPS):
                dr = offs_ref[k, 0]
                dc = offs_ref[k, 1]
                y = pltpu.roll(x, lax.rem(rim_rows - dr - 2, rim_rows), 0)
                y = pltpu.roll(y, lax.rem(rim_cols - dc, rim_cols), 1)
                acc = acc + w_ref[blk * block_c + c, k] * y
            out_ref[c] = acc[:lat_rows, :lon_cols].astype(jnp.bfloat16)

    return pl.pallas_call(
        body,
        grid_spec=pltpu.PrefetchScalarGridSpec(
            num_scalar_prefetch=2,
            grid=(channels // block_c,),
            in_specs=[pl.BlockSpec((block_c, rim_rows, rim_cols), lambda b, o, w: (b, 0, 0))],
            out_specs=pl.BlockSpec((block_c, lat_rows, lon_cols), lambda b, o, w: (b, 0, 0)),
        ),
        out_shape=jax.ShapeDtypeStruct((channels, lat_rows, lon_cols), jnp.bfloat16),
        cost_estimate=pl.CostEstimate(
            flops=40 * KTAPS * channels * rim_rows * rim_cols,
            transcendentals=0,
            bytes_accessed=channels * (rim_rows * rim_cols + lat_rows * lon_cols) * 2,
        ),
    )(offsets, conv_weight, rim)


def solution(mesh):
    placed = (P(None, "lat", "lon"), P(), P(), P(BOTH, None, None), P(), P(), P())
    return jax.shard_map(
        per_device, mesh=mesh, in_specs=placed, out_specs=P(None, "lat", "lon"), check_vma=False
    )
```

```python
import math

import jax
import jax.numpy as jnp
from jax import lax
from jax.sharding import PartitionSpec as P
from jax.experimental import pallas as pl
from jax.experimental.pallas import tpu as pltpu

KTAPS = 9
BOTH = ("lat", "lon")


def wave_table(orders, points, period, inverse_form):
    angles = (orders[:, None] * points[None, :] % period).astype(jnp.float32) * (
        2.0 * math.pi / period
    )
    factor = jnp.full(orders.shape, 1.0 / math.sqrt(period), jnp.float32)
    if inverse_form:
        factor = jnp.where(orders == 0, 1.0, 2.0).astype(jnp.float32) * factor
    stacked = jnp.stack(
        [factor[:, None] * jnp.cos(angles), -factor[:, None] * jnp.sin(angles)], axis=1
    )
    return stacked.astype(jnp.bfloat16)


def per_device(field, offsets, conv_weight, legendre, quad_weight, band_limit, mix_weight):
    channels, lat_rows, lon_cols = field.shape
    m_dev = legendre.shape[0]
    lon_count = lax.axis_size("lon")
    lat_count = lax.axis_size("lat")
    n_dev = lon_count * lat_count
    total_lon = lon_cols * lon_count
    total_lat = lat_rows * lat_count
    half_rows = total_lat // 2
    orders_all = m_dev * n_dev
    lon_points = lax.axis_index("lon") * lon_cols + lax.iota(jnp.int32, lon_cols)
    me = lax.axis_index("lat") * lon_count + lax.axis_index("lon")
    mine = me * m_dev + lax.iota(jnp.int32, m_dev)

    forward_rows = wave_table(
        lax.iota(jnp.int32, orders_all), lon_points, total_lon, False
    ).reshape(orders_all * 2, lon_cols)
    flat_field = field.reshape(channels * lat_rows, lon_cols)
    partial = lax.dot_general(
        forward_rows, flat_field, (((1,), (1,)), ((), ())), preferred_element_type=jnp.float32
    ).reshape(n_dev, m_dev, 2, channels, lat_rows)
    gathered_raw = lax.all_to_all(partial, BOTH, 0, 0, tiled=True)
    rim_cols = ((lon_cols + 4 + 127) // 128) * 128
    lat_n = lax.axis_size("lat")
    south = lax.ppermute(
        field[:, :2], "lat", [((i + 1), i) for i in range(lat_n - 1)]
    )
    north = lax.ppermute(
        field[:, lat_rows - 2 :], "lat", [(i, (i + 1)) for i in range(lat_n - 1)]
    )
    rows_ext = jnp.concatenate(
        [north, field, south, jnp.zeros((channels, 4, lon_cols), field.dtype)], axis=1
    )
    rim_rows = rows_ext.shape[1]
    east = lax.ppermute(
        rows_ext[:, :, :2], "lon", [((i + 1) % lon_count, i) for i in range(lon_count)]
    )
    west = lax.ppermute(
        rows_ext[:, :, lon_cols - 2 :], "lon", [(i, (i + 1) % lon_count) for i in range(lon_count)]
    )
    rim = jnp.concatenate(
        [
            rows_ext,
            east,
            jnp.zeros((channels, rim_rows, rim_cols - lon_cols - 4), field.dtype),
            west,
        ],
        axis=2,
    )
    conv_out = depthwise_conv(offsets, conv_weight, rim, lat_rows, lon_cols)
    gathered, conv_out = lax.optimization_barrier((gathered_raw, conv_out))
    summed = gathered.reshape(lat_count, lon_count, m_dev, 2, channels, lat_rows).sum(axis=1)
    raw_spec = jnp.transpose(summed, (1, 2, 3, 0, 4)).reshape(m_dev, 2, channels, total_lat)

    rim = jnp.pad(raw_spec, ((0, 0), (0, 0), (0, 0), (2, 2)))
    turns = ((mine[None, :] * offsets[:, 1:2]) % total_lon).astype(jnp.float32) * (
        2.0 * math.pi / total_lon
    )
    cos_all = jnp.cos(turns)
    sin_all = jnp.sin(turns)
    spec_acc = jnp.zeros(raw_spec.shape, jnp.float32)
    for tap_index in range(KTAPS):
        window = lax.dynamic_slice_in_dim(rim, 2 + offsets[tap_index, 0], total_lat, axis=3)
        cos_t = cos_all[tap_index][:, None, None]
        sin_t = sin_all[tap_index][:, None, None]
        real_part = cos_t * window[:, 0] - sin_t * window[:, 1]
        imag_part = sin_t * window[:, 0] + cos_t * window[:, 1]
        tap_w = conv_weight[:, tap_index][None, None, :, None]
        spec_acc = spec_acc + tap_w * jnp.stack([real_part, imag_part], axis=1)
    spectrum = spec_acc.astype(jnp.bfloat16)

    north_part = spectrum[..., :half_rows].astype(jnp.float32)
    south_part = jnp.flip(spectrum[..., half_rows:], axis=3).astype(jnp.float32)
    kept_mask = (mine[:, None] < band_limit[None, :]).astype(jnp.float32)
    weight_q = quad_weight[None, :] * kept_mask * (1.0 / math.sqrt(half_rows))
    even_terms = (weight_q[:, None, None, :] * (north_part + south_part)).astype(jnp.bfloat16)
    odd_terms = (weight_q[:, None, None, :] * (north_part - south_part)).astype(jnp.bfloat16)
    paired = legendre.reshape(m_dev, orders_all // 2, 2, half_rows)
    mix_pairs = mix_weight.reshape(2, orders_all // 2, 2, channels, channels)
    even_sum = jnp.zeros((m_dev, 2, channels, half_rows), jnp.float32)
    odd_sum = jnp.zeros((m_dev, 2, channels, half_rows), jnp.float32)
    for parity in range(2):
        same_parity = ((parity + mine) % 2 == 0)[:, None, None, None]
        operand = jnp.where(same_parity, even_terms, odd_terms)
        degree_plane = paired[:, :, parity]
        coeffs = jnp.einsum(
            "mui,mpci->mupc", degree_plane, operand, preferred_element_type=jnp.float32
        )
        degrees = 2 * lax.iota(jnp.int32, orders_all // 2) + parity
        triangle = (degrees[None, :] >= mine[:, None]).astype(jnp.float32)
        coeffs = (coeffs * triangle[:, :, None, None]).astype(jnp.bfloat16)
        with_real = jnp.einsum(
            "mupc,ucd->mupd", coeffs, mix_pairs[0, :, parity], preferred_element_type=jnp.float32
        )
        with_imag = jnp.einsum(
            "mupc,ucd->mupd", coeffs, mix_pairs[1, :, parity], preferred_element_type=jnp.float32
        )
        mixed = jnp.stack(
            [with_real[:, :, 0] - with_imag[:, :, 1], with_real[:, :, 1] + with_imag[:, :, 0]],
            axis=2,
        ).astype(jnp.bfloat16)
        returned = jnp.einsum(
            "mui,mupc->mpci", degree_plane, mixed, preferred_element_type=jnp.float32
        )
        even_sum = even_sum + jnp.where(same_parity, returned, 0.0)
        odd_sum = odd_sum + jnp.where(same_parity, 0.0, returned)
    north_out = (even_sum + odd_sum) * kept_mask[:, None, None, :]
    south_out = (even_sum - odd_sum) * kept_mask[:, None, None, :]
    grid_spectrum = jnp.concatenate([north_out, jnp.flip(south_out, axis=3)], axis=3).astype(
        jnp.bfloat16
    )

    by_group = jnp.transpose(
        grid_spectrum.reshape(m_dev, 2, channels, lat_count, lat_rows), (3, 0, 1, 2, 4)
    )
    outgoing = jnp.broadcast_to(
        by_group[:, None], (lat_count, lon_count, m_dev, 2, channels, lat_rows)
    ).reshape(n_dev, m_dev, 2, channels, lat_rows)
    full_rows = lax.all_to_all(outgoing, BOTH, 0, 0, tiled=True)
    spectral_rows = full_rows.reshape(orders_all * 2, channels * lat_rows)
    inverse_rows = wave_table(
        lax.iota(jnp.int32, orders_all), lon_points, total_lon, True
    ).reshape(orders_all * 2, lon_cols)
    synthesis = lax.dot_general(
        spectral_rows, inverse_rows, (((0,), (0,)), ((), ())), preferred_element_type=jnp.float32
    ).reshape(channels, lat_rows, lon_cols)

    return (conv_out.astype(jnp.float32) + jax.nn.gelu(synthesis, approximate=True)).astype(
        jnp.bfloat16
    )


def depthwise_conv(offsets, conv_weight, rim, lat_rows, lon_cols):
    channels, rim_rows, rim_cols = rim.shape
    block_c = 8
    chunk = 4
    flat = rim_rows * rim_cols

    def body(offs_ref, rim_ref, w_ref, out_ref, planes, shifted, result):
        tiles = rim_cols // 128
        for c in range(block_c):
            x = rim_ref[c].astype(jnp.float32)
            for t in range(tiles):
                planes[t, pl.ds(c * rim_rows, rim_rows), :] = x[:, t * 128 : (t + 1) * 128]
        for row in range(rim_rows):
            v = jnp.concatenate(
                [planes[t, pl.ds(row, block_c, stride=rim_rows), :] for t in range(tiles)], axis=1
            )
            for s in range(5):
                turn = (2 - s) % rim_cols
                shifted[s, :, pl.ds(row * rim_cols, rim_cols)] = (
                    v if turn == 0 else pltpu.roll(v, turn, 1)
                )
        weights = w_ref[...]
        for r0 in range(0, lat_rows, chunk):
            acc = jnp.zeros((block_c, chunk * rim_cols), jnp.float32)
            for k in range(KTAPS):
                dr = offs_ref[k, 0]
                dc = offs_ref[k, 1]
                start = pl.multiple_of((r0 + 2 + dr) * rim_cols, rim_cols)
                acc = acc + weights[:, k : k + 1] * shifted[dc + 2, :, pl.ds(start, chunk * rim_cols)]
            for i in range(chunk):
                for t in range(tiles):
                    result[t, pl.ds(r0 + i, block_c, stride=lat_rows), :] = acc[
                        :, i * rim_cols + t * 128 : i * rim_cols + (t + 1) * 128
                    ]
        for c in range(block_c):
            full = jnp.concatenate(
                [result[t, pl.ds(c * lat_rows, lat_rows), :] for t in range(tiles)], axis=1
            )
            out_ref[c] = full[:, :lon_cols].astype(jnp.bfloat16)

    return pl.pallas_call(
        body,
        grid_spec=pltpu.PrefetchScalarGridSpec(
            num_scalar_prefetch=1,
            grid=(channels // block_c,),
            in_specs=[
                pl.BlockSpec((block_c, rim_rows, rim_cols), lambda b, o: (b, 0, 0)),
                pl.BlockSpec((block_c, KTAPS), lambda b, o: (b, 0)),
            ],
            out_specs=pl.BlockSpec((block_c, lat_rows, lon_cols), lambda b, o: (b, 0, 0)),
            scratch_shapes=[
                pltpu.VMEM((rim_cols // 128, block_c * rim_rows, 128), jnp.float32),
                pltpu.VMEM((5, block_c, flat), jnp.float32),
                pltpu.VMEM((rim_cols // 128, block_c * lat_rows, 128), jnp.float32),
            ],
        ),
        out_shape=jax.ShapeDtypeStruct((channels, lat_rows, lon_cols), jnp.bfloat16),
        compiler_params=pltpu.CompilerParams(vmem_limit_bytes=48 * 1024 * 1024),
        cost_estimate=pl.CostEstimate(
            flops=8 * KTAPS * channels * rim_rows * rim_cols,
            transcendentals=0,
            bytes_accessed=channels * (rim_rows * rim_cols + lat_rows * lon_cols) * 2,
        ),
    )(offsets, rim, conv_weight)


def solution(mesh):
    placed = (P(None, "lat", "lon"), P(), P(), P(BOTH, None, None), P(), P(), P())
    return jax.shard_map(
        per_device, mesh=mesh, in_specs=placed, out_specs=P(None, "lat", "lon"), check_vma=False
    )
```

```python
import math

import jax
import jax.numpy as jnp
from jax import lax
from jax.sharding import PartitionSpec as P
from jax.experimental import pallas as pl
from jax.experimental.pallas import tpu as pltpu

KTAPS = 9
BOTH = ("lat", "lon")


def wave_table(orders, points, period, inverse_form):
    angles = (orders[:, None] * points[None, :] % period).astype(jnp.float32) * (
        2.0 * math.pi / period
    )
    factor = jnp.full(orders.shape, 1.0 / math.sqrt(period), jnp.float32)
    if inverse_form:
        factor = jnp.where(orders == 0, 1.0, 2.0).astype(jnp.float32) * factor
    stacked = jnp.stack(
        [factor[:, None] * jnp.cos(angles), -factor[:, None] * jnp.sin(angles)], axis=1
    )
    return stacked.astype(jnp.bfloat16)


def per_device(field, offsets, conv_weight, legendre, quad_weight, band_limit, mix_weight):
    channels, lat_rows, lon_cols = field.shape
    m_dev = legendre.shape[0]
    lon_count = lax.axis_size("lon")
    lat_count = lax.axis_size("lat")
    n_dev = lon_count * lat_count
    total_lon = lon_cols * lon_count
    total_lat = lat_rows * lat_count
    half_rows = total_lat // 2
    orders_all = m_dev * n_dev
    lon_points = lax.axis_index("lon") * lon_cols + lax.iota(jnp.int32, lon_cols)
    me = lax.axis_index("lat") * lon_count + lax.axis_index("lon")
    mine = me * m_dev + lax.iota(jnp.int32, m_dev)

    forward_rows = wave_table(
        lax.iota(jnp.int32, orders_all), lon_points, total_lon, False
    ).reshape(orders_all * 2, lon_cols)
    flat_field = field.reshape(channels * lat_rows, lon_cols)
    partial = lax.dot_general(
        forward_rows, flat_field, (((1,), (1,)), ((), ())), preferred_element_type=jnp.float32
    ).reshape(n_dev, m_dev * 2 * channels * lat_rows)
    gathered_raw = lax.all_to_all(partial, BOTH, 0, 0, tiled=True)
    rim_cols = ((lon_cols + 4 + 127) // 128) * 128
    lat_n = lax.axis_size("lat")
    south = lax.ppermute(
        field[:, :2], "lat", [((i + 1), i) for i in range(lat_n - 1)]
    )
    north = lax.ppermute(
        field[:, lat_rows - 2 :], "lat", [(i, (i + 1)) for i in range(lat_n - 1)]
    )
    rows_ext = jnp.concatenate(
        [north, field, south, jnp.zeros((channels, 4, lon_cols), field.dtype)], axis=1
    )
    rim_rows = rows_ext.shape[1]
    east = lax.ppermute(
        rows_ext[:, :, :2], "lon", [((i + 1) % lon_count, i) for i in range(lon_count)]
    )
    west = lax.ppermute(
        rows_ext[:, :, lon_cols - 2 :], "lon", [(i, (i + 1) % lon_count) for i in range(lon_count)]
    )
    rim = jnp.concatenate(
        [
            rows_ext,
            east,
            jnp.zeros((channels, rim_rows, rim_cols - lon_cols - 4), field.dtype),
            west,
        ],
        axis=2,
    )
    conv_out = depthwise_conv(offsets, conv_weight, rim, lat_rows, lon_cols)
    gathered, conv_out = lax.optimization_barrier((gathered_raw, conv_out))
    summed = gathered.reshape(lat_count, lon_count, m_dev * 2 * channels * lat_rows).sum(axis=1)
    summed = summed.reshape(lat_count, m_dev, 2, channels, lat_rows)
    raw_spec = jnp.transpose(summed, (1, 2, 3, 0, 4)).reshape(m_dev, 2, channels, total_lat)

    rim = jnp.pad(raw_spec, ((0, 0), (0, 0), (0, 0), (2, 2)))
    turns = ((mine[None, :] * offsets[:, 1:2]) % total_lon).astype(jnp.float32) * (
        2.0 * math.pi / total_lon
    )
    cos_all = jnp.cos(turns)
    sin_all = jnp.sin(turns)
    spec_acc = jnp.zeros(raw_spec.shape, jnp.float32)
    for tap_index in range(KTAPS):
        window = lax.dynamic_slice_in_dim(rim, 2 + offsets[tap_index, 0], total_lat, axis=3)
        cos_t = cos_all[tap_index][:, None, None]
        sin_t = sin_all[tap_index][:, None, None]
        real_part = cos_t * window[:, 0] - sin_t * window[:, 1]
        imag_part = sin_t * window[:, 0] + cos_t * window[:, 1]
        tap_w = conv_weight[:, tap_index][None, None, :, None]
        spec_acc = spec_acc + tap_w * jnp.stack([real_part, imag_part], axis=1)
    spectrum = spec_acc.astype(jnp.bfloat16)

    north_part = spectrum[..., :half_rows].astype(jnp.float32)
    south_part = jnp.flip(spectrum[..., half_rows:], axis=3).astype(jnp.float32)
    kept_mask = (mine[:, None] < band_limit[None, :]).astype(jnp.float32)
    weight_q = quad_weight[None, :] * kept_mask * (1.0 / math.sqrt(half_rows))
    even_terms = (weight_q[:, None, None, :] * (north_part + south_part)).astype(jnp.bfloat16)
    odd_terms = (weight_q[:, None, None, :] * (north_part - south_part)).astype(jnp.bfloat16)
    paired = legendre.reshape(m_dev, orders_all // 2, 2, half_rows)
    mix_pairs = mix_weight.reshape(2, orders_all // 2, 2, channels, channels)
    even_sum = jnp.zeros((m_dev, 2, channels, half_rows), jnp.float32)
    odd_sum = jnp.zeros((m_dev, 2, channels, half_rows), jnp.float32)
    for parity in range(2):
        same_parity = ((parity + mine) % 2 == 0)[:, None, None, None]
        operand = jnp.where(same_parity, even_terms, odd_terms)
        degree_plane = paired[:, :, parity]
        coeffs = jnp.einsum(
            "mui,mpci->mupc", degree_plane, operand, preferred_element_type=jnp.float32
        )
        degrees = 2 * lax.iota(jnp.int32, orders_all // 2) + parity
        triangle = (degrees[None, :] >= mine[:, None]).astype(jnp.float32)
        coeffs = (coeffs * triangle[:, :, None, None]).astype(jnp.bfloat16)
        with_real = jnp.einsum(
            "mupc,ucd->mupd", coeffs, mix_pairs[0, :, parity], preferred_element_type=jnp.float32
        )
        with_imag = jnp.einsum(
            "mupc,ucd->mupd", coeffs, mix_pairs[1, :, parity], preferred_element_type=jnp.float32
        )
        mixed = jnp.stack(
            [with_real[:, :, 0] - with_imag[:, :, 1], with_real[:, :, 1] + with_imag[:, :, 0]],
            axis=2,
        ).astype(jnp.bfloat16)
        returned = jnp.einsum(
            "mui,mupc->mpci", degree_plane, mixed, preferred_element_type=jnp.float32
        )
        even_sum = even_sum + jnp.where(same_parity, returned, 0.0)
        odd_sum = odd_sum + jnp.where(same_parity, 0.0, returned)
    north_out = (even_sum + odd_sum) * kept_mask[:, None, None, :]
    south_out = (even_sum - odd_sum) * kept_mask[:, None, None, :]
    grid_spectrum = jnp.concatenate([north_out, jnp.flip(south_out, axis=3)], axis=3).astype(
        jnp.bfloat16
    )

    by_group = jnp.transpose(
        grid_spectrum.reshape(m_dev, 2, channels, lat_count, lat_rows), (3, 0, 1, 2, 4)
    )
    outgoing = jnp.broadcast_to(
        by_group[:, None], (lat_count, lon_count, m_dev, 2, channels, lat_rows)
    ).reshape(n_dev, m_dev * 2 * channels * lat_rows)
    full_rows = lax.all_to_all(outgoing, BOTH, 0, 0, tiled=True)
    spectral_rows = full_rows.reshape(orders_all * 2, channels * lat_rows)
    inverse_rows = wave_table(
        lax.iota(jnp.int32, orders_all), lon_points, total_lon, True
    ).reshape(orders_all * 2, lon_cols)
    synthesis = lax.dot_general(
        spectral_rows, inverse_rows, (((0,), (0,)), ((), ())), preferred_element_type=jnp.float32
    ).reshape(channels, lat_rows, lon_cols)

    return (conv_out.astype(jnp.float32) + jax.nn.gelu(synthesis, approximate=True)).astype(
        jnp.bfloat16
    )


def depthwise_conv(offsets, conv_weight, rim, lat_rows, lon_cols):
    channels, rim_rows, rim_cols = rim.shape
    block_c = 8
    chunk = 4
    flat = rim_rows * rim_cols

    def body(offs_ref, rim_ref, w_ref, out_ref, planes, shifted, result):
        tiles = rim_cols // 128
        for c in range(block_c):
            x = rim_ref[c].astype(jnp.float32)
            for t in range(tiles):
                planes[t, pl.ds(c * rim_rows, rim_rows), :] = x[:, t * 128 : (t + 1) * 128]
        for row in range(rim_rows):
            v = jnp.concatenate(
                [planes[t, pl.ds(row, block_c, stride=rim_rows), :] for t in range(tiles)], axis=1
            )
            for s in range(5):
                turn = (2 - s) % rim_cols
                shifted[s, :, pl.ds(row * rim_cols, rim_cols)] = (
                    v if turn == 0 else pltpu.roll(v, turn, 1)
                )
        weights = w_ref[...]
        for r0 in range(0, lat_rows, chunk):
            acc = jnp.zeros((block_c, chunk * rim_cols), jnp.float32)
            for k in range(KTAPS):
                dr = offs_ref[k, 0]
                dc = offs_ref[k, 1]
                start = pl.multiple_of((r0 + 2 + dr) * rim_cols, rim_cols)
                acc = acc + weights[:, k : k + 1] * shifted[dc + 2, :, pl.ds(start, chunk * rim_cols)]
            for i in range(chunk):
                for t in range(tiles):
                    result[t, pl.ds(r0 + i, block_c, stride=lat_rows), :] = acc[
                        :, i * rim_cols + t * 128 : i * rim_cols + (t + 1) * 128
                    ]
        for c in range(block_c):
            full = jnp.concatenate(
                [result[t, pl.ds(c * lat_rows, lat_rows), :] for t in range(tiles)], axis=1
            )
            out_ref[c] = full[:, :lon_cols].astype(jnp.bfloat16)

    return pl.pallas_call(
        body,
        grid_spec=pltpu.PrefetchScalarGridSpec(
            num_scalar_prefetch=1,
            grid=(channels // block_c,),
            in_specs=[
                pl.BlockSpec((block_c, rim_rows, rim_cols), lambda b, o: (b, 0, 0)),
                pl.BlockSpec((block_c, KTAPS), lambda b, o: (b, 0)),
            ],
            out_specs=pl.BlockSpec((block_c, lat_rows, lon_cols), lambda b, o: (b, 0, 0)),
            scratch_shapes=[
                pltpu.VMEM((rim_cols // 128, block_c * rim_rows, 128), jnp.float32),
                pltpu.VMEM((5, block_c, flat), jnp.float32),
                pltpu.VMEM((rim_cols // 128, block_c * lat_rows, 128), jnp.float32),
            ],
        ),
        out_shape=jax.ShapeDtypeStruct((channels, lat_rows, lon_cols), jnp.bfloat16),
        compiler_params=pltpu.CompilerParams(vmem_limit_bytes=48 * 1024 * 1024),
        cost_estimate=pl.CostEstimate(
            flops=8 * KTAPS * channels * rim_rows * rim_cols,
            transcendentals=0,
            bytes_accessed=channels * (rim_rows * rim_cols + lat_rows * lon_cols) * 2,
        ),
    )(offsets, rim, conv_weight)


def solution(mesh):
    placed = (P(None, "lat", "lon"), P(), P(), P(BOTH, None, None), P(), P(), P())
    return jax.shard_map(
        per_device, mesh=mesh, in_specs=placed, out_specs=P(None, "lat", "lon"), check_vma=False
    )
```

```python
import math

import jax
import jax.numpy as jnp
from jax import lax
from jax.sharding import PartitionSpec as P
from jax.experimental import pallas as pl
from jax.experimental.pallas import tpu as pltpu

KTAPS = 9
BOTH = ("lat", "lon")


def wave_table(orders, points, period, inverse_form):
    angles = (orders[:, None] * points[None, :] % period).astype(jnp.float32) * (
        2.0 * math.pi / period
    )
    factor = jnp.full(orders.shape, 1.0 / math.sqrt(period), jnp.float32)
    if inverse_form:
        factor = jnp.where(orders == 0, 1.0, 2.0).astype(jnp.float32) * factor
    stacked = jnp.stack(
        [factor[:, None] * jnp.cos(angles), -factor[:, None] * jnp.sin(angles)], axis=1
    )
    return stacked.astype(jnp.bfloat16)


def per_device(field, offsets, conv_weight, legendre, quad_weight, band_limit, mix_weight):
    channels, lat_rows, lon_cols = field.shape
    m_dev = legendre.shape[0]
    lon_count = lax.axis_size("lon")
    lat_count = lax.axis_size("lat")
    n_dev = lon_count * lat_count
    total_lon = lon_cols * lon_count
    total_lat = lat_rows * lat_count
    half_rows = total_lat // 2
    orders_all = m_dev * n_dev
    lon_points = lax.axis_index("lon") * lon_cols + lax.iota(jnp.int32, lon_cols)
    me = lax.axis_index("lat") * lon_count + lax.axis_index("lon")
    mine = me * m_dev + lax.iota(jnp.int32, m_dev)

    forward_rows = wave_table(
        lax.iota(jnp.int32, orders_all), lon_points, total_lon, False
    ).reshape(orders_all * 2, lon_cols)
    flat_field = field.reshape(channels * lat_rows, lon_cols)
    partial = lax.dot_general(
        forward_rows, flat_field, (((1,), (1,)), ((), ())), preferred_element_type=jnp.float32
    ).reshape(n_dev, m_dev * 2 * channels * lat_rows)
    gathered_raw = lax.all_to_all(partial, BOTH, 0, 0, tiled=True)
    rim_cols = ((lon_cols + 4 + 127) // 128) * 128
    lat_n = lax.axis_size("lat")
    south = lax.ppermute(
        field[:, :2], "lat", [((i + 1), i) for i in range(lat_n - 1)]
    )
    north = lax.ppermute(
        field[:, lat_rows - 2 :], "lat", [(i, (i + 1)) for i in range(lat_n - 1)]
    )
    rows_ext = jnp.concatenate(
        [north, field, south, jnp.zeros((channels, 4, lon_cols), field.dtype)], axis=1
    )
    rim_rows = rows_ext.shape[1]
    def lane_dense(edge):
        return jnp.transpose(edge, (2, 0, 1)).reshape(2, channels * rim_rows)

    def from_lanes(packed):
        return jnp.transpose(packed.reshape(2, channels, rim_rows), (1, 2, 0))

    east = from_lanes(
        lax.ppermute(
            lane_dense(rows_ext[:, :, :2]),
            "lon",
            [((i + 1) % lon_count, i) for i in range(lon_count)],
        )
    )
    west = from_lanes(
        lax.ppermute(
            lane_dense(rows_ext[:, :, lon_cols - 2 :]),
            "lon",
            [(i, (i + 1) % lon_count) for i in range(lon_count)],
        )
    )
    rim = jnp.concatenate(
        [
            rows_ext,
            east,
            jnp.zeros((channels, rim_rows, rim_cols - lon_cols - 4), field.dtype),
            west,
        ],
        axis=2,
    )
    conv_out = depthwise_conv(offsets, conv_weight, rim, lat_rows, lon_cols)
    gathered, conv_out = lax.optimization_barrier((gathered_raw, conv_out))
    summed = gathered.reshape(lat_count, lon_count, m_dev * 2 * channels * lat_rows).sum(axis=1)
    summed = summed.reshape(lat_count, m_dev, 2, channels, lat_rows)
    raw_spec = jnp.transpose(summed, (1, 2, 3, 0, 4)).reshape(m_dev, 2, channels, total_lat)

    rim = jnp.pad(raw_spec, ((0, 0), (0, 0), (0, 0), (2, 2)))
    turns = ((mine[None, :] * offsets[:, 1:2]) % total_lon).astype(jnp.float32) * (
        2.0 * math.pi / total_lon
    )
    cos_all = jnp.cos(turns)
    sin_all = jnp.sin(turns)
    spec_acc = jnp.zeros(raw_spec.shape, jnp.float32)
    for tap_index in range(KTAPS):
        window = lax.dynamic_slice_in_dim(rim, 2 + offsets[tap_index, 0], total_lat, axis=3)
        cos_t = cos_all[tap_index][:, None, None]
        sin_t = sin_all[tap_index][:, None, None]
        real_part = cos_t * window[:, 0] - sin_t * window[:, 1]
        imag_part = sin_t * window[:, 0] + cos_t * window[:, 1]
        tap_w = conv_weight[:, tap_index][None, None, :, None]
        spec_acc = spec_acc + tap_w * jnp.stack([real_part, imag_part], axis=1)
    spectrum = spec_acc.astype(jnp.bfloat16)

    north_part = spectrum[..., :half_rows].astype(jnp.float32)
    south_part = jnp.flip(spectrum[..., half_rows:], axis=3).astype(jnp.float32)
    kept_mask = (mine[:, None] < band_limit[None, :]).astype(jnp.float32)
    weight_q = quad_weight[None, :] * kept_mask * (1.0 / math.sqrt(half_rows))
    even_terms = (weight_q[:, None, None, :] * (north_part + south_part)).astype(jnp.bfloat16)
    odd_terms = (weight_q[:, None, None, :] * (north_part - south_part)).astype(jnp.bfloat16)
    paired = legendre.reshape(m_dev, orders_all // 2, 2, half_rows)
    mix_pairs = mix_weight.reshape(2, orders_all // 2, 2, channels, channels)
    even_sum = jnp.zeros((m_dev, 2, channels, half_rows), jnp.float32)
    odd_sum = jnp.zeros((m_dev, 2, channels, half_rows), jnp.float32)
    for parity in range(2):
        same_parity = ((parity + mine) % 2 == 0)[:, None, None, None]
        operand = jnp.where(same_parity, even_terms, odd_terms)
        degree_plane = paired[:, :, parity]
        coeffs = jnp.einsum(
            "mui,mpci->mupc", degree_plane, operand, preferred_element_type=jnp.float32
        )
        degrees = 2 * lax.iota(jnp.int32, orders_all // 2) + parity
        triangle = (degrees[None, :] >= mine[:, None]).astype(jnp.float32)
        coeffs = (coeffs * triangle[:, :, None, None]).astype(jnp.bfloat16)
        with_real = jnp.einsum(
            "mupc,ucd->mupd", coeffs, mix_pairs[0, :, parity], preferred_element_type=jnp.float32
        )
        with_imag = jnp.einsum(
            "mupc,ucd->mupd", coeffs, mix_pairs[1, :, parity], preferred_element_type=jnp.float32
        )
        mixed = jnp.stack(
            [with_real[:, :, 0] - with_imag[:, :, 1], with_real[:, :, 1] + with_imag[:, :, 0]],
            axis=2,
        ).astype(jnp.bfloat16)
        returned = jnp.einsum(
            "mui,mupc->mpci", degree_plane, mixed, preferred_element_type=jnp.float32
        )
        even_sum = even_sum + jnp.where(same_parity, returned, 0.0)
        odd_sum = odd_sum + jnp.where(same_parity, 0.0, returned)
    north_out = (even_sum + odd_sum) * kept_mask[:, None, None, :]
    south_out = (even_sum - odd_sum) * kept_mask[:, None, None, :]
    grid_spectrum = jnp.concatenate([north_out, jnp.flip(south_out, axis=3)], axis=3).astype(
        jnp.bfloat16
    )

    by_group = jnp.transpose(
        grid_spectrum.reshape(m_dev, 2, channels, lat_count, lat_rows), (3, 0, 1, 2, 4)
    )
    outgoing = jnp.broadcast_to(
        by_group[:, None], (lat_count, lon_count, m_dev, 2, channels, lat_rows)
    ).reshape(n_dev, m_dev * 2 * channels * lat_rows)
    full_rows = lax.all_to_all(outgoing, BOTH, 0, 0, tiled=True)
    spectral_rows = full_rows.reshape(orders_all * 2, channels * lat_rows)
    inverse_rows = wave_table(
        lax.iota(jnp.int32, orders_all), lon_points, total_lon, True
    ).reshape(orders_all * 2, lon_cols)
    synthesis = lax.dot_general(
        spectral_rows, inverse_rows, (((0,), (0,)), ((), ())), preferred_element_type=jnp.float32
    ).reshape(channels, lat_rows, lon_cols)

    return (conv_out.astype(jnp.float32) + jax.nn.gelu(synthesis, approximate=True)).astype(
        jnp.bfloat16
    )


def depthwise_conv(offsets, conv_weight, rim, lat_rows, lon_cols):
    channels, rim_rows, rim_cols = rim.shape
    block_c = 8
    chunk = 4
    flat = rim_rows * rim_cols

    def body(offs_ref, rim_ref, w_ref, out_ref, planes, shifted, result):
        tiles = rim_cols // 128
        for c in range(block_c):
            x = rim_ref[c].astype(jnp.float32)
            for t in range(tiles):
                planes[t, pl.ds(c * rim_rows, rim_rows), :] = x[:, t * 128 : (t + 1) * 128]
        for row in range(rim_rows):
            v = jnp.concatenate(
                [planes[t, pl.ds(row, block_c, stride=rim_rows), :] for t in range(tiles)], axis=1
            )
            for s in range(5):
                turn = (2 - s) % rim_cols
                shifted[s, :, pl.ds(row * rim_cols, rim_cols)] = (
                    v if turn == 0 else pltpu.roll(v, turn, 1)
                )
        weights = w_ref[...]
        for r0 in range(0, lat_rows, chunk):
            acc = jnp.zeros((block_c, chunk * rim_cols), jnp.float32)
            for k in range(KTAPS):
                dr = offs_ref[k, 0]
                dc = offs_ref[k, 1]
                start = pl.multiple_of((r0 + 2 + dr) * rim_cols, rim_cols)
                acc = acc + weights[:, k : k + 1] * shifted[dc + 2, :, pl.ds(start, chunk * rim_cols)]
            for i in range(chunk):
                for t in range(tiles):
                    result[t, pl.ds(r0 + i, block_c, stride=lat_rows), :] = acc[
                        :, i * rim_cols + t * 128 : i * rim_cols + (t + 1) * 128
                    ]
        for c in range(block_c):
            full = jnp.concatenate(
                [result[t, pl.ds(c * lat_rows, lat_rows), :] for t in range(tiles)], axis=1
            )
            out_ref[c] = full[:, :lon_cols].astype(jnp.bfloat16)

    return pl.pallas_call(
        body,
        grid_spec=pltpu.PrefetchScalarGridSpec(
            num_scalar_prefetch=1,
            grid=(channels // block_c,),
            in_specs=[
                pl.BlockSpec((block_c, rim_rows, rim_cols), lambda b, o: (b, 0, 0)),
                pl.BlockSpec((block_c, KTAPS), lambda b, o: (b, 0)),
            ],
            out_specs=pl.BlockSpec((block_c, lat_rows, lon_cols), lambda b, o: (b, 0, 0)),
            scratch_shapes=[
                pltpu.VMEM((rim_cols // 128, block_c * rim_rows, 128), jnp.float32),
                pltpu.VMEM((5, block_c, flat), jnp.float32),
                pltpu.VMEM((rim_cols // 128, block_c * lat_rows, 128), jnp.float32),
            ],
        ),
        out_shape=jax.ShapeDtypeStruct((channels, lat_rows, lon_cols), jnp.bfloat16),
        compiler_params=pltpu.CompilerParams(vmem_limit_bytes=48 * 1024 * 1024),
        cost_estimate=pl.CostEstimate(
            flops=8 * KTAPS * channels * rim_rows * rim_cols,
            transcendentals=0,
            bytes_accessed=channels * (rim_rows * rim_cols + lat_rows * lon_cols) * 2,
        ),
    )(offsets, rim, conv_weight)


def solution(mesh):
    placed = (P(None, "lat", "lon"), P(), P(), P(BOTH, None, None), P(), P(), P())
    return jax.shard_map(
        per_device, mesh=mesh, in_specs=placed, out_specs=P(None, "lat", "lon"), check_vma=False
    )
```

```python
import math

import jax
import jax.numpy as jnp
from jax import lax
from jax.sharding import PartitionSpec as P
from jax.experimental import pallas as pl
from jax.experimental.pallas import tpu as pltpu

KTAPS = 9
BOTH = ("lat", "lon")


def wave_table(orders, points, period, inverse_form):
    angles = (orders[:, None] * points[None, :] % period).astype(jnp.float32) * (
        2.0 * math.pi / period
    )
    factor = jnp.full(orders.shape, 1.0 / math.sqrt(period), jnp.float32)
    if inverse_form:
        factor = jnp.where(orders == 0, 1.0, 2.0).astype(jnp.float32) * factor
    stacked = jnp.stack(
        [factor[:, None] * jnp.cos(angles), -factor[:, None] * jnp.sin(angles)], axis=1
    )
    return stacked.astype(jnp.bfloat16)


def per_device(field, offsets, conv_weight, legendre, quad_weight, band_limit, mix_weight):
    channels, lat_rows, lon_cols = field.shape
    m_dev = legendre.shape[0]
    lon_count = lax.axis_size("lon")
    lat_count = lax.axis_size("lat")
    n_dev = lon_count * lat_count
    total_lon = lon_cols * lon_count
    total_lat = lat_rows * lat_count
    half_rows = total_lat // 2
    orders_all = m_dev * n_dev
    lon_points = lax.axis_index("lon") * lon_cols + lax.iota(jnp.int32, lon_cols)
    me = lax.axis_index("lat") * lon_count + lax.axis_index("lon")
    mine = me * m_dev + lax.iota(jnp.int32, m_dev)

    forward_rows = wave_table(
        lax.iota(jnp.int32, orders_all), lon_points, total_lon, False
    ).reshape(orders_all * 2, lon_cols)
    flat_field = field.reshape(channels * lat_rows, lon_cols)
    partial = lax.dot_general(
        forward_rows, flat_field, (((1,), (1,)), ((), ())), preferred_element_type=jnp.float32
    ).reshape(n_dev, 8, m_dev * 2 * channels * lat_rows // 8)
    gathered_raw = lax.all_to_all(partial, BOTH, 0, 0, tiled=True)
    rim_cols = ((lon_cols + 4 + 127) // 128) * 128
    lat_n = lax.axis_size("lat")
    south = lax.ppermute(
        field[:, :2], "lat", [((i + 1), i) for i in range(lat_n - 1)]
    )
    north = lax.ppermute(
        field[:, lat_rows - 2 :], "lat", [(i, (i + 1)) for i in range(lat_n - 1)]
    )
    rows_ext = jnp.concatenate(
        [north, field, south, jnp.zeros((channels, 4, lon_cols), field.dtype)], axis=1
    )
    rim_rows = rows_ext.shape[1]
    def lane_dense(edge):
        return jnp.transpose(edge, (2, 0, 1)).reshape(2, channels * rim_rows)

    def from_lanes(packed):
        return jnp.transpose(packed.reshape(2, channels, rim_rows), (1, 2, 0))

    east = from_lanes(
        lax.ppermute(
            lane_dense(rows_ext[:, :, :2]),
            "lon",
            [((i + 1) % lon_count, i) for i in range(lon_count)],
        )
    )
    west = from_lanes(
        lax.ppermute(
            lane_dense(rows_ext[:, :, lon_cols - 2 :]),
            "lon",
            [(i, (i + 1) % lon_count) for i in range(lon_count)],
        )
    )
    rim = jnp.concatenate(
        [
            rows_ext,
            east,
            jnp.zeros((channels, rim_rows, rim_cols - lon_cols - 4), field.dtype),
            west,
        ],
        axis=2,
    )
    conv_out = depthwise_conv(offsets, conv_weight, rim, lat_rows, lon_cols)
    gathered, conv_out = lax.optimization_barrier((gathered_raw, conv_out))
    summed = gathered.reshape(lat_count, lon_count, m_dev * 2 * channels * lat_rows).sum(axis=1)
    summed = summed.reshape(lat_count, m_dev, 2, channels, lat_rows)
    raw_spec = jnp.transpose(summed, (1, 2, 3, 0, 4)).reshape(m_dev, 2, channels, total_lat)

    rim = jnp.pad(raw_spec, ((0, 0), (0, 0), (0, 0), (2, 2)))
    turns = ((mine[None, :] * offsets[:, 1:2]) % total_lon).astype(jnp.float32) * (
        2.0 * math.pi / total_lon
    )
    cos_all = jnp.cos(turns)
    sin_all = jnp.sin(turns)
    spec_acc = jnp.zeros(raw_spec.shape, jnp.float32)
    for tap_index in range(KTAPS):
        window = lax.dynamic_slice_in_dim(rim, 2 + offsets[tap_index, 0], total_lat, axis=3)
        cos_t = cos_all[tap_index][:, None, None]
        sin_t = sin_all[tap_index][:, None, None]
        real_part = cos_t * window[:, 0] - sin_t * window[:, 1]
        imag_part = sin_t * window[:, 0] + cos_t * window[:, 1]
        tap_w = conv_weight[:, tap_index][None, None, :, None]
        spec_acc = spec_acc + tap_w * jnp.stack([real_part, imag_part], axis=1)
    spectrum = spec_acc.astype(jnp.bfloat16)

    north_part = spectrum[..., :half_rows].astype(jnp.float32)
    south_part = jnp.flip(spectrum[..., half_rows:], axis=3).astype(jnp.float32)
    kept_mask = (mine[:, None] < band_limit[None, :]).astype(jnp.float32)
    weight_q = quad_weight[None, :] * kept_mask * (1.0 / math.sqrt(half_rows))
    even_terms = (weight_q[:, None, None, :] * (north_part + south_part)).astype(jnp.bfloat16)
    odd_terms = (weight_q[:, None, None, :] * (north_part - south_part)).astype(jnp.bfloat16)
    paired = legendre.reshape(m_dev, orders_all // 2, 2, half_rows)
    mix_pairs = mix_weight.reshape(2, orders_all // 2, 2, channels, channels)
    even_sum = jnp.zeros((m_dev, 2, channels, half_rows), jnp.float32)
    odd_sum = jnp.zeros((m_dev, 2, channels, half_rows), jnp.float32)
    for parity in range(2):
        same_parity = ((parity + mine) % 2 == 0)[:, None, None, None]
        operand = jnp.where(same_parity, even_terms, odd_terms)
        degree_plane = paired[:, :, parity]
        coeffs = jnp.einsum(
            "mui,mpci->mupc", degree_plane, operand, preferred_element_type=jnp.float32
        )
        degrees = 2 * lax.iota(jnp.int32, orders_all // 2) + parity
        triangle = (degrees[None, :] >= mine[:, None]).astype(jnp.float32)
        coeffs = (coeffs * triangle[:, :, None, None]).astype(jnp.bfloat16)
        with_real = jnp.einsum(
            "mupc,ucd->mupd", coeffs, mix_pairs[0, :, parity], preferred_element_type=jnp.float32
        )
        with_imag = jnp.einsum(
            "mupc,ucd->mupd", coeffs, mix_pairs[1, :, parity], preferred_element_type=jnp.float32
        )
        mixed = jnp.stack(
            [with_real[:, :, 0] - with_imag[:, :, 1], with_real[:, :, 1] + with_imag[:, :, 0]],
            axis=2,
        ).astype(jnp.bfloat16)
        returned = jnp.einsum(
            "mui,mupc->mpci", degree_plane, mixed, preferred_element_type=jnp.float32
        )
        even_sum = even_sum + jnp.where(same_parity, returned, 0.0)
        odd_sum = odd_sum + jnp.where(same_parity, 0.0, returned)
    north_out = (even_sum + odd_sum) * kept_mask[:, None, None, :]
    south_out = (even_sum - odd_sum) * kept_mask[:, None, None, :]
    grid_spectrum = jnp.concatenate([north_out, jnp.flip(south_out, axis=3)], axis=3).astype(
        jnp.bfloat16
    )

    by_group = jnp.transpose(
        grid_spectrum.reshape(m_dev, 2, channels, lat_count, lat_rows), (3, 0, 1, 2, 4)
    )
    outgoing = jnp.broadcast_to(
        by_group[:, None], (lat_count, lon_count, m_dev, 2, channels, lat_rows)
    ).reshape(n_dev, 16, m_dev * 2 * channels * lat_rows // 16)
    full_rows = lax.all_to_all(outgoing, BOTH, 0, 0, tiled=True)
    spectral_rows = full_rows.reshape(orders_all * 2, channels * lat_rows)
    inverse_rows = wave_table(
        lax.iota(jnp.int32, orders_all), lon_points, total_lon, True
    ).reshape(orders_all * 2, lon_cols)
    synthesis = lax.dot_general(
        spectral_rows, inverse_rows, (((0,), (0,)), ((), ())), preferred_element_type=jnp.float32
    ).reshape(channels, lat_rows, lon_cols)

    return (conv_out.astype(jnp.float32) + jax.nn.gelu(synthesis, approximate=True)).astype(
        jnp.bfloat16
    )


def depthwise_conv(offsets, conv_weight, rim, lat_rows, lon_cols):
    channels, rim_rows, rim_cols = rim.shape
    block_c = 8
    chunk = 4
    flat = rim_rows * rim_cols

    def body(offs_ref, rim_ref, w_ref, out_ref, planes, shifted, result):
        tiles = rim_cols // 128
        for c in range(block_c):
            x = rim_ref[c].astype(jnp.float32)
            for t in range(tiles):
                planes[t, pl.ds(c * rim_rows, rim_rows), :] = x[:, t * 128 : (t + 1) * 128]
        for row in range(rim_rows):
            v = jnp.concatenate(
                [planes[t, pl.ds(row, block_c, stride=rim_rows), :] for t in range(tiles)], axis=1
            )
            for s in range(5):
                turn = (2 - s) % rim_cols
                shifted[s, :, pl.ds(row * rim_cols, rim_cols)] = (
                    v if turn == 0 else pltpu.roll(v, turn, 1)
                )
        weights = w_ref[...]
        for r0 in range(0, lat_rows, chunk):
            acc = jnp.zeros((block_c, chunk * rim_cols), jnp.float32)
            for k in range(KTAPS):
                dr = offs_ref[k, 0]
                dc = offs_ref[k, 1]
                start = pl.multiple_of((r0 + 2 + dr) * rim_cols, rim_cols)
                acc = acc + weights[:, k : k + 1] * shifted[dc + 2, :, pl.ds(start, chunk * rim_cols)]
            for i in range(chunk):
                for t in range(tiles):
                    result[t, pl.ds(r0 + i, block_c, stride=lat_rows), :] = acc[
                        :, i * rim_cols + t * 128 : i * rim_cols + (t + 1) * 128
                    ]
        for c in range(block_c):
            full = jnp.concatenate(
                [result[t, pl.ds(c * lat_rows, lat_rows), :] for t in range(tiles)], axis=1
            )
            out_ref[c] = full[:, :lon_cols].astype(jnp.bfloat16)

    return pl.pallas_call(
        body,
        grid_spec=pltpu.PrefetchScalarGridSpec(
            num_scalar_prefetch=1,
            grid=(channels // block_c,),
            in_specs=[
                pl.BlockSpec((block_c, rim_rows, rim_cols), lambda b, o: (b, 0, 0)),
                pl.BlockSpec((block_c, KTAPS), lambda b, o: (b, 0)),
            ],
            out_specs=pl.BlockSpec((block_c, lat_rows, lon_cols), lambda b, o: (b, 0, 0)),
            scratch_shapes=[
                pltpu.VMEM((rim_cols // 128, block_c * rim_rows, 128), jnp.float32),
                pltpu.VMEM((5, block_c, flat), jnp.float32),
                pltpu.VMEM((rim_cols // 128, block_c * lat_rows, 128), jnp.float32),
            ],
        ),
        out_shape=jax.ShapeDtypeStruct((channels, lat_rows, lon_cols), jnp.bfloat16),
        compiler_params=pltpu.CompilerParams(vmem_limit_bytes=48 * 1024 * 1024),
        cost_estimate=pl.CostEstimate(
            flops=8 * KTAPS * channels * rim_rows * rim_cols,
            transcendentals=0,
            bytes_accessed=channels * (rim_rows * rim_cols + lat_rows * lon_cols) * 2,
        ),
    )(offsets, rim, conv_weight)


def solution(mesh):
    placed = (P(None, "lat", "lon"), P(), P(), P(BOTH, None, None), P(), P(), P())
    return jax.shard_map(
        per_device, mesh=mesh, in_specs=placed, out_specs=P(None, "lat", "lon"), check_vma=False
    )
```

```python
import math

import jax
import jax.numpy as jnp
from jax import lax
from jax.sharding import PartitionSpec as P
from jax.experimental import pallas as pl
from jax.experimental.pallas import tpu as pltpu

KTAPS = 9
BOTH = ("lat", "lon")


def wave_table(orders, points, period, inverse_form):
    angles = (orders[:, None] * points[None, :] % period).astype(jnp.float32) * (
        2.0 * math.pi / period
    )
    factor = jnp.full(orders.shape, 1.0 / math.sqrt(period), jnp.float32)
    if inverse_form:
        factor = jnp.where(orders == 0, 1.0, 2.0).astype(jnp.float32) * factor
    stacked = jnp.stack(
        [factor[:, None] * jnp.cos(angles), -factor[:, None] * jnp.sin(angles)], axis=1
    )
    return stacked.astype(jnp.bfloat16)


def per_device(field, offsets, conv_weight, legendre, quad_weight, band_limit, mix_weight):
    channels, lat_rows, lon_cols = field.shape
    m_dev = legendre.shape[0]
    lon_count = lax.axis_size("lon")
    lat_count = lax.axis_size("lat")
    n_dev = lon_count * lat_count
    total_lon = lon_cols * lon_count
    total_lat = lat_rows * lat_count
    half_rows = total_lat // 2
    orders_all = m_dev * n_dev
    lon_points = lax.axis_index("lon") * lon_cols + lax.iota(jnp.int32, lon_cols)
    me = lax.axis_index("lat") * lon_count + lax.axis_index("lon")
    mine = me * m_dev + lax.iota(jnp.int32, m_dev)

    forward_rows = wave_table(
        lax.iota(jnp.int32, orders_all), lon_points, total_lon, False
    ).reshape(orders_all * 2, lon_cols)
    flat_field = field.reshape(channels * lat_rows, lon_cols)
    partial = lax.dot_general(
        forward_rows, flat_field, (((1,), (1,)), ((), ())), preferred_element_type=jnp.float32
    ).reshape(n_dev, 16, m_dev * 2 * channels * lat_rows // 16)
    gathered_raw = lax.all_to_all(partial.astype(jnp.bfloat16), BOTH, 0, 0, tiled=True)
    rim_cols = ((lon_cols + 4 + 127) // 128) * 128
    lat_n = lax.axis_size("lat")
    south = lax.ppermute(
        field[:, :2], "lat", [((i + 1), i) for i in range(lat_n - 1)]
    )
    north = lax.ppermute(
        field[:, lat_rows - 2 :], "lat", [(i, (i + 1)) for i in range(lat_n - 1)]
    )
    rows_ext = jnp.concatenate(
        [north, field, south, jnp.zeros((channels, 4, lon_cols), field.dtype)], axis=1
    )
    rim_rows = rows_ext.shape[1]
    def lane_dense(edge):
        return jnp.transpose(edge, (2, 0, 1)).reshape(2, channels * rim_rows)

    def from_lanes(packed):
        return jnp.transpose(packed.reshape(2, channels, rim_rows), (1, 2, 0))

    east = from_lanes(
        lax.ppermute(
            lane_dense(rows_ext[:, :, :2]),
            "lon",
            [((i + 1) % lon_count, i) for i in range(lon_count)],
        )
    )
    west = from_lanes(
        lax.ppermute(
            lane_dense(rows_ext[:, :, lon_cols - 2 :]),
            "lon",
            [(i, (i + 1) % lon_count) for i in range(lon_count)],
        )
    )
    rim = jnp.concatenate(
        [
            rows_ext,
            east,
            jnp.zeros((channels, rim_rows, rim_cols - lon_cols - 4), field.dtype),
            west,
        ],
        axis=2,
    )
    conv_out = depthwise_conv(offsets, conv_weight, rim, lat_rows, lon_cols)
    gathered, conv_out = lax.optimization_barrier((gathered_raw, conv_out))
    summed = (
        gathered.astype(jnp.float32)
        .reshape(lat_count, lon_count, m_dev * 2 * channels * lat_rows)
        .sum(axis=1)
    )
    summed = summed.reshape(lat_count, m_dev, 2, channels, lat_rows)
    raw_spec = jnp.transpose(summed, (1, 2, 3, 0, 4)).reshape(m_dev, 2, channels, total_lat)

    rim = jnp.pad(raw_spec, ((0, 0), (0, 0), (0, 0), (2, 2)))
    turns = ((mine[None, :] * offsets[:, 1:2]) % total_lon).astype(jnp.float32) * (
        2.0 * math.pi / total_lon
    )
    cos_all = jnp.cos(turns)
    sin_all = jnp.sin(turns)
    spec_acc = jnp.zeros(raw_spec.shape, jnp.float32)
    for tap_index in range(KTAPS):
        window = lax.dynamic_slice_in_dim(rim, 2 + offsets[tap_index, 0], total_lat, axis=3)
        cos_t = cos_all[tap_index][:, None, None]
        sin_t = sin_all[tap_index][:, None, None]
        real_part = cos_t * window[:, 0] - sin_t * window[:, 1]
        imag_part = sin_t * window[:, 0] + cos_t * window[:, 1]
        tap_w = conv_weight[:, tap_index][None, None, :, None]
        spec_acc = spec_acc + tap_w * jnp.stack([real_part, imag_part], axis=1)
    spectrum = spec_acc.astype(jnp.bfloat16)

    north_part = spectrum[..., :half_rows].astype(jnp.float32)
    south_part = jnp.flip(spectrum[..., half_rows:], axis=3).astype(jnp.float32)
    kept_mask = (mine[:, None] < band_limit[None, :]).astype(jnp.float32)
    weight_q = quad_weight[None, :] * kept_mask * (1.0 / math.sqrt(half_rows))
    even_terms = (weight_q[:, None, None, :] * (north_part + south_part)).astype(jnp.bfloat16)
    odd_terms = (weight_q[:, None, None, :] * (north_part - south_part)).astype(jnp.bfloat16)
    paired = legendre.reshape(m_dev, orders_all // 2, 2, half_rows)
    mix_pairs = mix_weight.reshape(2, orders_all // 2, 2, channels, channels)
    even_sum = jnp.zeros((m_dev, 2, channels, half_rows), jnp.float32)
    odd_sum = jnp.zeros((m_dev, 2, channels, half_rows), jnp.float32)
    for parity in range(2):
        same_parity = ((parity + mine) % 2 == 0)[:, None, None, None]
        operand = jnp.where(same_parity, even_terms, odd_terms)
        degree_plane = paired[:, :, parity]
        coeffs = jnp.einsum(
            "mui,mpci->mupc", degree_plane, operand, preferred_element_type=jnp.float32
        )
        degrees = 2 * lax.iota(jnp.int32, orders_all // 2) + parity
        triangle = (degrees[None, :] >= mine[:, None]).astype(jnp.float32)
        coeffs = (coeffs * triangle[:, :, None, None]).astype(jnp.bfloat16)
        with_real = jnp.einsum(
            "mupc,ucd->mupd", coeffs, mix_pairs[0, :, parity], preferred_element_type=jnp.float32
        )
        with_imag = jnp.einsum(
            "mupc,ucd->mupd", coeffs, mix_pairs[1, :, parity], preferred_element_type=jnp.float32
        )
        mixed = jnp.stack(
            [with_real[:, :, 0] - with_imag[:, :, 1], with_real[:, :, 1] + with_imag[:, :, 0]],
            axis=2,
        ).astype(jnp.bfloat16)
        returned = jnp.einsum(
            "mui,mupc->mpci", degree_plane, mixed, preferred_element_type=jnp.float32
        )
        even_sum = even_sum + jnp.where(same_parity, returned, 0.0)
        odd_sum = odd_sum + jnp.where(same_parity, 0.0, returned)
    north_out = (even_sum + odd_sum) * kept_mask[:, None, None, :]
    south_out = (even_sum - odd_sum) * kept_mask[:, None, None, :]
    grid_spectrum = jnp.concatenate([north_out, jnp.flip(south_out, axis=3)], axis=3).astype(
        jnp.bfloat16
    )

    by_group = jnp.transpose(
        grid_spectrum.reshape(m_dev, 2, channels, lat_count, lat_rows), (3, 0, 1, 2, 4)
    )
    outgoing = jnp.broadcast_to(
        by_group[:, None], (lat_count, lon_count, m_dev, 2, channels, lat_rows)
    ).reshape(n_dev, 16, m_dev * 2 * channels * lat_rows // 16)
    full_rows = lax.all_to_all(outgoing, BOTH, 0, 0, tiled=True)
    spectral_rows = full_rows.reshape(orders_all * 2, channels * lat_rows)
    inverse_rows = wave_table(
        lax.iota(jnp.int32, orders_all), lon_points, total_lon, True
    ).reshape(orders_all * 2, lon_cols)
    synthesis = lax.dot_general(
        spectral_rows, inverse_rows, (((0,), (0,)), ((), ())), preferred_element_type=jnp.float32
    ).reshape(channels, lat_rows, lon_cols)

    return (conv_out.astype(jnp.float32) + jax.nn.gelu(synthesis, approximate=True)).astype(
        jnp.bfloat16
    )


def depthwise_conv(offsets, conv_weight, rim, lat_rows, lon_cols):
    channels, rim_rows, rim_cols = rim.shape
    block_c = 8
    chunk = 4
    flat = rim_rows * rim_cols

    def body(offs_ref, rim_ref, w_ref, out_ref, planes, shifted, result):
        tiles = rim_cols // 128
        for c in range(block_c):
            x = rim_ref[c].astype(jnp.float32)
            for t in range(tiles):
                planes[t, pl.ds(c * rim_rows, rim_rows), :] = x[:, t * 128 : (t + 1) * 128]
        for row in range(rim_rows):
            v = jnp.concatenate(
                [planes[t, pl.ds(row, block_c, stride=rim_rows), :] for t in range(tiles)], axis=1
            )
            for s in range(5):
                turn = (2 - s) % rim_cols
                shifted[s, :, pl.ds(row * rim_cols, rim_cols)] = (
                    v if turn == 0 else pltpu.roll(v, turn, 1)
                )
        weights = w_ref[...]
        for r0 in range(0, lat_rows, chunk):
            acc = jnp.zeros((block_c, chunk * rim_cols), jnp.float32)
            for k in range(KTAPS):
                dr = offs_ref[k, 0]
                dc = offs_ref[k, 1]
                start = pl.multiple_of((r0 + 2 + dr) * rim_cols, rim_cols)
                acc = acc + weights[:, k : k + 1] * shifted[dc + 2, :, pl.ds(start, chunk * rim_cols)]
            for i in range(chunk):
                for t in range(tiles):
                    result[t, pl.ds(r0 + i, block_c, stride=lat_rows), :] = acc[
                        :, i * rim_cols + t * 128 : i * rim_cols + (t + 1) * 128
                    ]
        for c in range(block_c):
            full = jnp.concatenate(
                [result[t, pl.ds(c * lat_rows, lat_rows), :] for t in range(tiles)], axis=1
            )
            out_ref[c] = full[:, :lon_cols].astype(jnp.bfloat16)

    return pl.pallas_call(
        body,
        grid_spec=pltpu.PrefetchScalarGridSpec(
            num_scalar_prefetch=1,
            grid=(channels // block_c,),
            in_specs=[
                pl.BlockSpec((block_c, rim_rows, rim_cols), lambda b, o: (b, 0, 0)),
                pl.BlockSpec((block_c, KTAPS), lambda b, o: (b, 0)),
            ],
            out_specs=pl.BlockSpec((block_c, lat_rows, lon_cols), lambda b, o: (b, 0, 0)),
            scratch_shapes=[
                pltpu.VMEM((rim_cols // 128, block_c * rim_rows, 128), jnp.float32),
                pltpu.VMEM((5, block_c, flat), jnp.float32),
                pltpu.VMEM((rim_cols // 128, block_c * lat_rows, 128), jnp.float32),
            ],
        ),
        out_shape=jax.ShapeDtypeStruct((channels, lat_rows, lon_cols), jnp.bfloat16),
        compiler_params=pltpu.CompilerParams(vmem_limit_bytes=48 * 1024 * 1024),
        cost_estimate=pl.CostEstimate(
            flops=8 * KTAPS * channels * rim_rows * rim_cols,
            transcendentals=0,
            bytes_accessed=channels * (rim_rows * rim_cols + lat_rows * lon_cols) * 2,
        ),
    )(offsets, rim, conv_weight)


def solution(mesh):
    placed = (P(None, "lat", "lon"), P(), P(), P(BOTH, None, None), P(), P(), P())
    return jax.shard_map(
        per_device, mesh=mesh, in_specs=placed, out_specs=P(None, "lat", "lon"), check_vma=False
    )
```

```python
import math

import jax
import jax.numpy as jnp
from jax import lax
from jax.sharding import PartitionSpec as P
from jax.experimental import pallas as pl
from jax.experimental.pallas import tpu as pltpu

KTAPS = 9
BOTH = ("lat", "lon")


def wave_table(orders, points, period, inverse_form):
    angles = (orders[:, None] * points[None, :] % period).astype(jnp.float32) * (
        2.0 * math.pi / period
    )
    factor = jnp.full(orders.shape, 1.0 / math.sqrt(period), jnp.float32)
    if inverse_form:
        factor = jnp.where(orders == 0, 1.0, 2.0).astype(jnp.float32) * factor
    stacked = jnp.stack(
        [factor[:, None] * jnp.cos(angles), -factor[:, None] * jnp.sin(angles)], axis=1
    )
    return stacked.astype(jnp.bfloat16)


def per_device(field, offsets, conv_weight, legendre, quad_weight, band_limit, mix_weight):
    channels, lat_rows, lon_cols = field.shape
    m_dev = legendre.shape[0]
    lon_count = lax.axis_size("lon")
    lat_count = lax.axis_size("lat")
    n_dev = lon_count * lat_count
    total_lon = lon_cols * lon_count
    total_lat = lat_rows * lat_count
    half_rows = total_lat // 2
    orders_all = m_dev * n_dev
    lon_points = lax.axis_index("lon") * lon_cols + lax.iota(jnp.int32, lon_cols)
    me = lax.axis_index("lat") * lon_count + lax.axis_index("lon")
    mine = me * m_dev + lax.iota(jnp.int32, m_dev)

    forward_rows = wave_table(
        lax.iota(jnp.int32, orders_all), lon_points, total_lon, False
    ).reshape(orders_all * 2, lon_cols)
    flat_field = field.reshape(channels * lat_rows, lon_cols)
    partial = lax.dot_general(
        forward_rows, flat_field, (((1,), (1,)), ((), ())), preferred_element_type=jnp.float32
    ).reshape(n_dev, 16, m_dev * 2 * channels * lat_rows // 16)
    gathered_raw = lax.all_to_all(partial.astype(jnp.bfloat16), BOTH, 0, 0, tiled=True)
    rim_cols = ((lon_cols + 4 + 127) // 128) * 128
    lat_n = lax.axis_size("lat")
    south = lax.ppermute(
        field[:, :2], "lat", [((i + 1), i) for i in range(lat_n - 1)]
    )
    north = lax.ppermute(
        field[:, lat_rows - 2 :], "lat", [(i, (i + 1)) for i in range(lat_n - 1)]
    )
    rows_ext = jnp.concatenate(
        [north, field, south, jnp.zeros((channels, 4, lon_cols), field.dtype)], axis=1
    )
    rim_rows = rows_ext.shape[1]
    def lane_dense(edge):
        return jnp.transpose(edge, (2, 0, 1)).reshape(2, channels * rim_rows)

    def from_lanes(packed):
        return jnp.transpose(packed.reshape(2, channels, rim_rows), (1, 2, 0))

    east = from_lanes(
        lax.ppermute(
            lane_dense(rows_ext[:, :, :2]),
            "lon",
            [((i + 1) % lon_count, i) for i in range(lon_count)],
        )
    )
    west = from_lanes(
        lax.ppermute(
            lane_dense(rows_ext[:, :, lon_cols - 2 :]),
            "lon",
            [(i, (i + 1) % lon_count) for i in range(lon_count)],
        )
    )
    rim = jnp.concatenate(
        [
            rows_ext,
            east,
            jnp.zeros((channels, rim_rows, rim_cols - lon_cols - 4), field.dtype),
            west,
        ],
        axis=2,
    )
    conv_out = depthwise_conv(offsets, conv_weight, rim, lat_rows, lon_cols)
    gathered, conv_out = lax.optimization_barrier((gathered_raw, conv_out))
    summed = (
        gathered.astype(jnp.float32)
        .reshape(lat_count, lon_count, m_dev * 2 * channels * lat_rows)
        .sum(axis=1)
    )
    summed = summed.reshape(lat_count, m_dev, 2, channels, lat_rows)
    raw_spec = jnp.transpose(summed, (1, 2, 3, 0, 4)).reshape(m_dev, 2, channels, total_lat)

    rim = jnp.pad(raw_spec, ((0, 0), (0, 0), (0, 0), (2, 2)))
    turns = ((mine[None, :] * offsets[:, 1:2]) % total_lon).astype(jnp.float32) * (
        2.0 * math.pi / total_lon
    )
    cos_all = jnp.cos(turns)
    sin_all = jnp.sin(turns)
    real_acc = jnp.zeros((m_dev, channels, total_lat), jnp.float32)
    imag_acc = jnp.zeros((m_dev, channels, total_lat), jnp.float32)
    for shift in range(-2, 3):
        chosen = (offsets[:, 0] == shift).astype(jnp.float32)[:, None] * conv_weight.T
        coef_re = jnp.einsum("kc,ko->oc", chosen, cos_all)[:, :, None]
        coef_im = jnp.einsum("kc,ko->oc", chosen, sin_all)[:, :, None]
        window = rim[..., 2 + shift : 2 + shift + total_lat]
        real_acc = real_acc + coef_re * window[:, 0] - coef_im * window[:, 1]
        imag_acc = imag_acc + coef_im * window[:, 0] + coef_re * window[:, 1]
    spec_acc = jnp.stack([real_acc, imag_acc], axis=1)
    spectrum = spec_acc.astype(jnp.bfloat16)

    north_part = spectrum[..., :half_rows].astype(jnp.float32)
    south_part = jnp.flip(spectrum[..., half_rows:], axis=3).astype(jnp.float32)
    kept_mask = (mine[:, None] < band_limit[None, :]).astype(jnp.float32)
    weight_q = quad_weight[None, :] * kept_mask * (1.0 / math.sqrt(half_rows))
    even_terms = (weight_q[:, None, None, :] * (north_part + south_part)).astype(jnp.bfloat16)
    odd_terms = (weight_q[:, None, None, :] * (north_part - south_part)).astype(jnp.bfloat16)
    paired = legendre.reshape(m_dev, orders_all // 2, 2, half_rows)
    mix_pairs = mix_weight.reshape(2, orders_all // 2, 2, channels, channels)
    even_sum = jnp.zeros((m_dev, 2, channels, half_rows), jnp.float32)
    odd_sum = jnp.zeros((m_dev, 2, channels, half_rows), jnp.float32)
    for parity in range(2):
        same_parity = ((parity + mine) % 2 == 0)[:, None, None, None]
        operand = jnp.where(same_parity, even_terms, odd_terms)
        degree_plane = paired[:, :, parity]
        coeffs = jnp.einsum(
            "mui,mpci->mupc", degree_plane, operand, preferred_element_type=jnp.float32
        )
        degrees = 2 * lax.iota(jnp.int32, orders_all // 2) + parity
        triangle = (degrees[None, :] >= mine[:, None]).astype(jnp.float32)
        coeffs = (coeffs * triangle[:, :, None, None]).astype(jnp.bfloat16)
        with_real = jnp.einsum(
            "mupc,ucd->mupd", coeffs, mix_pairs[0, :, parity], preferred_element_type=jnp.float32
        )
        with_imag = jnp.einsum(
            "mupc,ucd->mupd", coeffs, mix_pairs[1, :, parity], preferred_element_type=jnp.float32
        )
        mixed = jnp.stack(
            [with_real[:, :, 0] - with_imag[:, :, 1], with_real[:, :, 1] + with_imag[:, :, 0]],
            axis=2,
        ).astype(jnp.bfloat16)
        returned = jnp.einsum(
            "mui,mupc->mpci", degree_plane, mixed, preferred_element_type=jnp.float32
        )
        even_sum = even_sum + jnp.where(same_parity, returned, 0.0)
        odd_sum = odd_sum + jnp.where(same_parity, 0.0, returned)
    north_out = (even_sum + odd_sum) * kept_mask[:, None, None, :]
    south_out = (even_sum - odd_sum) * kept_mask[:, None, None, :]
    grid_spectrum = jnp.concatenate([north_out, jnp.flip(south_out, axis=3)], axis=3).astype(
        jnp.bfloat16
    )

    by_group = jnp.transpose(
        grid_spectrum.reshape(m_dev, 2, channels, lat_count, lat_rows), (3, 0, 1, 2, 4)
    )
    outgoing = jnp.broadcast_to(
        by_group[:, None], (lat_count, lon_count, m_dev, 2, channels, lat_rows)
    ).reshape(n_dev, 16, m_dev * 2 * channels * lat_rows // 16)
    full_rows = lax.all_to_all(outgoing, BOTH, 0, 0, tiled=True)
    spectral_rows = full_rows.reshape(orders_all * 2, channels * lat_rows)
    inverse_rows = wave_table(
        lax.iota(jnp.int32, orders_all), lon_points, total_lon, True
    ).reshape(orders_all * 2, lon_cols)
    synthesis = lax.dot_general(
        spectral_rows, inverse_rows, (((0,), (0,)), ((), ())), preferred_element_type=jnp.float32
    ).reshape(channels, lat_rows, lon_cols)

    return (conv_out.astype(jnp.float32) + jax.nn.gelu(synthesis, approximate=True)).astype(
        jnp.bfloat16
    )


def depthwise_conv(offsets, conv_weight, rim, lat_rows, lon_cols):
    channels, rim_rows, rim_cols = rim.shape
    block_c = 8
    chunk = 4
    flat = rim_rows * rim_cols

    def body(offs_ref, rim_ref, w_ref, out_ref, planes, shifted, result):
        tiles = rim_cols // 128
        for c in range(block_c):
            x = rim_ref[c].astype(jnp.float32)
            for t in range(tiles):
                planes[t, pl.ds(c * rim_rows, rim_rows), :] = x[:, t * 128 : (t + 1) * 128]
        for row in range(rim_rows):
            v = jnp.concatenate(
                [planes[t, pl.ds(row, block_c, stride=rim_rows), :] for t in range(tiles)], axis=1
            )
            for s in range(5):
                turn = (2 - s) % rim_cols
                shifted[s, :, pl.ds(row * rim_cols, rim_cols)] = (
                    v if turn == 0 else pltpu.roll(v, turn, 1)
                )
        weights = w_ref[...]
        for r0 in range(0, lat_rows, chunk):
            acc = jnp.zeros((block_c, chunk * rim_cols), jnp.float32)
            for k in range(KTAPS):
                dr = offs_ref[k, 0]
                dc = offs_ref[k, 1]
                start = pl.multiple_of((r0 + 2 + dr) * rim_cols, rim_cols)
                acc = acc + weights[:, k : k + 1] * shifted[dc + 2, :, pl.ds(start, chunk * rim_cols)]
            for i in range(chunk):
                for t in range(tiles):
                    result[t, pl.ds(r0 + i, block_c, stride=lat_rows), :] = acc[
                        :, i * rim_cols + t * 128 : i * rim_cols + (t + 1) * 128
                    ]
        for c in range(block_c):
            full = jnp.concatenate(
                [result[t, pl.ds(c * lat_rows, lat_rows), :] for t in range(tiles)], axis=1
            )
            out_ref[c] = full[:, :lon_cols].astype(jnp.bfloat16)

    return pl.pallas_call(
        body,
        grid_spec=pltpu.PrefetchScalarGridSpec(
            num_scalar_prefetch=1,
            grid=(channels // block_c,),
            in_specs=[
                pl.BlockSpec((block_c, rim_rows, rim_cols), lambda b, o: (b, 0, 0)),
                pl.BlockSpec((block_c, KTAPS), lambda b, o: (b, 0)),
            ],
            out_specs=pl.BlockSpec((block_c, lat_rows, lon_cols), lambda b, o: (b, 0, 0)),
            scratch_shapes=[
                pltpu.VMEM((rim_cols // 128, block_c * rim_rows, 128), jnp.float32),
                pltpu.VMEM((5, block_c, flat), jnp.float32),
                pltpu.VMEM((rim_cols // 128, block_c * lat_rows, 128), jnp.float32),
            ],
        ),
        out_shape=jax.ShapeDtypeStruct((channels, lat_rows, lon_cols), jnp.bfloat16),
        compiler_params=pltpu.CompilerParams(vmem_limit_bytes=48 * 1024 * 1024),
        cost_estimate=pl.CostEstimate(
            flops=8 * KTAPS * channels * rim_rows * rim_cols,
            transcendentals=0,
            bytes_accessed=channels * (rim_rows * rim_cols + lat_rows * lon_cols) * 2,
        ),
    )(offsets, rim, conv_weight)


def solution(mesh):
    placed = (P(None, "lat", "lon"), P(), P(), P(BOTH, None, None), P(), P(), P())
    return jax.shard_map(
        per_device, mesh=mesh, in_specs=placed, out_specs=P(None, "lat", "lon"), check_vma=False
    )
```

```python
import math

import jax
import jax.numpy as jnp
from jax import lax
from jax.sharding import PartitionSpec as P
from jax.experimental import pallas as pl
from jax.experimental.pallas import tpu as pltpu

KTAPS = 9
BOTH = ("lat", "lon")


def wave_table(orders, points, period, inverse_form):
    angles = (orders[:, None] * points[None, :] % period).astype(jnp.float32) * (
        2.0 * math.pi / period
    )
    factor = jnp.full(orders.shape, 1.0 / math.sqrt(period), jnp.float32)
    if inverse_form:
        factor = jnp.where(orders == 0, 1.0, 2.0).astype(jnp.float32) * factor
    stacked = jnp.stack(
        [factor[:, None] * jnp.cos(angles), -factor[:, None] * jnp.sin(angles)], axis=1
    )
    return stacked.astype(jnp.bfloat16)


def per_device(field, offsets, conv_weight, legendre, quad_weight, band_limit, mix_weight):
    channels, lat_rows, lon_cols = field.shape
    m_dev = legendre.shape[0]
    lon_count = lax.axis_size("lon")
    lat_count = lax.axis_size("lat")
    n_dev = lon_count * lat_count
    total_lon = lon_cols * lon_count
    total_lat = lat_rows * lat_count
    half_rows = total_lat // 2
    orders_all = m_dev * n_dev
    lon_points = lax.axis_index("lon") * lon_cols + lax.iota(jnp.int32, lon_cols)
    me = lax.axis_index("lat") * lon_count + lax.axis_index("lon")
    mine = me * m_dev + lax.iota(jnp.int32, m_dev)

    forward_rows = wave_table(
        lax.iota(jnp.int32, orders_all), lon_points, total_lon, False
    ).reshape(orders_all * 2, lon_cols)
    flat_field = field.reshape(channels * lat_rows, lon_cols)
    partial = lax.dot_general(
        forward_rows, flat_field, (((1,), (1,)), ((), ())), preferred_element_type=jnp.float32
    ).reshape(n_dev, 16, m_dev * 2 * channels * lat_rows // 16)
    gathered_raw = lax.all_to_all(partial.astype(jnp.bfloat16), BOTH, 0, 0, tiled=True)
    rim_cols = ((lon_cols + 4 + 127) // 128) * 128
    lat_n = lax.axis_size("lat")
    south = lax.ppermute(
        field[:, :2], "lat", [((i + 1), i) for i in range(lat_n - 1)]
    )
    north = lax.ppermute(
        field[:, lat_rows - 2 :], "lat", [(i, (i + 1)) for i in range(lat_n - 1)]
    )
    rows_ext = jnp.concatenate(
        [north, field, south, jnp.zeros((channels, 4, lon_cols), field.dtype)], axis=1
    )
    rim_rows = rows_ext.shape[1]
    def lane_dense(edge):
        return jnp.transpose(edge, (2, 0, 1)).reshape(2, channels * rim_rows)

    def from_lanes(packed):
        return jnp.transpose(packed.reshape(2, channels, rim_rows), (1, 2, 0))

    east = from_lanes(
        lax.ppermute(
            lane_dense(rows_ext[:, :, :2]),
            "lon",
            [((i + 1) % lon_count, i) for i in range(lon_count)],
        )
    )
    west = from_lanes(
        lax.ppermute(
            lane_dense(rows_ext[:, :, lon_cols - 2 :]),
            "lon",
            [(i, (i + 1) % lon_count) for i in range(lon_count)],
        )
    )
    rim = jnp.concatenate(
        [
            rows_ext,
            east,
            jnp.zeros((channels, rim_rows, rim_cols - lon_cols - 4), field.dtype),
            west,
        ],
        axis=2,
    )
    conv_out = depthwise_conv(offsets, conv_weight, rim, lat_rows, lon_cols)
    gathered = gathered_raw
    summed = (
        gathered.astype(jnp.float32)
        .reshape(lat_count, lon_count, m_dev * 2 * channels * lat_rows)
        .sum(axis=1)
    )
    summed = summed.reshape(lat_count, m_dev, 2, channels, lat_rows)
    raw_spec = jnp.transpose(summed, (1, 2, 3, 0, 4)).reshape(m_dev, 2, channels, total_lat)

    rim = jnp.pad(raw_spec, ((0, 0), (0, 0), (0, 0), (2, 2)))
    turns = ((mine[None, :] * offsets[:, 1:2]) % total_lon).astype(jnp.float32) * (
        2.0 * math.pi / total_lon
    )
    cos_all = jnp.cos(turns)
    sin_all = jnp.sin(turns)
    real_acc = jnp.zeros((m_dev, channels, total_lat), jnp.float32)
    imag_acc = jnp.zeros((m_dev, channels, total_lat), jnp.float32)
    for shift in range(-2, 3):
        chosen = (offsets[:, 0] == shift).astype(jnp.float32)[:, None] * conv_weight.T
        coef_re = jnp.einsum("kc,ko->oc", chosen, cos_all)[:, :, None]
        coef_im = jnp.einsum("kc,ko->oc", chosen, sin_all)[:, :, None]
        window = rim[..., 2 + shift : 2 + shift + total_lat]
        real_acc = real_acc + coef_re * window[:, 0] - coef_im * window[:, 1]
        imag_acc = imag_acc + coef_im * window[:, 0] + coef_re * window[:, 1]
    spec_acc = jnp.stack([real_acc, imag_acc], axis=1)
    spectrum = spec_acc.astype(jnp.bfloat16)

    north_part = spectrum[..., :half_rows].astype(jnp.float32)
    south_part = jnp.flip(spectrum[..., half_rows:], axis=3).astype(jnp.float32)
    kept_mask = (mine[:, None] < band_limit[None, :]).astype(jnp.float32)
    weight_q = quad_weight[None, :] * kept_mask * (1.0 / math.sqrt(half_rows))
    even_terms = (weight_q[:, None, None, :] * (north_part + south_part)).astype(jnp.bfloat16)
    odd_terms = (weight_q[:, None, None, :] * (north_part - south_part)).astype(jnp.bfloat16)
    paired = legendre.reshape(m_dev, orders_all // 2, 2, half_rows)
    mix_pairs = mix_weight.reshape(2, orders_all // 2, 2, channels, channels)
    even_sum = jnp.zeros((m_dev, 2, channels, half_rows), jnp.float32)
    odd_sum = jnp.zeros((m_dev, 2, channels, half_rows), jnp.float32)
    for parity in range(2):
        same_parity = ((parity + mine) % 2 == 0)[:, None, None, None]
        operand = jnp.where(same_parity, even_terms, odd_terms)
        degree_plane = paired[:, :, parity]
        coeffs = jnp.einsum(
            "mui,mpci->mupc", degree_plane, operand, preferred_element_type=jnp.float32
        )
        degrees = 2 * lax.iota(jnp.int32, orders_all // 2) + parity
        triangle = (degrees[None, :] >= mine[:, None]).astype(jnp.float32)
        coeffs = (coeffs * triangle[:, :, None, None]).astype(jnp.bfloat16)
        with_real = jnp.einsum(
            "mupc,ucd->mupd", coeffs, mix_pairs[0, :, parity], preferred_element_type=jnp.float32
        )
        with_imag = jnp.einsum(
            "mupc,ucd->mupd", coeffs, mix_pairs[1, :, parity], preferred_element_type=jnp.float32
        )
        mixed = jnp.stack(
            [with_real[:, :, 0] - with_imag[:, :, 1], with_real[:, :, 1] + with_imag[:, :, 0]],
            axis=2,
        ).astype(jnp.bfloat16)
        returned = jnp.einsum(
            "mui,mupc->mpci", degree_plane, mixed, preferred_element_type=jnp.float32
        )
        even_sum = even_sum + jnp.where(same_parity, returned, 0.0)
        odd_sum = odd_sum + jnp.where(same_parity, 0.0, returned)
    north_out = (even_sum + odd_sum) * kept_mask[:, None, None, :]
    south_out = (even_sum - odd_sum) * kept_mask[:, None, None, :]
    grid_spectrum = jnp.concatenate([north_out, jnp.flip(south_out, axis=3)], axis=3).astype(
        jnp.bfloat16
    )

    by_group = jnp.transpose(
        grid_spectrum.reshape(m_dev, 2, channels, lat_count, lat_rows), (3, 0, 1, 2, 4)
    )
    outgoing = jnp.broadcast_to(
        by_group[:, None], (lat_count, lon_count, m_dev, 2, channels, lat_rows)
    ).reshape(n_dev, 16, m_dev * 2 * channels * lat_rows // 16)
    full_rows = lax.all_to_all(outgoing, BOTH, 0, 0, tiled=True)
    full_rows, conv_out = lax.optimization_barrier((full_rows, conv_out))
    spectral_rows = full_rows.reshape(orders_all * 2, channels * lat_rows)
    inverse_rows = wave_table(
        lax.iota(jnp.int32, orders_all), lon_points, total_lon, True
    ).reshape(orders_all * 2, lon_cols)
    synthesis = lax.dot_general(
        spectral_rows, inverse_rows, (((0,), (0,)), ((), ())), preferred_element_type=jnp.float32
    ).reshape(channels, lat_rows, lon_cols)

    return (conv_out.astype(jnp.float32) + jax.nn.gelu(synthesis, approximate=True)).astype(
        jnp.bfloat16
    )


def depthwise_conv(offsets, conv_weight, rim, lat_rows, lon_cols):
    channels, rim_rows, rim_cols = rim.shape
    block_c = 8
    chunk = 4
    flat = rim_rows * rim_cols

    def body(offs_ref, rim_ref, w_ref, out_ref, planes, shifted, result):
        tiles = rim_cols // 128
        for c in range(block_c):
            x = rim_ref[c].astype(jnp.float32)
            for t in range(tiles):
                planes[t, pl.ds(c * rim_rows, rim_rows), :] = x[:, t * 128 : (t + 1) * 128]
        for row in range(rim_rows):
            v = jnp.concatenate(
                [planes[t, pl.ds(row, block_c, stride=rim_rows), :] for t in range(tiles)], axis=1
            )
            for s in range(5):
                turn = (2 - s) % rim_cols
                shifted[s, :, pl.ds(row * rim_cols, rim_cols)] = (
                    v if turn == 0 else pltpu.roll(v, turn, 1)
                )
        weights = w_ref[...]
        for r0 in range(0, lat_rows, chunk):
            acc = jnp.zeros((block_c, chunk * rim_cols), jnp.float32)
            for k in range(KTAPS):
                dr = offs_ref[k, 0]
                dc = offs_ref[k, 1]
                start = pl.multiple_of((r0 + 2 + dr) * rim_cols, rim_cols)
                acc = acc + weights[:, k : k + 1] * shifted[dc + 2, :, pl.ds(start, chunk * rim_cols)]
            for i in range(chunk):
                for t in range(tiles):
                    result[t, pl.ds(r0 + i, block_c, stride=lat_rows), :] = acc[
                        :, i * rim_cols + t * 128 : i * rim_cols + (t + 1) * 128
                    ]
        for c in range(block_c):
            full = jnp.concatenate(
                [result[t, pl.ds(c * lat_rows, lat_rows), :] for t in range(tiles)], axis=1
            )
            out_ref[c] = full[:, :lon_cols].astype(jnp.bfloat16)

    return pl.pallas_call(
        body,
        grid_spec=pltpu.PrefetchScalarGridSpec(
            num_scalar_prefetch=1,
            grid=(channels // block_c,),
            in_specs=[
                pl.BlockSpec((block_c, rim_rows, rim_cols), lambda b, o: (b, 0, 0)),
                pl.BlockSpec((block_c, KTAPS), lambda b, o: (b, 0)),
            ],
            out_specs=pl.BlockSpec((block_c, lat_rows, lon_cols), lambda b, o: (b, 0, 0)),
            scratch_shapes=[
                pltpu.VMEM((rim_cols // 128, block_c * rim_rows, 128), jnp.float32),
                pltpu.VMEM((5, block_c, flat), jnp.float32),
                pltpu.VMEM((rim_cols // 128, block_c * lat_rows, 128), jnp.float32),
            ],
        ),
        out_shape=jax.ShapeDtypeStruct((channels, lat_rows, lon_cols), jnp.bfloat16),
        compiler_params=pltpu.CompilerParams(vmem_limit_bytes=48 * 1024 * 1024),
        cost_estimate=pl.CostEstimate(
            flops=8 * KTAPS * channels * rim_rows * rim_cols,
            transcendentals=0,
            bytes_accessed=channels * (rim_rows * rim_cols + lat_rows * lon_cols) * 2,
        ),
    )(offsets, rim, conv_weight)


def solution(mesh):
    placed = (P(None, "lat", "lon"), P(), P(), P(BOTH, None, None), P(), P(), P())
    return jax.shard_map(
        per_device, mesh=mesh, in_specs=placed, out_specs=P(None, "lat", "lon"), check_vma=False
    )
```

```python
import math

import jax
import jax.numpy as jnp
from jax import lax
from jax.sharding import PartitionSpec as P
from jax.experimental import pallas as pl
from jax.experimental.pallas import tpu as pltpu

KTAPS = 9
BOTH = ("lat", "lon")


def wave_table(orders, points, period, inverse_form):
    angles = (orders[:, None] * points[None, :] % period).astype(jnp.float32) * (
        2.0 * math.pi / period
    )
    factor = jnp.full(orders.shape, 1.0 / math.sqrt(period), jnp.float32)
    if inverse_form:
        factor = jnp.where(orders == 0, 1.0, 2.0).astype(jnp.float32) * factor
    stacked = jnp.stack(
        [factor[:, None] * jnp.cos(angles), -factor[:, None] * jnp.sin(angles)], axis=1
    )
    return stacked.astype(jnp.bfloat16)


def per_device(field, offsets, conv_weight, legendre, quad_weight, band_limit, mix_weight):
    channels, lat_rows, lon_cols = field.shape
    m_dev = legendre.shape[0]
    lon_count = lax.axis_size("lon")
    lat_count = lax.axis_size("lat")
    n_dev = lon_count * lat_count
    total_lon = lon_cols * lon_count
    total_lat = lat_rows * lat_count
    half_rows = total_lat // 2
    orders_all = m_dev * n_dev
    lon_points = lax.axis_index("lon") * lon_cols + lax.iota(jnp.int32, lon_cols)
    me = lax.axis_index("lat") * lon_count + lax.axis_index("lon")
    mine = me * m_dev + lax.iota(jnp.int32, m_dev)

    forward_rows = wave_table(
        lax.iota(jnp.int32, orders_all), lon_points, total_lon, False
    ).reshape(orders_all * 2, lon_cols)
    flat_field = field.reshape(channels * lat_rows, lon_cols)
    partial = lax.dot_general(
        forward_rows, flat_field, (((1,), (1,)), ((), ())), preferred_element_type=jnp.float32
    ).reshape(n_dev, 16, m_dev * 2 * channels * lat_rows // 16)
    gathered_raw = lax.all_to_all(partial.astype(jnp.bfloat16), BOTH, 0, 0, tiled=True)
    rim_cols = ((lon_cols + 4 + 127) // 128) * 128
    lat_n = lax.axis_size("lat")
    south = lax.ppermute(
        field[:, :2], "lat", [((i + 1), i) for i in range(lat_n - 1)]
    )
    north = lax.ppermute(
        field[:, lat_rows - 2 :], "lat", [(i, (i + 1)) for i in range(lat_n - 1)]
    )
    rows_ext = jnp.concatenate(
        [north, field, south, jnp.zeros((channels, 4, lon_cols), field.dtype)], axis=1
    )
    rim_rows = rows_ext.shape[1]
    def lane_dense(edge):
        return jnp.transpose(edge, (2, 0, 1)).reshape(2, channels * rim_rows)

    def from_lanes(packed):
        return jnp.transpose(packed.reshape(2, channels, rim_rows), (1, 2, 0))

    east = from_lanes(
        lax.ppermute(
            lane_dense(rows_ext[:, :, :2]),
            "lon",
            [((i + 1) % lon_count, i) for i in range(lon_count)],
        )
    )
    west = from_lanes(
        lax.ppermute(
            lane_dense(rows_ext[:, :, lon_cols - 2 :]),
            "lon",
            [(i, (i + 1) % lon_count) for i in range(lon_count)],
        )
    )
    rim = jnp.concatenate(
        [
            rows_ext,
            east,
            jnp.zeros((channels, rim_rows, rim_cols - lon_cols - 4), field.dtype),
            west,
        ],
        axis=2,
    )
    conv_out = depthwise_conv(offsets, conv_weight, rim, lat_rows, lon_cols)
    gathered = gathered_raw
    summed = (
        gathered.astype(jnp.float32)
        .reshape(lat_count, lon_count, m_dev * 2 * channels * lat_rows)
        .sum(axis=1)
    )
    summed = summed.reshape(lat_count, m_dev, 2, channels, lat_rows)
    raw_spec = jnp.transpose(summed, (1, 2, 3, 0, 4)).reshape(m_dev, 2, channels, total_lat)

    rim = jnp.pad(raw_spec, ((0, 0), (0, 0), (0, 0), (2, 2)))
    turns = ((mine[None, :] * offsets[:, 1:2]) % total_lon).astype(jnp.float32) * (
        2.0 * math.pi / total_lon
    )
    cos_all = jnp.cos(turns)
    sin_all = jnp.sin(turns)
    shifts = lax.iota(jnp.int32, 5) - 2
    chosen = (offsets[None, :, 0] == shifts[:, None]).astype(jnp.float32)
    coef_re = jnp.einsum("dk,ck,ko->doc", chosen, conv_weight, cos_all)[..., None]
    coef_im = jnp.einsum("dk,ck,ko->doc", chosen, conv_weight, sin_all)[..., None]
    real_acc = jnp.zeros((m_dev, channels, total_lat), jnp.float32)
    imag_acc = jnp.zeros((m_dev, channels, total_lat), jnp.float32)
    for shift in range(-2, 3):
        window = rim[..., 2 + shift : 2 + shift + total_lat]
        c_re = coef_re[shift + 2]
        c_im = coef_im[shift + 2]
        real_acc = real_acc + c_re * window[:, 0] - c_im * window[:, 1]
        imag_acc = imag_acc + c_im * window[:, 0] + c_re * window[:, 1]
    spec_acc = jnp.stack([real_acc, imag_acc], axis=1)
    spectrum = spec_acc.astype(jnp.bfloat16)

    north_part = spectrum[..., :half_rows].astype(jnp.float32)
    south_part = jnp.flip(spectrum[..., half_rows:], axis=3).astype(jnp.float32)
    kept_mask = (mine[:, None] < band_limit[None, :]).astype(jnp.float32)
    weight_q = quad_weight[None, :] * kept_mask * (1.0 / math.sqrt(half_rows))
    even_terms = (weight_q[:, None, None, :] * (north_part + south_part)).astype(jnp.bfloat16)
    odd_terms = (weight_q[:, None, None, :] * (north_part - south_part)).astype(jnp.bfloat16)
    paired = legendre.reshape(m_dev, orders_all // 2, 2, half_rows)
    mix_pairs = mix_weight.reshape(2, orders_all // 2, 2, channels, channels)
    even_sum = jnp.zeros((m_dev, 2, channels, half_rows), jnp.float32)
    odd_sum = jnp.zeros((m_dev, 2, channels, half_rows), jnp.float32)
    for parity in range(2):
        same_parity = ((parity + mine) % 2 == 0)[:, None, None, None]
        operand = jnp.where(same_parity, even_terms, odd_terms)
        degree_plane = paired[:, :, parity]
        coeffs = jnp.einsum(
            "mui,mpci->mupc", degree_plane, operand, preferred_element_type=jnp.float32
        )
        degrees = 2 * lax.iota(jnp.int32, orders_all // 2) + parity
        triangle = (degrees[None, :] >= mine[:, None]).astype(jnp.float32)
        coeffs = (coeffs * triangle[:, :, None, None]).astype(jnp.bfloat16)
        with_real = jnp.einsum(
            "mupc,ucd->mupd", coeffs, mix_pairs[0, :, parity], preferred_element_type=jnp.float32
        )
        with_imag = jnp.einsum(
            "mupc,ucd->mupd", coeffs, mix_pairs[1, :, parity], preferred_element_type=jnp.float32
        )
        mixed = jnp.stack(
            [with_real[:, :, 0] - with_imag[:, :, 1], with_real[:, :, 1] + with_imag[:, :, 0]],
            axis=2,
        ).astype(jnp.bfloat16)
        returned = jnp.einsum(
            "mui,mupc->mpci", degree_plane, mixed, preferred_element_type=jnp.float32
        )
        even_sum = even_sum + jnp.where(same_parity, returned, 0.0)
        odd_sum = odd_sum + jnp.where(same_parity, 0.0, returned)
    north_out = (even_sum + odd_sum) * kept_mask[:, None, None, :]
    south_out = (even_sum - odd_sum) * kept_mask[:, None, None, :]
    grid_spectrum = jnp.concatenate([north_out, jnp.flip(south_out, axis=3)], axis=3).astype(
        jnp.bfloat16
    )

    by_group = jnp.transpose(
        grid_spectrum.reshape(m_dev, 2, channels, lat_count, lat_rows), (3, 0, 1, 2, 4)
    )
    outgoing = jnp.broadcast_to(
        by_group[:, None], (lat_count, lon_count, m_dev, 2, channels, lat_rows)
    ).reshape(n_dev, 16, m_dev * 2 * channels * lat_rows // 16)
    full_rows = lax.all_to_all(outgoing, BOTH, 0, 0, tiled=True)
    full_rows, conv_out = lax.optimization_barrier((full_rows, conv_out))
    spectral_rows = full_rows.reshape(orders_all * 2, channels * lat_rows)
    inverse_rows = wave_table(
        lax.iota(jnp.int32, orders_all), lon_points, total_lon, True
    ).reshape(orders_all * 2, lon_cols)
    synthesis = lax.dot_general(
        spectral_rows, inverse_rows, (((0,), (0,)), ((), ())), preferred_element_type=jnp.float32
    ).reshape(channels, lat_rows, lon_cols)

    return (conv_out.astype(jnp.float32) + jax.nn.gelu(synthesis, approximate=True)).astype(
        jnp.bfloat16
    )


def depthwise_conv(offsets, conv_weight, rim, lat_rows, lon_cols):
    channels, rim_rows, rim_cols = rim.shape
    by_rows = jnp.transpose(rim, (1, 0, 2))
    block_c = 16
    chunk = 2

    def body(offs_ref, rim_ref, w_ref, out_ref, shifted):
        for row in range(rim_rows):
            v = rim_ref[row].astype(jnp.float32)
            for s in range(5):
                turn = (2 - s) % rim_cols
                shifted[s, :, pl.ds(row * rim_cols, rim_cols)] = (
                    v if turn == 0 else pltpu.roll(v, turn, 1)
                )
        weights = w_ref[...]
        for r0 in range(0, lat_rows, chunk):
            acc = jnp.zeros((block_c, chunk * rim_cols), jnp.float32)
            for k in range(KTAPS):
                dr = offs_ref[k, 0]
                dc = offs_ref[k, 1]
                start = pl.multiple_of((r0 + 2 + dr) * rim_cols, rim_cols)
                acc = acc + weights[:, k : k + 1] * shifted[dc + 2, :, pl.ds(start, chunk * rim_cols)]
            for i in range(chunk):
                out_ref[r0 + i] = acc[:, i * rim_cols : i * rim_cols + lon_cols].astype(jnp.bfloat16)

    by_rows_out = pl.pallas_call(
        body,
        grid_spec=pltpu.PrefetchScalarGridSpec(
            num_scalar_prefetch=1,
            grid=(channels // block_c,),
            in_specs=[
                pl.BlockSpec((rim_rows, block_c, rim_cols), lambda b, o: (0, b, 0)),
                pl.BlockSpec((block_c, KTAPS), lambda b, o: (b, 0)),
            ],
            out_specs=pl.BlockSpec((lat_rows, block_c, lon_cols), lambda b, o: (0, b, 0)),
            scratch_shapes=[pltpu.VMEM((5, block_c, rim_rows * rim_cols), jnp.float32)],
        ),
        out_shape=jax.ShapeDtypeStruct((lat_rows, channels, lon_cols), jnp.bfloat16),
        compiler_params=pltpu.CompilerParams(vmem_limit_bytes=48 * 1024 * 1024),
        cost_estimate=pl.CostEstimate(
            flops=8 * KTAPS * channels * rim_rows * rim_cols,
            transcendentals=0,
            bytes_accessed=channels * (rim_rows * rim_cols + lat_rows * lon_cols) * 2,
        ),
    )(offsets, by_rows, conv_weight)
    return jnp.transpose(by_rows_out, (1, 0, 2))


def solution(mesh):
    placed = (P(None, "lat", "lon"), P(), P(), P(BOTH, None, None), P(), P(), P())
    return jax.shard_map(
        per_device, mesh=mesh, in_specs=placed, out_specs=P(None, "lat", "lon"), check_vma=False
    )
```

```python
import math

import jax
import jax.numpy as jnp
from jax import lax
from jax.sharding import PartitionSpec as P
from jax.experimental import pallas as pl
from jax.experimental.pallas import tpu as pltpu

KTAPS = 9
BOTH = ("lat", "lon")


def wave_table(orders, points, period, inverse_form):
    angles = (orders[:, None] * points[None, :] % period).astype(jnp.float32) * (
        2.0 * math.pi / period
    )
    factor = jnp.full(orders.shape, 1.0 / math.sqrt(period), jnp.float32)
    if inverse_form:
        factor = jnp.where(orders == 0, 1.0, 2.0).astype(jnp.float32) * factor
    stacked = jnp.stack(
        [factor[:, None] * jnp.cos(angles), -factor[:, None] * jnp.sin(angles)], axis=1
    )
    return stacked.astype(jnp.bfloat16)


def per_device(field, offsets, conv_weight, legendre, quad_weight, band_limit, mix_weight):
    channels, lat_rows, lon_cols = field.shape
    m_dev = legendre.shape[0]
    lon_count = lax.axis_size("lon")
    lat_count = lax.axis_size("lat")
    n_dev = lon_count * lat_count
    total_lon = lon_cols * lon_count
    total_lat = lat_rows * lat_count
    half_rows = total_lat // 2
    orders_all = m_dev * n_dev
    lon_points = lax.axis_index("lon") * lon_cols + lax.iota(jnp.int32, lon_cols)
    me = lax.axis_index("lat") * lon_count + lax.axis_index("lon")
    mine = me * m_dev + lax.iota(jnp.int32, m_dev)

    forward_rows = wave_table(
        lax.iota(jnp.int32, orders_all), lon_points, total_lon, False
    ).reshape(orders_all * 2, lon_cols)
    flat_field = field.reshape(channels * lat_rows, lon_cols)
    partial = lax.dot_general(
        forward_rows, flat_field, (((1,), (1,)), ((), ())), preferred_element_type=jnp.float32
    ).reshape(n_dev, 16, m_dev * 2 * channels * lat_rows // 16)
    gathered_raw = lax.all_to_all(partial.astype(jnp.bfloat16), BOTH, 0, 0, tiled=True)
    rim_cols = ((lon_cols + 4 + 127) // 128) * 128
    lat_n = lax.axis_size("lat")
    south = lax.ppermute(
        field[:, :2], "lat", [((i + 1), i) for i in range(lat_n - 1)]
    )
    north = lax.ppermute(
        field[:, lat_rows - 2 :], "lat", [(i, (i + 1)) for i in range(lat_n - 1)]
    )
    rows_ext = jnp.concatenate(
        [north, field, south, jnp.zeros((channels, 4, lon_cols), field.dtype)], axis=1
    )
    rim_rows = rows_ext.shape[1]
    def lane_dense(edge):
        return jnp.transpose(edge, (2, 0, 1)).reshape(2, channels * rim_rows)

    def from_lanes(packed):
        return jnp.transpose(packed.reshape(2, channels, rim_rows), (1, 2, 0))

    east = from_lanes(
        lax.ppermute(
            lane_dense(rows_ext[:, :, :2]),
            "lon",
            [((i + 1) % lon_count, i) for i in range(lon_count)],
        )
    )
    west = from_lanes(
        lax.ppermute(
            lane_dense(rows_ext[:, :, lon_cols - 2 :]),
            "lon",
            [(i, (i + 1) % lon_count) for i in range(lon_count)],
        )
    )
    rim = jnp.concatenate(
        [
            rows_ext,
            east,
            jnp.zeros((channels, rim_rows, rim_cols - lon_cols - 4), field.dtype),
            west,
        ],
        axis=2,
    )
    conv_out = depthwise_conv(offsets, conv_weight, rim, lat_rows, lon_cols)
    gathered = gathered_raw
    summed = (
        gathered.astype(jnp.float32)
        .reshape(lat_count, lon_count, m_dev * 2 * channels * lat_rows)
        .sum(axis=1)
    )
    summed = summed.reshape(lat_count, m_dev, 2, channels, lat_rows)
    raw_spec = jnp.transpose(summed, (1, 2, 3, 0, 4)).reshape(m_dev, 2, channels, total_lat)

    rim = jnp.pad(raw_spec, ((0, 0), (0, 0), (0, 0), (2, 2)))
    turns = ((mine[None, :] * offsets[:, 1:2]) % total_lon).astype(jnp.float32) * (
        2.0 * math.pi / total_lon
    )
    cos_all = jnp.cos(turns)
    sin_all = jnp.sin(turns)
    shifts = lax.iota(jnp.int32, 5) - 2
    chosen = (offsets[None, :, 0] == shifts[:, None]).astype(jnp.float32)
    coef_re = jnp.einsum("dk,ck,ko->doc", chosen, conv_weight, cos_all)[..., None]
    coef_im = jnp.einsum("dk,ck,ko->doc", chosen, conv_weight, sin_all)[..., None]
    real_acc = jnp.zeros((m_dev, channels, total_lat), jnp.float32)
    imag_acc = jnp.zeros((m_dev, channels, total_lat), jnp.float32)
    for shift in range(-2, 3):
        window = rim[..., 2 + shift : 2 + shift + total_lat]
        c_re = coef_re[shift + 2]
        c_im = coef_im[shift + 2]
        real_acc = real_acc + c_re * window[:, 0] - c_im * window[:, 1]
        imag_acc = imag_acc + c_im * window[:, 0] + c_re * window[:, 1]
    spec_acc = jnp.stack([real_acc, imag_acc], axis=1)
    spectrum = spec_acc.astype(jnp.bfloat16)

    north_part = spectrum[..., :half_rows].astype(jnp.float32)
    south_part = jnp.flip(spectrum[..., half_rows:], axis=3).astype(jnp.float32)
    kept_mask = (mine[:, None] < band_limit[None, :]).astype(jnp.float32)
    weight_q = quad_weight[None, :] * kept_mask * (1.0 / math.sqrt(half_rows))
    even_terms = (weight_q[:, None, None, :] * (north_part + south_part)).astype(jnp.bfloat16)
    odd_terms = (weight_q[:, None, None, :] * (north_part - south_part)).astype(jnp.bfloat16)
    degrees = lax.iota(jnp.int32, orders_all)
    same = ((degrees[None, :] + mine[:, None]) % 2 == 0)[:, :, None]
    zero = jnp.zeros((), legendre.dtype)
    leg_same = jnp.where(same, legendre, zero)
    leg_diff = jnp.where(same, zero, legendre)
    coeffs = jnp.einsum(
        "mli,mpci->mlpc", leg_same, even_terms, preferred_element_type=jnp.float32
    ) + jnp.einsum("mli,mpci->mlpc", leg_diff, odd_terms, preferred_element_type=jnp.float32)
    triangle = (degrees[None, :] >= mine[:, None]).astype(jnp.float32)
    coeffs = (coeffs * triangle[:, :, None, None]).astype(jnp.bfloat16)
    with_real = jnp.einsum(
        "mlpc,lcd->mlpd", coeffs, mix_weight[0], preferred_element_type=jnp.float32
    )
    with_imag = jnp.einsum(
        "mlpc,lcd->mlpd", coeffs, mix_weight[1], preferred_element_type=jnp.float32
    )
    mixed = jnp.stack(
        [with_real[:, :, 0] - with_imag[:, :, 1], with_real[:, :, 1] + with_imag[:, :, 0]],
        axis=2,
    ).astype(jnp.bfloat16)
    even_sum = jnp.einsum("mli,mlpc->mpci", leg_same, mixed, preferred_element_type=jnp.float32)
    odd_sum = jnp.einsum("mli,mlpc->mpci", leg_diff, mixed, preferred_element_type=jnp.float32)
    north_out = (even_sum + odd_sum) * kept_mask[:, None, None, :]
    south_out = (even_sum - odd_sum) * kept_mask[:, None, None, :]
    grid_spectrum = jnp.concatenate([north_out, jnp.flip(south_out, axis=3)], axis=3).astype(
        jnp.bfloat16
    )

    by_group = jnp.transpose(
        grid_spectrum.reshape(m_dev, 2, channels, lat_count, lat_rows), (3, 0, 1, 2, 4)
    )
    outgoing = jnp.broadcast_to(
        by_group[:, None], (lat_count, lon_count, m_dev, 2, channels, lat_rows)
    ).reshape(n_dev, 16, m_dev * 2 * channels * lat_rows // 16)
    full_rows = lax.all_to_all(outgoing, BOTH, 0, 0, tiled=True)
    full_rows, conv_out = lax.optimization_barrier((full_rows, conv_out))
    spectral_rows = full_rows.reshape(orders_all * 2, channels * lat_rows)
    inverse_rows = wave_table(
        lax.iota(jnp.int32, orders_all), lon_points, total_lon, True
    ).reshape(orders_all * 2, lon_cols)
    synthesis = lax.dot_general(
        spectral_rows, inverse_rows, (((0,), (0,)), ((), ())), preferred_element_type=jnp.float32
    ).reshape(channels, lat_rows, lon_cols)

    return (conv_out.astype(jnp.float32) + jax.nn.gelu(synthesis, approximate=True)).astype(
        jnp.bfloat16
    )


def depthwise_conv(offsets, conv_weight, rim, lat_rows, lon_cols):
    channels, rim_rows, rim_cols = rim.shape
    by_rows = jnp.transpose(rim, (1, 0, 2))
    block_c = 16
    chunk = 2

    def body(offs_ref, rim_ref, w_ref, out_ref, shifted):
        for row in range(rim_rows):
            v = rim_ref[row].astype(jnp.float32)
            for s in range(5):
                turn = (2 - s) % rim_cols
                shifted[s, :, pl.ds(row * rim_cols, rim_cols)] = (
                    v if turn == 0 else pltpu.roll(v, turn, 1)
                )
        weights = w_ref[...]
        for r0 in range(0, lat_rows, chunk):
            acc = jnp.zeros((block_c, chunk * rim_cols), jnp.float32)
            for k in range(KTAPS):
                dr = offs_ref[k, 0]
                dc = offs_ref[k, 1]
                start = pl.multiple_of((r0 + 2 + dr) * rim_cols, rim_cols)
                acc = acc + weights[:, k : k + 1] * shifted[dc + 2, :, pl.ds(start, chunk * rim_cols)]
            for i in range(chunk):
                out_ref[r0 + i] = acc[:, i * rim_cols : i * rim_cols + lon_cols].astype(jnp.bfloat16)

    by_rows_out = pl.pallas_call(
        body,
        grid_spec=pltpu.PrefetchScalarGridSpec(
            num_scalar_prefetch=1,
            grid=(channels // block_c,),
            in_specs=[
                pl.BlockSpec((rim_rows, block_c, rim_cols), lambda b, o: (0, b, 0)),
                pl.BlockSpec((block_c, KTAPS), lambda b, o: (b, 0)),
            ],
            out_specs=pl.BlockSpec((lat_rows, block_c, lon_cols), lambda b, o: (0, b, 0)),
            scratch_shapes=[pltpu.VMEM((5, block_c, rim_rows * rim_cols), jnp.float32)],
        ),
        out_shape=jax.ShapeDtypeStruct((lat_rows, channels, lon_cols), jnp.bfloat16),
        compiler_params=pltpu.CompilerParams(vmem_limit_bytes=48 * 1024 * 1024),
        cost_estimate=pl.CostEstimate(
            flops=8 * KTAPS * channels * rim_rows * rim_cols,
            transcendentals=0,
            bytes_accessed=channels * (rim_rows * rim_cols + lat_rows * lon_cols) * 2,
        ),
    )(offsets, by_rows, conv_weight)
    return jnp.transpose(by_rows_out, (1, 0, 2))


def solution(mesh):
    placed = (P(None, "lat", "lon"), P(), P(), P(BOTH, None, None), P(), P(), P())
    return jax.shard_map(
        per_device, mesh=mesh, in_specs=placed, out_specs=P(None, "lat", "lon"), check_vma=False
    )
```

```python
import math

import jax
import jax.numpy as jnp
from jax import lax
from jax.sharding import PartitionSpec as P
from jax.experimental import pallas as pl
from jax.experimental.pallas import tpu as pltpu

KTAPS = 9
BOTH = ("lat", "lon")


def wave_table(orders, points, period, inverse_form):
    angles = (orders[:, None] * points[None, :] % period).astype(jnp.float32) * (
        2.0 * math.pi / period
    )
    factor = jnp.full(orders.shape, 1.0 / math.sqrt(period), jnp.float32)
    if inverse_form:
        factor = jnp.where(orders == 0, 1.0, 2.0).astype(jnp.float32) * factor
    stacked = jnp.stack(
        [factor[:, None] * jnp.cos(angles), -factor[:, None] * jnp.sin(angles)], axis=1
    )
    return stacked.astype(jnp.bfloat16)


def per_device(field, offsets, conv_weight, legendre, quad_weight, band_limit, mix_weight):
    channels, lat_rows, lon_cols = field.shape
    m_dev = legendre.shape[0]
    lon_count = lax.axis_size("lon")
    lat_count = lax.axis_size("lat")
    n_dev = lon_count * lat_count
    total_lon = lon_cols * lon_count
    total_lat = lat_rows * lat_count
    half_rows = total_lat // 2
    orders_all = m_dev * n_dev
    lon_points = lax.axis_index("lon") * lon_cols + lax.iota(jnp.int32, lon_cols)
    me = lax.axis_index("lat") * lon_count + lax.axis_index("lon")
    mine = me * m_dev + lax.iota(jnp.int32, m_dev)

    forward_rows = wave_table(
        lax.iota(jnp.int32, orders_all), lon_points, total_lon, False
    ).reshape(orders_all * 2, lon_cols)
    flat_field = field.reshape(channels * lat_rows, lon_cols)
    partial = lax.dot_general(
        forward_rows, flat_field, (((1,), (1,)), ((), ())), preferred_element_type=jnp.float32
    ).reshape(n_dev, 16, m_dev * 2 * channels * lat_rows // 16)
    gathered_raw = lax.all_to_all(partial.astype(jnp.bfloat16), BOTH, 0, 0, tiled=True)
    rim_cols = ((lon_cols + 4 + 127) // 128) * 128
    lat_n = lax.axis_size("lat")
    south = lax.ppermute(
        field[:, :2], "lat", [((i + 1), i) for i in range(lat_n - 1)]
    )
    north = lax.ppermute(
        field[:, lat_rows - 2 :], "lat", [(i, (i + 1)) for i in range(lat_n - 1)]
    )
    rows_ext = jnp.concatenate(
        [north, field, south, jnp.zeros((channels, 4, lon_cols), field.dtype)], axis=1
    )
    rim_rows = rows_ext.shape[1]
    east = lax.ppermute(
        rows_ext[:, :, :2], "lon", [((i + 1) % lon_count, i) for i in range(lon_count)]
    )
    west = lax.ppermute(
        rows_ext[:, :, lon_cols - 2 :], "lon", [(i, (i + 1) % lon_count) for i in range(lon_count)]
    )
    rim = jnp.concatenate(
        [
            rows_ext,
            east,
            jnp.zeros((channels, rim_rows, rim_cols - lon_cols - 4), field.dtype),
            west,
        ],
        axis=2,
    )
    conv_out = depthwise_conv(offsets, conv_weight, rim, lat_rows, lon_cols)
    gathered = gathered_raw
    summed = (
        gathered.astype(jnp.float32)
        .reshape(lat_count, lon_count, m_dev * 2 * channels * lat_rows)
        .sum(axis=1)
    )
    summed = summed.reshape(lat_count, m_dev, 2, channels, lat_rows)
    raw_spec = jnp.transpose(summed, (1, 2, 3, 0, 4)).reshape(m_dev, 2, channels, total_lat)

    rim = jnp.pad(raw_spec, ((0, 0), (0, 0), (0, 0), (2, 2)))
    turns = ((mine[None, :] * offsets[:, 1:2]) % total_lon).astype(jnp.float32) * (
        2.0 * math.pi / total_lon
    )
    cos_all = jnp.cos(turns)
    sin_all = jnp.sin(turns)
    shifts = lax.iota(jnp.int32, 5) - 2
    chosen = (offsets[None, :, 0] == shifts[:, None]).astype(jnp.float32)
    coef_re = jnp.einsum("dk,ck,ko->doc", chosen, conv_weight, cos_all)[..., None]
    coef_im = jnp.einsum("dk,ck,ko->doc", chosen, conv_weight, sin_all)[..., None]
    real_acc = jnp.zeros((m_dev, channels, total_lat), jnp.float32)
    imag_acc = jnp.zeros((m_dev, channels, total_lat), jnp.float32)
    for shift in range(-2, 3):
        window = rim[..., 2 + shift : 2 + shift + total_lat]
        c_re = coef_re[shift + 2]
        c_im = coef_im[shift + 2]
        real_acc = real_acc + c_re * window[:, 0] - c_im * window[:, 1]
        imag_acc = imag_acc + c_im * window[:, 0] + c_re * window[:, 1]
    spec_acc = jnp.stack([real_acc, imag_acc], axis=1)
    spectrum = spec_acc.astype(jnp.bfloat16)

    north_part = spectrum[..., :half_rows].astype(jnp.float32)
    south_part = jnp.flip(spectrum[..., half_rows:], axis=3).astype(jnp.float32)
    kept_mask = (mine[:, None] < band_limit[None, :]).astype(jnp.float32)
    weight_q = quad_weight[None, :] * kept_mask * (1.0 / math.sqrt(half_rows))
    even_terms = (weight_q[:, None, None, :] * (north_part + south_part)).astype(jnp.bfloat16)
    odd_terms = (weight_q[:, None, None, :] * (north_part - south_part)).astype(jnp.bfloat16)
    degrees = lax.iota(jnp.int32, orders_all)
    same = ((degrees[None, :] + mine[:, None]) % 2 == 0)[:, :, None]
    zero = jnp.zeros((), legendre.dtype)
    leg_same = jnp.where(same, legendre, zero)
    leg_diff = jnp.where(same, zero, legendre)
    coeffs = jnp.einsum(
        "mli,mpci->mpcl", leg_same, even_terms, preferred_element_type=jnp.float32
    ) + jnp.einsum("mli,mpci->mpcl", leg_diff, odd_terms, preferred_element_type=jnp.float32)
    triangle = (degrees[None, :] >= mine[:, None]).astype(jnp.float32)
    coeffs = (coeffs * triangle[:, None, None, :]).astype(jnp.bfloat16).astype(jnp.float32)
    w_real = jnp.transpose(mix_weight[0], (1, 2, 0)).astype(jnp.float32)
    w_imag = jnp.transpose(mix_weight[1], (1, 2, 0)).astype(jnp.float32)
    with_real = jnp.sum(coeffs[:, :, :, None, :] * w_real[None, None], axis=2)
    with_imag = jnp.sum(coeffs[:, :, :, None, :] * w_imag[None, None], axis=2)
    mixed = jnp.stack(
        [with_real[:, 0] - with_imag[:, 1], with_real[:, 1] + with_imag[:, 0]], axis=1
    ).astype(jnp.bfloat16)
    even_sum = jnp.einsum("mli,mpdl->mpdi", leg_same, mixed, preferred_element_type=jnp.float32)
    odd_sum = jnp.einsum("mli,mpdl->mpdi", leg_diff, mixed, preferred_element_type=jnp.float32)
    north_out = (even_sum + odd_sum) * kept_mask[:, None, None, :]
    south_out = (even_sum - odd_sum) * kept_mask[:, None, None, :]
    grid_spectrum = jnp.concatenate([north_out, jnp.flip(south_out, axis=3)], axis=3).astype(
        jnp.bfloat16
    )

    by_group = jnp.transpose(
        grid_spectrum.reshape(m_dev, 2, channels, lat_count, lat_rows), (3, 0, 1, 2, 4)
    )
    outgoing = jnp.broadcast_to(
        by_group[:, None], (lat_count, lon_count, m_dev, 2, channels, lat_rows)
    ).reshape(n_dev, 16, m_dev * 2 * channels * lat_rows // 16)
    full_rows = lax.all_to_all(outgoing, BOTH, 0, 0, tiled=True)
    full_rows, conv_out = lax.optimization_barrier((full_rows, conv_out))
    spectral_rows = full_rows.reshape(orders_all * 2, channels * lat_rows)
    inverse_rows = wave_table(
        lax.iota(jnp.int32, orders_all), lon_points, total_lon, True
    ).reshape(orders_all * 2, lon_cols)
    synthesis = lax.dot_general(
        spectral_rows, inverse_rows, (((0,), (0,)), ((), ())), preferred_element_type=jnp.float32
    ).reshape(channels, lat_rows, lon_cols)

    return (conv_out.astype(jnp.float32) + jax.nn.gelu(synthesis, approximate=True)).astype(
        jnp.bfloat16
    )


def depthwise_conv(offsets, conv_weight, rim, lat_rows, lon_cols):
    channels, rim_rows, rim_cols = rim.shape
    by_rows = jnp.transpose(rim, (1, 0, 2))
    block_c = 16
    chunk = 2

    def body(offs_ref, rim_ref, w_ref, out_ref, shifted):
        for row in range(rim_rows):
            v = rim_ref[row].astype(jnp.float32)
            for s in range(5):
                turn = (2 - s) % rim_cols
                shifted[s, :, pl.ds(row * rim_cols, rim_cols)] = (
                    v if turn == 0 else pltpu.roll(v, turn, 1)
                )
        weights = w_ref[...]
        for r0 in range(0, lat_rows, chunk):
            acc = jnp.zeros((block_c, chunk * rim_cols), jnp.float32)
            for k in range(KTAPS):
                dr = offs_ref[k, 0]
                dc = offs_ref[k, 1]
                start = pl.multiple_of((r0 + 2 + dr) * rim_cols, rim_cols)
                acc = acc + weights[:, k : k + 1] * shifted[dc + 2, :, pl.ds(start, chunk * rim_cols)]
            for i in range(chunk):
                out_ref[r0 + i] = acc[:, i * rim_cols : i * rim_cols + lon_cols].astype(jnp.bfloat16)

    by_rows_out = pl.pallas_call(
        body,
        grid_spec=pltpu.PrefetchScalarGridSpec(
            num_scalar_prefetch=1,
            grid=(channels // block_c,),
            in_specs=[
                pl.BlockSpec((rim_rows, block_c, rim_cols), lambda b, o: (0, b, 0)),
                pl.BlockSpec((block_c, KTAPS), lambda b, o: (b, 0)),
            ],
            out_specs=pl.BlockSpec((lat_rows, block_c, lon_cols), lambda b, o: (0, b, 0)),
            scratch_shapes=[pltpu.VMEM((5, block_c, rim_rows * rim_cols), jnp.float32)],
        ),
        out_shape=jax.ShapeDtypeStruct((lat_rows, channels, lon_cols), jnp.bfloat16),
        compiler_params=pltpu.CompilerParams(vmem_limit_bytes=48 * 1024 * 1024),
        cost_estimate=pl.CostEstimate(
            flops=8 * KTAPS * channels * rim_rows * rim_cols,
            transcendentals=0,
            bytes_accessed=channels * (rim_rows * rim_cols + lat_rows * lon_cols) * 2,
        ),
    )(offsets, by_rows, conv_weight)
    return jnp.transpose(by_rows_out, (1, 0, 2))


def solution(mesh):
    placed = (P(None, "lat", "lon"), P(), P(), P(BOTH, None, None), P(), P(), P())
    return jax.shard_map(
        per_device, mesh=mesh, in_specs=placed, out_specs=P(None, "lat", "lon"), check_vma=False
    )
```

```python
import math

import jax
import jax.numpy as jnp
from jax import lax
from jax.sharding import PartitionSpec as P
from jax.experimental import pallas as pl
from jax.experimental.pallas import tpu as pltpu

KTAPS = 9
BOTH = ("lat", "lon")


def wave_table(orders, points, period, inverse_form):
    angles = (orders[:, None] * points[None, :] % period).astype(jnp.float32) * (
        2.0 * math.pi / period
    )
    factor = jnp.full(orders.shape, 1.0 / math.sqrt(period), jnp.float32)
    if inverse_form:
        factor = jnp.where(orders == 0, 1.0, 2.0).astype(jnp.float32) * factor
    stacked = jnp.stack(
        [factor[:, None] * jnp.cos(angles), -factor[:, None] * jnp.sin(angles)], axis=1
    )
    return stacked.astype(jnp.bfloat16)


def per_device(field, offsets, conv_weight, legendre, quad_weight, band_limit, mix_weight):
    channels, lat_rows, lon_cols = field.shape
    m_dev = legendre.shape[0]
    lon_count = lax.axis_size("lon")
    lat_count = lax.axis_size("lat")
    n_dev = lon_count * lat_count
    total_lon = lon_cols * lon_count
    total_lat = lat_rows * lat_count
    half_rows = total_lat // 2
    orders_all = m_dev * n_dev
    lon_points = lax.axis_index("lon") * lon_cols + lax.iota(jnp.int32, lon_cols)
    me = lax.axis_index("lat") * lon_count + lax.axis_index("lon")
    mine = me * m_dev + lax.iota(jnp.int32, m_dev)

    forward_rows = wave_table(
        lax.iota(jnp.int32, orders_all), lon_points, total_lon, False
    ).reshape(orders_all * 2, lon_cols)
    flat_field = field.reshape(channels * lat_rows, lon_cols)
    partial = lax.dot_general(
        forward_rows, flat_field, (((1,), (1,)), ((), ())), preferred_element_type=jnp.float32
    ).reshape(n_dev, 16, m_dev * 2 * channels * lat_rows // 16)
    gathered_raw = lax.all_to_all(partial.astype(jnp.bfloat16), BOTH, 0, 0, tiled=True)
    rim_cols = ((lon_cols + 4 + 127) // 128) * 128
    lat_n = lax.axis_size("lat")
    south = lax.ppermute(
        field[:, :2], "lat", [((i + 1), i) for i in range(lat_n - 1)]
    )
    north = lax.ppermute(
        field[:, lat_rows - 2 :], "lat", [(i, (i + 1)) for i in range(lat_n - 1)]
    )
    rows_ext = jnp.concatenate(
        [north, field, south, jnp.zeros((channels, 4, lon_cols), field.dtype)], axis=1
    )
    rim_rows = rows_ext.shape[1]
    east = lax.ppermute(
        rows_ext[:, :, :2], "lon", [((i + 1) % lon_count, i) for i in range(lon_count)]
    )
    west = lax.ppermute(
        rows_ext[:, :, lon_cols - 2 :], "lon", [(i, (i + 1) % lon_count) for i in range(lon_count)]
    )
    rim = jnp.concatenate(
        [
            rows_ext,
            east,
            jnp.zeros((channels, rim_rows, rim_cols - lon_cols - 4), field.dtype),
            west,
        ],
        axis=2,
    )
    conv_out = depthwise_conv(offsets, conv_weight, rim, lat_rows, lon_cols)
    gathered = gathered_raw
    summed = (
        gathered.astype(jnp.float32)
        .reshape(lat_count, lon_count, m_dev * 2 * channels * lat_rows)
        .sum(axis=1)
    )
    summed = summed.reshape(lat_count, m_dev, 2, channels, lat_rows)
    raw_spec = jnp.transpose(summed, (1, 2, 3, 0, 4)).reshape(m_dev, 2, channels, total_lat)

    rim = jnp.pad(raw_spec, ((0, 0), (0, 0), (0, 0), (2, 2)))
    turns = ((mine[None, :] * offsets[:, 1:2]) % total_lon).astype(jnp.float32) * (
        2.0 * math.pi / total_lon
    )
    cos_all = jnp.cos(turns)
    sin_all = jnp.sin(turns)
    shifts = lax.iota(jnp.int32, 5) - 2
    chosen = (offsets[None, :, 0] == shifts[:, None]).astype(jnp.float32)
    coef_re = jnp.einsum("dk,ck,ko->doc", chosen, conv_weight, cos_all)[..., None]
    coef_im = jnp.einsum("dk,ck,ko->doc", chosen, conv_weight, sin_all)[..., None]
    real_acc = jnp.zeros((m_dev, channels, total_lat), jnp.float32)
    imag_acc = jnp.zeros((m_dev, channels, total_lat), jnp.float32)
    for shift in range(-2, 3):
        window = rim[..., 2 + shift : 2 + shift + total_lat]
        c_re = coef_re[shift + 2]
        c_im = coef_im[shift + 2]
        real_acc = real_acc + c_re * window[:, 0] - c_im * window[:, 1]
        imag_acc = imag_acc + c_im * window[:, 0] + c_re * window[:, 1]
    spec_acc = jnp.stack([real_acc, imag_acc], axis=1)
    spectrum = spec_acc.astype(jnp.bfloat16)

    north_part = spectrum[..., :half_rows].astype(jnp.float32)
    south_part = jnp.flip(spectrum[..., half_rows:], axis=3).astype(jnp.float32)
    kept_mask = (mine[:, None] < band_limit[None, :]).astype(jnp.float32)
    weight_q = quad_weight[None, :] * kept_mask * (1.0 / math.sqrt(half_rows))
    even_terms = (weight_q[:, None, None, :] * (north_part + south_part)).astype(jnp.bfloat16)
    odd_terms = (weight_q[:, None, None, :] * (north_part - south_part)).astype(jnp.bfloat16)
    degrees = lax.iota(jnp.int32, orders_all)
    same = ((degrees[None, :] + mine[:, None]) % 2 == 0)[:, :, None]
    zero = jnp.zeros((), legendre.dtype)
    leg_same = jnp.where(same, legendre, zero)
    leg_diff = jnp.where(same, zero, legendre)
    coeffs = jnp.einsum(
        "mli,mpci->mlpc", leg_same, even_terms, preferred_element_type=jnp.float32
    ) + jnp.einsum("mli,mpci->mlpc", leg_diff, odd_terms, preferred_element_type=jnp.float32)
    triangle = (degrees[None, :] >= mine[:, None]).astype(jnp.float32)
    coeffs = (coeffs * triangle[:, :, None, None]).astype(jnp.bfloat16)
    with_real = jnp.einsum(
        "mlpc,lcd->mlpd", coeffs, mix_weight[0], preferred_element_type=jnp.float32
    )
    with_imag = jnp.einsum(
        "mlpc,lcd->mlpd", coeffs, mix_weight[1], preferred_element_type=jnp.float32
    )
    mixed = jnp.stack(
        [with_real[:, :, 0] - with_imag[:, :, 1], with_real[:, :, 1] + with_imag[:, :, 0]],
        axis=2,
    ).astype(jnp.bfloat16)
    even_sum = jnp.einsum("mli,mlpc->mpci", leg_same, mixed, preferred_element_type=jnp.float32)
    odd_sum = jnp.einsum("mli,mlpc->mpci", leg_diff, mixed, preferred_element_type=jnp.float32)
    north_out = (even_sum + odd_sum) * kept_mask[:, None, None, :]
    south_out = (even_sum - odd_sum) * kept_mask[:, None, None, :]
    grid_spectrum = jnp.concatenate([north_out, jnp.flip(south_out, axis=3)], axis=3).astype(
        jnp.bfloat16
    )

    by_group = jnp.transpose(
        grid_spectrum.reshape(m_dev, 2, channels, lat_count, lat_rows), (3, 0, 1, 2, 4)
    )
    outgoing = jnp.broadcast_to(
        by_group[:, None], (lat_count, lon_count, m_dev, 2, channels, lat_rows)
    ).reshape(n_dev, 16, m_dev * 2 * channels * lat_rows // 16)
    full_rows = lax.all_to_all(outgoing, BOTH, 0, 0, tiled=True)
    full_rows, conv_out = lax.optimization_barrier((full_rows, conv_out))
    spectral_rows = full_rows.reshape(orders_all * 2, channels * lat_rows)
    inverse_rows = wave_table(
        lax.iota(jnp.int32, orders_all), lon_points, total_lon, True
    ).reshape(orders_all * 2, lon_cols)
    synthesis = lax.dot_general(
        spectral_rows, inverse_rows, (((0,), (0,)), ((), ())), preferred_element_type=jnp.float32
    ).reshape(channels, lat_rows, lon_cols)

    return (conv_out.astype(jnp.float32) + jax.nn.gelu(synthesis, approximate=True)).astype(
        jnp.bfloat16
    )


def depthwise_conv(offsets, conv_weight, rim, lat_rows, lon_cols):
    channels, rim_rows, rim_cols = rim.shape
    by_rows = jnp.transpose(rim, (1, 0, 2))
    block_c = 16
    chunk = 2

    def body(offs_ref, rim_ref, w_ref, out_ref, shifted):
        for row in range(rim_rows):
            v = rim_ref[row].astype(jnp.float32)
            for s in range(5):
                turn = (2 - s) % rim_cols
                shifted[s, :, pl.ds(row * rim_cols, rim_cols)] = (
                    v if turn == 0 else pltpu.roll(v, turn, 1)
                )
        weights = w_ref[...]
        for r0 in range(0, lat_rows, chunk):
            acc = jnp.zeros((block_c, chunk * rim_cols), jnp.float32)
            for k in range(KTAPS):
                dr = offs_ref[k, 0]
                dc = offs_ref[k, 1]
                start = pl.multiple_of((r0 + 2 + dr) * rim_cols, rim_cols)
                acc = acc + weights[:, k : k + 1] * shifted[dc + 2, :, pl.ds(start, chunk * rim_cols)]
            for i in range(chunk):
                out_ref[r0 + i] = acc[:, i * rim_cols : i * rim_cols + lon_cols].astype(jnp.bfloat16)

    by_rows_out = pl.pallas_call(
        body,
        grid_spec=pltpu.PrefetchScalarGridSpec(
            num_scalar_prefetch=1,
            grid=(channels // block_c,),
            in_specs=[
                pl.BlockSpec((rim_rows, block_c, rim_cols), lambda b, o: (0, b, 0)),
                pl.BlockSpec((block_c, KTAPS), lambda b, o: (b, 0)),
            ],
            out_specs=pl.BlockSpec((lat_rows, block_c, lon_cols), lambda b, o: (0, b, 0)),
            scratch_shapes=[pltpu.VMEM((5, block_c, rim_rows * rim_cols), jnp.float32)],
        ),
        out_shape=jax.ShapeDtypeStruct((lat_rows, channels, lon_cols), jnp.bfloat16),
        compiler_params=pltpu.CompilerParams(vmem_limit_bytes=48 * 1024 * 1024),
        cost_estimate=pl.CostEstimate(
            flops=8 * KTAPS * channels * rim_rows * rim_cols,
            transcendentals=0,
            bytes_accessed=channels * (rim_rows * rim_cols + lat_rows * lon_cols) * 2,
        ),
    )(offsets, by_rows, conv_weight)
    return jnp.transpose(by_rows_out, (1, 0, 2))


def solution(mesh):
    placed = (P(None, "lat", "lon"), P(), P(), P(BOTH, None, None), P(), P(), P())
    return jax.shard_map(
        per_device, mesh=mesh, in_specs=placed, out_specs=P(None, "lat", "lon"), check_vma=False
    )
```

```python
import math

import jax
import jax.numpy as jnp
from jax import lax
from jax.sharding import PartitionSpec as P
from jax.experimental import pallas as pl
from jax.experimental.pallas import tpu as pltpu

KTAPS = 9
BOTH = ("lat", "lon")


def wave_table(orders, points, period, inverse_form):
    angles = (orders[:, None] * points[None, :] % period).astype(jnp.float32) * (
        2.0 * math.pi / period
    )
    factor = jnp.full(orders.shape, 1.0 / math.sqrt(period), jnp.float32)
    if inverse_form:
        factor = jnp.where(orders == 0, 1.0, 2.0).astype(jnp.float32) * factor
    stacked = jnp.stack(
        [factor[:, None] * jnp.cos(angles), -factor[:, None] * jnp.sin(angles)], axis=1
    )
    return stacked.astype(jnp.bfloat16)


def per_device(field, offsets, conv_weight, legendre, quad_weight, band_limit, mix_weight):
    channels, lat_rows, lon_cols = field.shape
    m_dev = legendre.shape[0]
    lon_count = lax.axis_size("lon")
    lat_count = lax.axis_size("lat")
    n_dev = lon_count * lat_count
    total_lon = lon_cols * lon_count
    total_lat = lat_rows * lat_count
    half_rows = total_lat // 2
    orders_all = m_dev * n_dev
    lon_points = lax.axis_index("lon") * lon_cols + lax.iota(jnp.int32, lon_cols)
    me = lax.axis_index("lat") * lon_count + lax.axis_index("lon")
    mine = me * m_dev + lax.iota(jnp.int32, m_dev)

    forward_rows = wave_table(
        lax.iota(jnp.int32, orders_all), lon_points, total_lon, False
    ).reshape(orders_all * 2, lon_cols)
    flat_field = field.reshape(channels * lat_rows, lon_cols)
    partial = lax.dot_general(
        forward_rows, flat_field, (((1,), (1,)), ((), ())), preferred_element_type=jnp.float32
    ).reshape(n_dev, 16, m_dev * 2 * channels * lat_rows // 16)
    gathered_raw = lax.all_to_all(partial.astype(jnp.bfloat16), BOTH, 0, 0, tiled=True)
    rim_cols = ((lon_cols + 4 + 127) // 128) * 128
    lat_n = lax.axis_size("lat")
    south = lax.ppermute(
        field[:, :2], "lat", [((i + 1), i) for i in range(lat_n - 1)]
    )
    north = lax.ppermute(
        field[:, lat_rows - 2 :], "lat", [(i, (i + 1)) for i in range(lat_n - 1)]
    )
    rows_ext = jnp.concatenate(
        [north, field, south, jnp.zeros((channels, 4, lon_cols), field.dtype)], axis=1
    )
    rim_rows = rows_ext.shape[1]
    east = lax.ppermute(
        rows_ext[:, :, :2], "lon", [((i + 1) % lon_count, i) for i in range(lon_count)]
    )
    west = lax.ppermute(
        rows_ext[:, :, lon_cols - 2 :], "lon", [(i, (i + 1) % lon_count) for i in range(lon_count)]
    )
    rim = jnp.concatenate(
        [
            rows_ext,
            east,
            jnp.zeros((channels, rim_rows, rim_cols - lon_cols - 4), field.dtype),
            west,
        ],
        axis=2,
    )
    conv_out = depthwise_conv(offsets, conv_weight, rim, lat_rows, lon_cols)
    gathered = gathered_raw
    summed = (
        gathered.astype(jnp.float32)
        .reshape(lat_count, lon_count, m_dev * 2 * channels * lat_rows)
        .sum(axis=1)
    )
    summed = summed.reshape(lat_count, m_dev, 2, channels, lat_rows)
    raw_spec = jnp.transpose(summed, (1, 2, 3, 0, 4)).reshape(m_dev, 2, channels, total_lat)

    rim = jnp.pad(raw_spec, ((0, 0), (0, 0), (0, 0), (2, 2)))
    turns = ((mine[None, :] * offsets[:, 1:2]) % total_lon).astype(jnp.float32) * (
        2.0 * math.pi / total_lon
    )
    cos_all = jnp.cos(turns)
    sin_all = jnp.sin(turns)
    shifts = lax.iota(jnp.int32, 5) - 2
    chosen = (offsets[None, :, 0] == shifts[:, None]).astype(jnp.float32)
    coef_re = jnp.einsum("dk,ck,ko->doc", chosen, conv_weight, cos_all)[..., None]
    coef_im = jnp.einsum("dk,ck,ko->doc", chosen, conv_weight, sin_all)[..., None]
    real_acc = jnp.zeros((m_dev, channels, total_lat), jnp.float32)
    imag_acc = jnp.zeros((m_dev, channels, total_lat), jnp.float32)
    for shift in range(-2, 3):
        window = rim[..., 2 + shift : 2 + shift + total_lat]
        c_re = coef_re[shift + 2]
        c_im = coef_im[shift + 2]
        real_acc = real_acc + c_re * window[:, 0] - c_im * window[:, 1]
        imag_acc = imag_acc + c_im * window[:, 0] + c_re * window[:, 1]
    spec_acc = jnp.stack([real_acc, imag_acc], axis=1)
    spectrum = spec_acc.astype(jnp.bfloat16)

    north_part = spectrum[..., :half_rows].astype(jnp.float32)
    south_part = jnp.flip(spectrum[..., half_rows:], axis=3).astype(jnp.float32)
    kept_mask = (mine[:, None] < band_limit[None, :]).astype(jnp.float32)
    weight_q = quad_weight[None, :] * kept_mask * (1.0 / math.sqrt(half_rows))
    even_terms = (weight_q[:, None, None, :] * (north_part + south_part)).astype(jnp.bfloat16)
    odd_terms = (weight_q[:, None, None, :] * (north_part - south_part)).astype(jnp.bfloat16)
    degrees = lax.iota(jnp.int32, orders_all)
    same = ((degrees[None, :] + mine[:, None]) % 2 == 0)[:, :, None]
    zero = jnp.zeros((), legendre.dtype)
    leg_same = jnp.where(same, legendre, zero)
    leg_diff = jnp.where(same, zero, legendre)
    coeffs = jnp.einsum(
        "mli,mpci->mlpc", leg_same, even_terms, preferred_element_type=jnp.float32
    ) + jnp.einsum("mli,mpci->mlpc", leg_diff, odd_terms, preferred_element_type=jnp.float32)
    triangle = (degrees[None, :] >= mine[:, None]).astype(jnp.float32)
    coeffs = (coeffs * triangle[:, :, None, None]).astype(jnp.bfloat16)
    both_parts = jnp.einsum(
        "mlpc,qlcd->qmlpd", coeffs, mix_weight, preferred_element_type=jnp.float32
    )
    with_real = both_parts[0]
    with_imag = both_parts[1]
    mixed = jnp.stack(
        [with_real[:, :, 0] - with_imag[:, :, 1], with_real[:, :, 1] + with_imag[:, :, 0]],
        axis=2,
    ).astype(jnp.bfloat16)
    even_sum = jnp.einsum("mli,mlpc->mpci", leg_same, mixed, preferred_element_type=jnp.float32)
    odd_sum = jnp.einsum("mli,mlpc->mpci", leg_diff, mixed, preferred_element_type=jnp.float32)
    north_out = (even_sum + odd_sum) * kept_mask[:, None, None, :]
    south_out = (even_sum - odd_sum) * kept_mask[:, None, None, :]
    grid_spectrum = jnp.concatenate([north_out, jnp.flip(south_out, axis=3)], axis=3).astype(
        jnp.bfloat16
    )

    by_group = jnp.transpose(
        grid_spectrum.reshape(m_dev, 2, channels, lat_count, lat_rows), (3, 0, 1, 2, 4)
    )
    outgoing = jnp.broadcast_to(
        by_group[:, None], (lat_count, lon_count, m_dev, 2, channels, lat_rows)
    ).reshape(n_dev, 16, m_dev * 2 * channels * lat_rows // 16)
    full_rows = lax.all_to_all(outgoing, BOTH, 0, 0, tiled=True)
    full_rows, conv_out = lax.optimization_barrier((full_rows, conv_out))
    spectral_rows = full_rows.reshape(orders_all * 2, channels * lat_rows)
    inverse_rows = wave_table(
        lax.iota(jnp.int32, orders_all), lon_points, total_lon, True
    ).reshape(orders_all * 2, lon_cols)
    synthesis = lax.dot_general(
        spectral_rows, inverse_rows, (((0,), (0,)), ((), ())), preferred_element_type=jnp.float32
    ).reshape(channels, lat_rows, lon_cols)

    return (conv_out.astype(jnp.float32) + jax.nn.gelu(synthesis, approximate=True)).astype(
        jnp.bfloat16
    )


def depthwise_conv(offsets, conv_weight, rim, lat_rows, lon_cols):
    channels, rim_rows, rim_cols = rim.shape
    by_rows = jnp.transpose(rim, (1, 0, 2))
    block_c = 16
    chunk = 2

    def body(offs_ref, rim_ref, w_ref, out_ref, shifted):
        for row in range(rim_rows):
            v = rim_ref[row].astype(jnp.float32)
            for s in range(5):
                turn = (2 - s) % rim_cols
                shifted[s, :, pl.ds(row * rim_cols, rim_cols)] = (
                    v if turn == 0 else pltpu.roll(v, turn, 1)
                )
        weights = w_ref[...]
        for r0 in range(0, lat_rows, chunk):
            acc = jnp.zeros((block_c, chunk * rim_cols), jnp.float32)
            for k in range(KTAPS):
                dr = offs_ref[k, 0]
                dc = offs_ref[k, 1]
                start = pl.multiple_of((r0 + 2 + dr) * rim_cols, rim_cols)
                acc = acc + weights[:, k : k + 1] * shifted[dc + 2, :, pl.ds(start, chunk * rim_cols)]
            for i in range(chunk):
                out_ref[r0 + i] = acc[:, i * rim_cols : i * rim_cols + lon_cols].astype(jnp.bfloat16)

    by_rows_out = pl.pallas_call(
        body,
        grid_spec=pltpu.PrefetchScalarGridSpec(
            num_scalar_prefetch=1,
            grid=(channels // block_c,),
            in_specs=[
                pl.BlockSpec((rim_rows, block_c, rim_cols), lambda b, o: (0, b, 0)),
                pl.BlockSpec((block_c, KTAPS), lambda b, o: (b, 0)),
            ],
            out_specs=pl.BlockSpec((lat_rows, block_c, lon_cols), lambda b, o: (0, b, 0)),
            scratch_shapes=[pltpu.VMEM((5, block_c, rim_rows * rim_cols), jnp.float32)],
        ),
        out_shape=jax.ShapeDtypeStruct((lat_rows, channels, lon_cols), jnp.bfloat16),
        compiler_params=pltpu.CompilerParams(vmem_limit_bytes=48 * 1024 * 1024),
        cost_estimate=pl.CostEstimate(
            flops=8 * KTAPS * channels * rim_rows * rim_cols,
            transcendentals=0,
            bytes_accessed=channels * (rim_rows * rim_cols + lat_rows * lon_cols) * 2,
        ),
    )(offsets, by_rows, conv_weight)
    return jnp.transpose(by_rows_out, (1, 0, 2))


def solution(mesh):
    placed = (P(None, "lat", "lon"), P(), P(), P(BOTH, None, None), P(), P(), P())
    return jax.shard_map(
        per_device, mesh=mesh, in_specs=placed, out_specs=P(None, "lat", "lon"), check_vma=False
    )
```

```python
import math

import jax
import jax.numpy as jnp
from jax import lax
from jax.sharding import PartitionSpec as P
from jax.experimental import pallas as pl
from jax.experimental.pallas import tpu as pltpu

KTAPS = 9
BOTH = ("lat", "lon")


def wave_table(orders, points, period, inverse_form):
    angles = (orders[:, None] * points[None, :] % period).astype(jnp.float32) * (
        2.0 * math.pi / period
    )
    factor = jnp.full(orders.shape, 1.0 / math.sqrt(period), jnp.float32)
    if inverse_form:
        factor = jnp.where(orders == 0, 1.0, 2.0).astype(jnp.float32) * factor
    stacked = jnp.stack(
        [factor[:, None] * jnp.cos(angles), -factor[:, None] * jnp.sin(angles)], axis=1
    )
    return stacked.astype(jnp.bfloat16)


def per_device(field, offsets, conv_weight, legendre, quad_weight, band_limit, mix_weight):
    channels, lat_rows, lon_cols = field.shape
    m_dev = legendre.shape[0]
    lon_count = lax.axis_size("lon")
    lat_count = lax.axis_size("lat")
    n_dev = lon_count * lat_count
    total_lon = lon_cols * lon_count
    total_lat = lat_rows * lat_count
    half_rows = total_lat // 2
    orders_all = m_dev * n_dev
    lon_points = lax.axis_index("lon") * lon_cols + lax.iota(jnp.int32, lon_cols)
    me = lax.axis_index("lat") * lon_count + lax.axis_index("lon")
    mine = me * m_dev + lax.iota(jnp.int32, m_dev)

    forward_rows = wave_table(
        lax.iota(jnp.int32, orders_all), lon_points, total_lon, False
    ).reshape(orders_all * 2, lon_cols)
    flat_field = field.reshape(channels * lat_rows, lon_cols)
    partial = lax.dot_general(
        forward_rows, flat_field, (((1,), (1,)), ((), ())), preferred_element_type=jnp.float32
    ).reshape(n_dev, 16, m_dev * 2 * channels * lat_rows // 16)
    gathered_raw = lax.all_to_all(partial.astype(jnp.bfloat16), BOTH, 0, 0, tiled=True)
    rim_cols = ((lon_cols + 4 + 127) // 128) * 128
    lat_n = lax.axis_size("lat")
    south = lax.ppermute(
        field[:, :2], "lat", [((i + 1), i) for i in range(lat_n - 1)]
    )
    north = lax.ppermute(
        field[:, lat_rows - 2 :], "lat", [(i, (i + 1)) for i in range(lat_n - 1)]
    )
    rows_ext = jnp.concatenate(
        [north, field, south], axis=1
    )
    rim_rows = rows_ext.shape[1]
    east = lax.ppermute(
        rows_ext[:, :, :2], "lon", [((i + 1) % lon_count, i) for i in range(lon_count)]
    )
    west = lax.ppermute(
        rows_ext[:, :, lon_cols - 2 :], "lon", [(i, (i + 1) % lon_count) for i in range(lon_count)]
    )
    rim = jnp.concatenate(
        [
            rows_ext,
            east,
            jnp.zeros((channels, rim_rows, rim_cols - lon_cols - 4), field.dtype),
            west,
        ],
        axis=2,
    )
    conv_out = depthwise_conv(offsets, conv_weight, rim, lat_rows, lon_cols)
    gathered = gathered_raw
    summed = (
        gathered.astype(jnp.float32)
        .reshape(lat_count, lon_count, m_dev * 2 * channels * lat_rows)
        .sum(axis=1)
    )
    summed = summed.reshape(lat_count, m_dev, 2, channels, lat_rows)
    raw_spec = jnp.transpose(summed, (1, 2, 3, 0, 4)).reshape(m_dev, 2, channels, total_lat)

    rim = jnp.pad(raw_spec, ((0, 0), (0, 0), (0, 0), (2, 2)))
    turns = ((mine[None, :] * offsets[:, 1:2]) % total_lon).astype(jnp.float32) * (
        2.0 * math.pi / total_lon
    )
    cos_all = jnp.cos(turns)
    sin_all = jnp.sin(turns)
    shifts = lax.iota(jnp.int32, 5) - 2
    chosen = (offsets[None, :, 0] == shifts[:, None]).astype(jnp.float32)
    coef_re = jnp.einsum("dk,ck,ko->doc", chosen, conv_weight, cos_all)[..., None]
    coef_im = jnp.einsum("dk,ck,ko->doc", chosen, conv_weight, sin_all)[..., None]
    real_acc = jnp.zeros((m_dev, channels, total_lat), jnp.float32)
    imag_acc = jnp.zeros((m_dev, channels, total_lat), jnp.float32)
    for shift in range(-2, 3):
        window = rim[..., 2 + shift : 2 + shift + total_lat]
        c_re = coef_re[shift + 2]
        c_im = coef_im[shift + 2]
        real_acc = real_acc + c_re * window[:, 0] - c_im * window[:, 1]
        imag_acc = imag_acc + c_im * window[:, 0] + c_re * window[:, 1]
    spec_acc = jnp.stack([real_acc, imag_acc], axis=1)
    spectrum = spec_acc.astype(jnp.bfloat16)

    north_part = spectrum[..., :half_rows].astype(jnp.float32)
    south_part = jnp.flip(spectrum[..., half_rows:], axis=3).astype(jnp.float32)
    kept_mask = (mine[:, None] < band_limit[None, :]).astype(jnp.float32)
    weight_q = quad_weight[None, :] * kept_mask * (1.0 / math.sqrt(half_rows))
    even_terms = (weight_q[:, None, None, :] * (north_part + south_part)).astype(jnp.bfloat16)
    odd_terms = (weight_q[:, None, None, :] * (north_part - south_part)).astype(jnp.bfloat16)
    degrees = lax.iota(jnp.int32, orders_all)
    same = ((degrees[None, :] + mine[:, None]) % 2 == 0)[:, :, None]
    zero = jnp.zeros((), legendre.dtype)
    leg_same = jnp.where(same, legendre, zero)
    leg_diff = jnp.where(same, zero, legendre)
    coeffs = jnp.einsum(
        "mli,mpci->mlpc", leg_same, even_terms, preferred_element_type=jnp.float32
    ) + jnp.einsum("mli,mpci->mlpc", leg_diff, odd_terms, preferred_element_type=jnp.float32)
    triangle = (degrees[None, :] >= mine[:, None]).astype(jnp.float32)
    coeffs = (coeffs * triangle[:, :, None, None]).astype(jnp.bfloat16)
    with_real = jnp.einsum(
        "mlpc,lcd->mlpd", coeffs, mix_weight[0], preferred_element_type=jnp.float32
    )
    with_imag = jnp.einsum(
        "mlpc,lcd->mlpd", coeffs, mix_weight[1], preferred_element_type=jnp.float32
    )
    mixed = jnp.stack(
        [with_real[:, :, 0] - with_imag[:, :, 1], with_real[:, :, 1] + with_imag[:, :, 0]],
        axis=2,
    ).astype(jnp.bfloat16)
    even_sum = jnp.einsum("mli,mlpc->mpci", leg_same, mixed, preferred_element_type=jnp.float32)
    odd_sum = jnp.einsum("mli,mlpc->mpci", leg_diff, mixed, preferred_element_type=jnp.float32)
    north_out = (even_sum + odd_sum) * kept_mask[:, None, None, :]
    south_out = (even_sum - odd_sum) * kept_mask[:, None, None, :]
    grid_spectrum = jnp.concatenate([north_out, jnp.flip(south_out, axis=3)], axis=3).astype(
        jnp.bfloat16
    )

    by_group = jnp.transpose(
        grid_spectrum.reshape(m_dev, 2, channels, lat_count, lat_rows), (3, 0, 1, 2, 4)
    )
    outgoing = jnp.broadcast_to(
        by_group[:, None], (lat_count, lon_count, m_dev, 2, channels, lat_rows)
    ).reshape(n_dev, 16, m_dev * 2 * channels * lat_rows // 16)
    full_rows = lax.all_to_all(outgoing, BOTH, 0, 0, tiled=True)
    full_rows, conv_out = lax.optimization_barrier((full_rows, conv_out))
    spectral_rows = full_rows.reshape(orders_all * 2, channels * lat_rows)
    inverse_rows = wave_table(
        lax.iota(jnp.int32, orders_all), lon_points, total_lon, True
    ).reshape(orders_all * 2, lon_cols)
    synthesis = lax.dot_general(
        spectral_rows, inverse_rows, (((0,), (0,)), ((), ())), preferred_element_type=jnp.float32
    ).reshape(channels, lat_rows, lon_cols)

    return (conv_out.astype(jnp.float32) + jax.nn.gelu(synthesis, approximate=True)).astype(
        jnp.bfloat16
    )


def depthwise_conv(offsets, conv_weight, rim, lat_rows, lon_cols):
    channels, rim_rows, rim_cols = rim.shape
    by_rows = jnp.transpose(rim, (1, 0, 2))
    block_c = 16
    chunk = 2

    def body(offs_ref, rim_ref, w_ref, out_ref, shifted):
        for row in range(rim_rows):
            v = rim_ref[row].astype(jnp.float32)
            for s in range(5):
                turn = (2 - s) % rim_cols
                shifted[s, :, pl.ds(row * rim_cols, rim_cols)] = (
                    v if turn == 0 else pltpu.roll(v, turn, 1)
                )
        weights = w_ref[...]
        for r0 in range(0, lat_rows, chunk):
            acc = jnp.zeros((block_c, chunk * rim_cols), jnp.float32)
            for k in range(KTAPS):
                dr = offs_ref[k, 0]
                dc = offs_ref[k, 1]
                start = pl.multiple_of((r0 + 2 + dr) * rim_cols, rim_cols)
                acc = acc + weights[:, k : k + 1] * shifted[dc + 2, :, pl.ds(start, chunk * rim_cols)]
            for i in range(chunk):
                out_ref[r0 + i] = acc[:, i * rim_cols : i * rim_cols + lon_cols].astype(jnp.bfloat16)

    by_rows_out = pl.pallas_call(
        body,
        grid_spec=pltpu.PrefetchScalarGridSpec(
            num_scalar_prefetch=1,
            grid=(channels // block_c,),
            in_specs=[
                pl.BlockSpec((rim_rows, block_c, rim_cols), lambda b, o: (0, b, 0)),
                pl.BlockSpec((block_c, KTAPS), lambda b, o: (b, 0)),
            ],
            out_specs=pl.BlockSpec((lat_rows, block_c, lon_cols), lambda b, o: (0, b, 0)),
            scratch_shapes=[pltpu.VMEM((5, block_c, rim_rows * rim_cols), jnp.float32)],
        ),
        out_shape=jax.ShapeDtypeStruct((lat_rows, channels, lon_cols), jnp.bfloat16),
        compiler_params=pltpu.CompilerParams(vmem_limit_bytes=48 * 1024 * 1024),
        cost_estimate=pl.CostEstimate(
            flops=8 * KTAPS * channels * rim_rows * rim_cols,
            transcendentals=0,
            bytes_accessed=channels * (rim_rows * rim_cols + lat_rows * lon_cols) * 2,
        ),
    )(offsets, by_rows, conv_weight)
    return jnp.transpose(by_rows_out, (1, 0, 2))


def solution(mesh):
    placed = (P(None, "lat", "lon"), P(), P(), P(BOTH, None, None), P(), P(), P())
    return jax.shard_map(
        per_device, mesh=mesh, in_specs=placed, out_specs=P(None, "lat", "lon"), check_vma=False
    )
```

```python
import math

import jax
import jax.numpy as jnp
from jax import lax
from jax.sharding import PartitionSpec as P
from jax.experimental import pallas as pl
from jax.experimental.pallas import tpu as pltpu

KTAPS = 9
BOTH = ("lat", "lon")


def wave_table(orders, points, period, inverse_form):
    angles = (orders[:, None] * points[None, :] % period).astype(jnp.float32) * (
        2.0 * math.pi / period
    )
    factor = jnp.full(orders.shape, 1.0 / math.sqrt(period), jnp.float32)
    if inverse_form:
        factor = jnp.where(orders == 0, 1.0, 2.0).astype(jnp.float32) * factor
    stacked = jnp.stack(
        [factor[:, None] * jnp.cos(angles), -factor[:, None] * jnp.sin(angles)], axis=1
    )
    return stacked.astype(jnp.bfloat16)


def per_device(field, offsets, conv_weight, legendre, quad_weight, band_limit, mix_weight):
    channels, lat_rows, lon_cols = field.shape
    m_dev = legendre.shape[0]
    lon_count = lax.axis_size("lon")
    lat_count = lax.axis_size("lat")
    n_dev = lon_count * lat_count
    total_lon = lon_cols * lon_count
    total_lat = lat_rows * lat_count
    half_rows = total_lat // 2
    orders_all = m_dev * n_dev
    lon_points = lax.axis_index("lon") * lon_cols + lax.iota(jnp.int32, lon_cols)
    me = lax.axis_index("lat") * lon_count + lax.axis_index("lon")
    mine = me * m_dev + lax.iota(jnp.int32, m_dev)

    forward_rows = wave_table(
        lax.iota(jnp.int32, orders_all), lon_points, total_lon, False
    ).reshape(orders_all * 2, lon_cols)
    flat_field = field.reshape(channels * lat_rows, lon_cols)
    partial = lax.dot_general(
        forward_rows, flat_field, (((1,), (1,)), ((), ())), preferred_element_type=jnp.float32
    ).reshape(n_dev, 16, m_dev * 2 * channels * lat_rows // 16)
    gathered_raw = lax.all_to_all(partial.astype(jnp.bfloat16), BOTH, 0, 0, tiled=True)
    rim_cols = ((lon_cols + 4 + 127) // 128) * 128
    lat_n = lax.axis_size("lat")
    south = lax.ppermute(
        field[:, :2], "lat", [((i + 1), i) for i in range(lat_n - 1)]
    )
    north = lax.ppermute(
        field[:, lat_rows - 2 :], "lat", [(i, (i + 1)) for i in range(lat_n - 1)]
    )
    rows_ext = jnp.concatenate(
        [north, field, south, jnp.zeros((channels, 4, lon_cols), field.dtype)], axis=1
    )
    rim_rows = rows_ext.shape[1]
    east = lax.ppermute(
        rows_ext[:, :, :2], "lon", [((i + 1) % lon_count, i) for i in range(lon_count)]
    )
    west = lax.ppermute(
        rows_ext[:, :, lon_cols - 2 :], "lon", [(i, (i + 1) % lon_count) for i in range(lon_count)]
    )
    rim = jnp.concatenate(
        [
            rows_ext,
            east,
            jnp.zeros((channels, rim_rows, rim_cols - lon_cols - 4), field.dtype),
            west,
        ],
        axis=2,
    )
    conv_out = depthwise_conv(offsets, conv_weight, rim, lat_rows, lon_cols)
    gathered = gathered_raw
    summed = (
        gathered.astype(jnp.float32)
        .reshape(lat_count, lon_count, m_dev * 2 * channels * lat_rows)
        .sum(axis=1)
    )
    summed = summed.reshape(lat_count, m_dev, 2, channels, lat_rows)
    raw_spec = jnp.transpose(summed, (1, 2, 3, 0, 4)).reshape(m_dev, 2, channels, total_lat)

    rim = jnp.pad(raw_spec, ((0, 0), (0, 0), (0, 0), (2, 2)))
    turns = ((mine[None, :] * offsets[:, 1:2]) % total_lon).astype(jnp.float32) * (
        2.0 * math.pi / total_lon
    )
    cos_all = jnp.cos(turns)
    sin_all = jnp.sin(turns)
    shifts = lax.iota(jnp.int32, 5) - 2
    chosen = (offsets[None, :, 0] == shifts[:, None]).astype(jnp.float32)
    coef_re = jnp.einsum("dk,ck,ko->doc", chosen, conv_weight, cos_all)[..., None]
    coef_im = jnp.einsum("dk,ck,ko->doc", chosen, conv_weight, sin_all)[..., None]
    real_acc = jnp.zeros((m_dev, channels, total_lat), jnp.float32)
    imag_acc = jnp.zeros((m_dev, channels, total_lat), jnp.float32)
    for shift in range(-2, 3):
        window = rim[..., 2 + shift : 2 + shift + total_lat]
        c_re = coef_re[shift + 2]
        c_im = coef_im[shift + 2]
        real_acc = real_acc + c_re * window[:, 0] - c_im * window[:, 1]
        imag_acc = imag_acc + c_im * window[:, 0] + c_re * window[:, 1]
    spec_acc = jnp.stack([real_acc, imag_acc], axis=1)
    spectrum = spec_acc.astype(jnp.bfloat16)

    north_part = spectrum[..., :half_rows].astype(jnp.float32)
    south_part = jnp.flip(spectrum[..., half_rows:], axis=3).astype(jnp.float32)
    kept_mask = (mine[:, None] < band_limit[None, :]).astype(jnp.float32)
    weight_q = quad_weight[None, :] * kept_mask * (1.0 / math.sqrt(half_rows))
    even_terms = (weight_q[:, None, None, :] * (north_part + south_part)).astype(jnp.bfloat16)
    odd_terms = (weight_q[:, None, None, :] * (north_part - south_part)).astype(jnp.bfloat16)
    degrees = lax.iota(jnp.int32, orders_all)
    same = ((degrees[None, :] + mine[:, None]) % 2 == 0)[:, :, None]
    zero = jnp.zeros((), legendre.dtype)
    leg_same = jnp.where(same, legendre, zero)
    leg_diff = jnp.where(same, zero, legendre)
    coeffs = jnp.einsum(
        "mli,mpci->mlpc", leg_same, even_terms, preferred_element_type=jnp.float32
    ) + jnp.einsum("mli,mpci->mlpc", leg_diff, odd_terms, preferred_element_type=jnp.float32)
    triangle = (degrees[None, :] >= mine[:, None]).astype(jnp.float32)
    coeffs = (coeffs * triangle[:, :, None, None]).astype(jnp.bfloat16)
    with_real = jnp.einsum(
        "mlpc,lcd->mlpd", coeffs, mix_weight[0], preferred_element_type=jnp.float32
    )
    with_imag = jnp.einsum(
        "mlpc,lcd->mlpd", coeffs, mix_weight[1], preferred_element_type=jnp.float32
    )
    mixed = jnp.stack(
        [with_real[:, :, 0] - with_imag[:, :, 1], with_real[:, :, 1] + with_imag[:, :, 0]],
        axis=2,
    ).astype(jnp.bfloat16)
    even_sum = jnp.einsum("mli,mlpc->mpci", leg_same, mixed, preferred_element_type=jnp.float32)
    odd_sum = jnp.einsum("mli,mlpc->mpci", leg_diff, mixed, preferred_element_type=jnp.float32)
    north_out = (even_sum + odd_sum) * kept_mask[:, None, None, :]
    south_out = (even_sum - odd_sum) * kept_mask[:, None, None, :]
    grid_spectrum = jnp.concatenate([north_out, jnp.flip(south_out, axis=3)], axis=3).astype(
        jnp.bfloat16
    )

    by_group = jnp.transpose(
        grid_spectrum.reshape(m_dev, 2, channels, lat_count, lat_rows), (3, 0, 1, 2, 4)
    )
    outgoing = jnp.broadcast_to(
        by_group[:, None], (lat_count, lon_count, m_dev, 2, channels, lat_rows)
    ).reshape(n_dev, 16, m_dev * 2 * channels * lat_rows // 16)
    full_rows = lax.all_to_all(outgoing, BOTH, 0, 0, tiled=True)
    full_rows, conv_out = lax.optimization_barrier((full_rows, conv_out))
    spectral_rows = full_rows.reshape(orders_all * 2, channels * lat_rows)
    inverse_rows = wave_table(
        lax.iota(jnp.int32, orders_all), lon_points, total_lon, True
    ).reshape(orders_all * 2, lon_cols)
    synthesis = lax.dot_general(
        spectral_rows, inverse_rows, (((0,), (0,)), ((), ())), preferred_element_type=jnp.float32
    ).reshape(channels, lat_rows, lon_cols)

    return (conv_out.astype(jnp.float32) + jax.nn.gelu(synthesis, approximate=True)).astype(
        jnp.bfloat16
    )


def depthwise_conv(offsets, conv_weight, rim, lat_rows, lon_cols):
    channels, rim_rows, rim_cols = rim.shape
    by_rows = jnp.transpose(rim, (1, 0, 2))
    block_c = 16
    chunk = 1

    def body(offs_ref, rim_ref, w_ref, out_ref, shifted):
        for row in range(rim_rows):
            v = rim_ref[row].astype(jnp.float32)
            for s in range(5):
                turn = (2 - s) % rim_cols
                shifted[s, :, pl.ds(row * rim_cols, rim_cols)] = (
                    v if turn == 0 else pltpu.roll(v, turn, 1)
                )
        weights = w_ref[...]
        for r0 in range(0, lat_rows, chunk):
            acc = jnp.zeros((block_c, chunk * rim_cols), jnp.float32)
            for k in range(KTAPS):
                dr = offs_ref[k, 0]
                dc = offs_ref[k, 1]
                start = pl.multiple_of((r0 + 2 + dr) * rim_cols, rim_cols)
                acc = acc + weights[:, k : k + 1] * shifted[dc + 2, :, pl.ds(start, chunk * rim_cols)]
            for i in range(chunk):
                out_ref[r0 + i] = acc[:, i * rim_cols : i * rim_cols + lon_cols].astype(jnp.bfloat16)

    by_rows_out = pl.pallas_call(
        body,
        grid_spec=pltpu.PrefetchScalarGridSpec(
            num_scalar_prefetch=1,
            grid=(channels // block_c,),
            in_specs=[
                pl.BlockSpec((rim_rows, block_c, rim_cols), lambda b, o: (0, b, 0)),
                pl.BlockSpec((block_c, KTAPS), lambda b, o: (b, 0)),
            ],
            out_specs=pl.BlockSpec((lat_rows, block_c, lon_cols), lambda b, o: (0, b, 0)),
            scratch_shapes=[pltpu.VMEM((5, block_c, rim_rows * rim_cols), jnp.float32)],
        ),
        out_shape=jax.ShapeDtypeStruct((lat_rows, channels, lon_cols), jnp.bfloat16),
        compiler_params=pltpu.CompilerParams(vmem_limit_bytes=48 * 1024 * 1024),
        cost_estimate=pl.CostEstimate(
            flops=8 * KTAPS * channels * rim_rows * rim_cols,
            transcendentals=0,
            bytes_accessed=channels * (rim_rows * rim_cols + lat_rows * lon_cols) * 2,
        ),
    )(offsets, by_rows, conv_weight)
    return jnp.transpose(by_rows_out, (1, 0, 2))


def solution(mesh):
    placed = (P(None, "lat", "lon"), P(), P(), P(BOTH, None, None), P(), P(), P())
    return jax.shard_map(
        per_device, mesh=mesh, in_specs=placed, out_specs=P(None, "lat", "lon"), check_vma=False
    )
```
